32 devices in a mesh: shard: 4 (over y, x), replica: 8 (over z, core).
Axes of the slice: x: 2, y: 2, z: 4, core: 2. Of those that a mesh axis runs over, the one named last changes fastest.
Arguments:
- images: float32 [32, 197, 384], P(('shard', 'replica')), may hold values from -6 to 6
- cotangent: float32 [32, 197, 384], P(('shard', 'replica')), may hold values from -6 to 6
- counts: int32 [32], P(('shard', 'replica')), may hold values from 0 to 1, as said below
- w_qkv: bfloat16 [2, 384, 1152], P(None, 'shard'), may hold values from -0.3125 to 0.3125
- w_out: bfloat16 [2, 384, 384], P(None, 'shard'), may hold values from -1.25 to 1.25
- w_up: bfloat16 [2, 384, 1536], P(None, 'shard'), may hold values from -0.3125 to 0.3125
- w_down: bfloat16 [2, 1536, 384], P(None, 'shard'), may hold values from -0.15625 to 0.15625
- gains: bfloat16 [2, 2, 384], P(None, None, 'shard'), may hold values from 0.25 to 1.75
- biases: bfloat16 [2, 6, 384], P(None, None, 'shard'), may hold values from -1.796875 to 1.796875
- up_bias: bfloat16 [2, 1536], P(None, 'shard'), may hold values from -1.796875 to 1.796875
Outputs:
- activations: float32 [32, 197, 384], P(('shard', 'replica'))
- input_grad: float32 [32, 197, 384], P(('shard', 'replica'))
- grad_qkv: float32 [2, 384, 1152], P(None, 'shard')
- grad_out: float32 [2, 384, 384], P(None, 'shard')
- grad_up: float32 [2, 384, 1536], P(None, 'shard')
- grad_down: float32 [2, 1536, 384], P(None, 'shard')
- grad_gains: float32 [2, 2, 384], P(None, None, 'shard')
- grad_biases: float32 [2, 6, 384], P(None, None, 'shard')
- grad_upbias: float32 [2, 1536], P(None, 'shard')
The draws below stay inside these ranges and needn't reach their ends.
Inputs may be any that keep to these rules, and one draw needn't show every extreme that they name: `counts`: some device has all 1 slots live and some other device has none.
All inputs are finite; a program needn't handle non-finite values.
Results may differ from the reference program's by a relative error of at most 0.018.
Values may be sent and summed in bfloat16 or wider, within the bound.
A program may use at most 128 MiB of HBM per device.

```python
import jax
import jax.numpy as jnp
from jax import lax

D = 384
HEADS = 6
FF = 1536
HD = 64
S = 197
LAYERS = 2
IMG_DEV = 1
HOLDERS = 32
SLOTS = 32


def draw_counts(key, part):
    first, second, third = jax.random.split(jax.random.fold_in(key, 7), 3)
    filled = jax.random.randint(first, (HOLDERS,), 0, IMG_DEV + 1)
    where = jax.random.randint(second, (), 0, HOLDERS)
    offset = jax.random.randint(third, (), 1, HOLDERS)
    other = (where + offset) % HOLDERS
    filled = filled.at[where].set(IMG_DEV)
    filled = filled.at[other].set(0)
    return filled.astype(jnp.int32)


def levels(stream_key, extent, shards, smallest, high):
    def one(position, shards_of):
        steps = jax.random.uniform(jax.random.fold_in(jax.random.fold_in(stream_key, 6), position), (shards_of,), jnp.float32, smallest / len(shards), high / len(shards))
        return jnp.repeat(jnp.exp(steps), extent[position] // shards_of).reshape((-1,) + (1,) * (len(extent) - position - 1))

    level = one(*shards[0])
    for cut in shards[1:]:
        level = level * one(*cut)
    return level


def bell_draw(rng, shape, deviation, bound, cuts=(), held_as=jnp.bfloat16):
    loudness = levels(rng, shape, cuts, -0.22, 0.18) if cuts else 1.0
    values = jax.random.normal(rng, shape, jnp.float32) * deviation * loudness
    return jnp.minimum(jnp.maximum(values, -bound), bound).astype(held_as)


def setup_inputs(seed: int = 0) -> dict:
    keys = jax.random.split(jax.random.key(seed), 11)
    return {
        "images": bell_draw(keys[0], (SLOTS, S, D), 1.0, 6.0, ((0, 32),), jnp.float32),
        "cotangent": bell_draw(keys[1], (SLOTS, S, D), 1.0, 6.0, ((0, 32),), jnp.float32),
        "counts": draw_counts(jax.random.fold_in(keys[10], 71), 0),
        "w_qkv": bell_draw(keys[3], (LAYERS, D, 3 * D), D ** -0.5, 0.3125, ((1, 4),)),
        "w_out": bell_draw(keys[4], (LAYERS, D, D), (D // 16) ** -0.5, 1.25, ((1, 4),)),
        "w_up": bell_draw(keys[5], (LAYERS, D, FF), D ** -0.5, 0.3125, ((1, 4),)),
        "w_down": bell_draw(keys[6], (LAYERS, FF, D), FF ** -0.5, 0.15625, ((1, 4),)),
        "gains": jnp.clip(1.0 + 0.15 * jax.random.normal(keys[7], (LAYERS, 2, D), jnp.float32), 0.25, 1.75).astype(jnp.bfloat16),
        "biases": bell_draw(keys[8], (LAYERS, 6, D), 0.3, 1.796875, ((2, 4),)),
        "up_bias": bell_draw(keys[9], (LAYERS, FF), 0.3, 1.796875, ((1, 4),)),
    }


EPS = 1e-06
INV_ROOT_TWO = 0.7071067811865476
INV_ROOT_TWO_PI = 0.3989422804014327

def normalize(values, gain, shift):
    center = lax.optimization_barrier(jnp.mean(values, -1, keepdims=True))
    centered = values - center
    spread = lax.optimization_barrier(jnp.mean(centered * centered, -1, keepdims=True))
    inverse = lax.rsqrt(spread + EPS)
    unit = centered * inverse
    return (unit * gain + shift, unit, inverse)

def norm_back(upstream, unit, inverse, gain):
    scaled = upstream * gain
    inner = scaled - lax.optimization_barrier(jnp.mean(scaled, -1, keepdims=True)) - unit * lax.optimization_barrier(jnp.mean(scaled * unit, -1, keepdims=True))
    return (inverse * inner, lax.optimization_barrier(jnp.sum(upstream * unit, 0)), lax.optimization_barrier(jnp.sum(upstream, 0)))

def normal_cdf(values):
    return 0.5 * (1.0 + jax.scipy.special.erf(values * INV_ROOT_TWO))

def product(left, right):
    return jnp.dot(left, right, preferred_element_type=jnp.float32)

def product_left(left, right):
    return jnp.dot(left.T, right, preferred_element_type=jnp.float32)

def product_right(left, right):
    return jnp.dot(left, right.T, preferred_element_type=jnp.float32)

def batched(form, left, right):
    return jnp.einsum(form, left.astype(jnp.float32), right.astype(jnp.float32))

def inner_layer(stream, params, log_total):
    w_qkv, w_out, w_up, w_down, gains, biases, up_bias = params
    gains = gains.astype(jnp.float32)
    biases = biases.astype(jnp.float32)
    up_bias = up_bias.astype(jnp.float32)
    blocks = stream.shape[0]
    factor = HD ** (-0.5)
    rows_in = stream.reshape(-1, D)
    normed_f, unit_one, scale_one = normalize(rows_in, gains[0], biases[0])
    normed_one = normed_f.astype(jnp.bfloat16)
    project = product(normed_one, w_qkv)
    queries = ((project[:, :D] + biases[1]) * factor).astype(jnp.bfloat16).reshape(blocks, S, HEADS, HD)
    key_rows = project[:, D:2 * D].astype(jnp.bfloat16).reshape(blocks, S, HEADS, HD)
    values = (project[:, 2 * D:] + biases[2]).astype(jnp.bfloat16).reshape(blocks, S, HEADS, HD)
    scores = batched('bqhe,bkhe->bhqk', queries, key_rows)
    if log_total is None:
        log_total = jnp.log(lax.optimization_barrier(jnp.sum(jnp.exp(scores), -1, keepdims=True)))
    probs = jnp.exp(scores - log_total)
    prob_low = probs.astype(jnp.bfloat16)
    mixed = batched('bhqk,bkhe->bqhe', prob_low, values).reshape(-1, D).astype(jnp.bfloat16)
    middle = rows_in + product(mixed, w_out) + biases[3]
    normed_g, unit_two, scale_two = normalize(middle, gains[1], biases[4])
    normed_two = normed_g.astype(jnp.bfloat16)
    hidden = product(normed_two, w_up) + up_bias
    activated = (hidden * normal_cdf(hidden)).astype(jnp.bfloat16)
    result = middle + product(activated, w_down) + biases[5]
    saved = (normed_one, unit_one, scale_one, queries, key_rows, values, probs, prob_low, mixed, normed_two, unit_two, scale_two, hidden, activated)
    return (result.reshape(stream.shape), log_total, saved)

def backward_layer(stream, log_total, grad, params):
    w_qkv, w_out, w_up, w_down, gains, biases, up_bias = params
    gains_f = gains.astype(jnp.float32)
    blocks = stream.shape[0]
    factor = HD ** (-0.5)
    _, _, saved = inner_layer(stream, params, log_total)
    normed_one, unit_one, scale_one, queries, key_rows, values, probs, prob_low, mixed, normed_two, unit_two, scale_two, hidden, activated = saved
    low = grad.astype(jnp.bfloat16)
    down_grad = product_left(activated, low)
    shift_five = lax.optimization_barrier(jnp.sum(grad, 0))
    act_grad = product_right(low, w_down)
    dens = jnp.exp(-0.5 * hidden * hidden) * INV_ROOT_TWO_PI
    hid_grad = act_grad * (normal_cdf(hidden) + hidden * dens)
    hid_low = hid_grad.astype(jnp.bfloat16)
    up_grad = product_left(normed_two, hid_low)
    upbias_grad = lax.optimization_barrier(jnp.sum(hid_grad, 0))
    norm_grad = product_right(hid_low, w_up)
    back_two, gain_two, shift_four = norm_back(norm_grad, unit_two, scale_two, gains_f[1])
    mid_grad = grad + back_two
    mid_low = mid_grad.astype(jnp.bfloat16)
    out_grad = product_left(mixed, mid_low)
    shift_three = lax.optimization_barrier(jnp.sum(mid_grad, 0))
    mixed_grad = product_right(mid_low, w_out).astype(jnp.bfloat16).reshape(blocks, S, HEADS, HD)
    prob_grad = batched('bqhe,bkhe->bhqk', mixed_grad, values)
    row_dot = lax.optimization_barrier(jnp.sum(probs * prob_grad, -1, keepdims=True))
    score_grad = (probs * (prob_grad - row_dot)).astype(jnp.bfloat16)
    query_grad = (batched('bhqk,bkhe->bqhe', score_grad, key_rows) * factor).reshape(-1, D)
    key_grad = batched('bhqk,bqhe->bkhe', score_grad, queries).reshape(-1, D)
    value_grad = batched('bhqk,bqhe->bkhe', prob_low, mixed_grad).reshape(-1, D)
    project_grad = jnp.concatenate([query_grad, key_grad, value_grad], 1).astype(jnp.bfloat16)
    qkv_grad = product_left(normed_one, project_grad)
    first_grad = product_right(project_grad, w_qkv)
    back_one, gain_one, shift_zero = norm_back(first_grad, unit_one, scale_one, gains_f[0])
    stream_grad = mid_grad + back_one
    grads = (qkv_grad, out_grad, up_grad, down_grad, jnp.stack([gain_one, gain_two], 0), jnp.stack([shift_zero, lax.optimization_barrier(jnp.sum(query_grad, 0)), lax.optimization_barrier(jnp.sum(value_grad, 0)), shift_three, shift_four, shift_five], 0), upbias_grad)
    return (stream_grad, grads)

def reference(images, cotangent, counts, w_qkv, w_out, w_up, w_down, gains, biases, up_bias):
    stacks = (w_qkv, w_out, w_up, w_down, gains, biases, up_bias)
    image_blocks = images.reshape(HOLDERS, IMG_DEV, S, D)
    cot_blocks = cotangent.reshape(HOLDERS, IMG_DEV, S, D)
    starting = tuple((jnp.zeros(stack.shape, jnp.float32) for stack in stacks))

    def step(totals, item):
        block, cot_block, count = item
        live = (jnp.arange(IMG_DEV, dtype=jnp.int32) < count).astype(jnp.float32)[:, None, None]
        stream = block
        kept = []
        for layer in range(LAYERS):
            params = tuple((stack[layer] for stack in stacks))
            result, log_total, _ = inner_layer(stream, params, None)
            kept.append((stream, log_total))
            stream = result
        output = stream * live
        grad = (cot_block * live).reshape(-1, D)
        totals = list(totals)
        for layer in reversed(range(LAYERS)):
            params = tuple((stack[layer] for stack in stacks))
            grad, grads = backward_layer(kept[layer][0], kept[layer][1], grad, params)
            totals = [total.at[layer].add(piece) for total, piece in zip(totals, grads)]
        return (tuple(totals), (output, grad.reshape(IMG_DEV, S, D)))
    totals, (outputs, grads_in) = lax.scan(step, starting, (image_blocks, cot_blocks, counts))
    activations = outputs.reshape(SLOTS, S, D)
    input_grad = grads_in.reshape(SLOTS, S, D)
    return (activations, input_grad, totals[0], totals[1], totals[2], totals[3], totals[4], totals[5], totals[6])
```

```python
import functools

import jax
import jax.numpy as jnp
from jax import lax
from jax.experimental import pallas as pl
from jax.experimental.pallas import tpu as pltpu
from jax.sharding import PartitionSpec as P

HD = 64
EPS = 1e-06
INV_ROOT_TWO = 0.7071067811865476
INV_ROOT_TWO_PI = 0.3989422804014327
LOW = jnp.bfloat16
FULL = jnp.float32
MESH = pl.DeviceIdType.MESH
VMEM_LIMIT = 60 * 1024 * 1024

QKV, OUT, UP, DOWN = range(4)
GAIN_ROWS, BIAS_ROWS = 2, 6


def product(left, right):
    return jnp.dot(left, right, preferred_element_type=FULL)


def product_left(left, right):
    return lax.dot_general(
        left, right, (((0,), (0,)), ((), ())), preferred_element_type=FULL
    )


def product_right(left, right):
    return lax.dot_general(
        left, right, (((1,), (1,)), ((), ())), preferred_element_type=FULL
    )


def wide(value):
    return value.astype(FULL)


def column_sum(value):
    return jnp.sum(value, 0, keepdims=True)


def standardize(values):
    center = jnp.mean(values, -1, keepdims=True)
    centered = values - center
    spread = jnp.mean(centered * centered, -1, keepdims=True)
    inverse = lax.rsqrt(spread + EPS)
    return centered * inverse, inverse


def norm_back(upstream, unit, inverse, gain):
    scaled = upstream * gain
    inner = (
        scaled
        - jnp.mean(scaled, -1, keepdims=True)
        - unit * jnp.mean(scaled * unit, -1, keepdims=True)
    )
    return inverse * inner, column_sum(upstream * unit), column_sum(upstream)


def fused_kernel(shards, deep, *refs):
    (images, cotangent, counts, *own_w), refs = refs[:7], refs[7:]
    (gains, biases, up_bias), refs = refs[:3], refs[3:]
    (act_out, grad_out), refs = refs[:2], refs[2:]
    totals, refs = refs[:4], refs[4:]
    small_out, refs = refs[:3], refs[3:]
    (x_in, cot, stream, grad, w_qkv, w_out, w_up, w_down, par, par_up, small, small_all, wide_small,
     wide_all), refs = refs[:14], refs[14:]
    (unit_one, inv_one, normed_one, queries, key_rows, values, probs, mixed, unit_two, inv_two,
     normed_two, activated, slope, hid_low, mix_grad, pgrad), refs = refs[:16], refs[16:]
    own_g, refs = refs[:4], refs[4:]
    n_sub = 5 * own_w[0].shape[0]
    buf_a, refs = refs[:n_sub], refs[n_sub:]
    buf_s, refs = refs[:n_sub], refs[n_sub:]
    buf_b, refs = refs[:n_sub], refs[n_sub:]
    z_own, refs = refs[: n_sub + 1], refs[n_sub + 1 :]
    z_in, refs = refs[: n_sub + 1], refs[n_sub + 1 :]
    z_cross, refs = refs[: n_sub + 1], refs[n_sub + 1 :]
    z_fin, refs = refs[: n_sub + 1], refs[n_sub + 1 :]
    (tiny, tiny_in), refs = refs[:2], refs[2:]
    (f_send, f_recv, r_send, r_recv, m_send, m_recv, x_send, x_recv, q_send, q_recv, p_send, p_recv,
     own_sem, io_sem, a_send, a_recv, b_send, b_recv, c_send, c_recv, z_send, z_recv, e_send, e_recv,
     fin_sem, t_send, t_recv) = refs

    layers, rows_d, _ = own_w[QKV].shape
    width = x_in.shape[2]
    tokens = x_in.shape[1]
    padded = stream.shape[0]
    heads = width // HD
    ff = w_up.shape[2]
    factor = HD ** (-0.5)
    weights = (w_qkv, w_out, w_up, w_down)

    me = lax.axis_index("shard")
    rep = lax.axis_index("replica")
    core = lax.rem(rep, 2)
    depth = lax.div(rep, 2)
    parity = lax.rem(depth, 2)
    mid = deep // 2
    left = depth < mid
    place = jnp.where(left, depth, deep - 1 - depth)
    inner_depth = jnp.where(left, depth + 1, depth - 1)
    outer_depth = jnp.where(left, depth - 1, depth + 1)
    mate = (me, rep + 1 - 2 * core)
    across = (me, (depth + 1 - 2 * parity) * 2 + core)
    inner = (me, inner_depth * 2 + core)
    outer = (me, outer_depth * 2 + core)
    side_me = (me + 1 - 2 * lax.rem(me, 2), lax.rem(me + 2, shards))
    side = [(s, rep) for s in side_me]
    far_me = shards - 1 - me
    inside = place > 0
    center = place == mid - 1

    def local(src, dst, sem):
        copy = pltpu.make_async_copy(src, dst, sem)
        copy.start()
        return copy

    load_x = local(images, x_in, io_sem.at[0])
    load_cot = local(cotangent, cot, io_sem.at[1])

    barrier = pltpu.get_barrier_semaphore()
    for device in (mate, across, side[0], side[1], (far_me, rep), inner):
        pl.semaphore_signal(barrier, inc=1, device_id=device, device_id_type=MESH)

    @pl.when(inside)
    def _():
        pl.semaphore_signal(barrier, inc=1, device_id=outer, device_id_type=MESH)

    sent = []

    def remote(src, dst, send_sem, recv_sem, device, keep=True):
        copy = pltpu.make_async_remote_copy(
            src_ref=src, dst_ref=dst, send_sem=send_sem, recv_sem=recv_sem, device_id=device,
            device_id_type=MESH)
        copy.start()
        if keep:
            sent.append(copy)
        return copy

    items = [(kind, layer) for layer in range(layers) for kind in (QKV, OUT, UP, DOWN)]

    def part(ref, kind, layer, first_row, rows, which):
        half = rows // 2
        start = first_row + core * half
        if kind == UP:
            cut = ff // 2
            return ref.at[layer, pl.ds(pl.multiple_of(start, 16), half),
                          pl.ds(pl.multiple_of(which * cut, 128), cut)]
        if kind == DOWN:
            return ref.at[layer, pl.ds(pl.multiple_of(start + which * (half // 2), 16), half // 2)]
        return ref.at[layer, pl.ds(pl.multiple_of(start, 16), half)]

    def held(item, shard, which):
        kind, layer = items[item]
        rows = own_w[kind].shape[1]
        return part(weights[kind], kind, layer, shard * rows, rows, which)

    firsts, relays, passed, crossed, again, owned = {}, {}, {}, {}, {}, {}

    def first(item):
        kind, layer = items[item]
        rows = own_w[kind].shape[1]
        src = part(own_w[kind], kind, layer, 0, rows, parity)
        firsts[item] = [
            remote(src, held(item, me, parity), f_send.at[item, k], f_recv.at[item, k], side[k])
            for k in range(2)
        ]
        owned[item] = local(
            own_w[kind].at[layer],
            weights[kind].at[layer, pl.ds(pl.multiple_of(me * rows, 16), rows)], own_sem.at[item])
        passed[item] = []
        crossed[item] = []

    def hand_on(item, slot, shard):
        piece = held(item, shard, parity)
        if items[item][0] in (UP, DOWN):
            crossed[item].append((slot, shard, remote(
                piece, piece, x_send.at[item, slot], x_recv.at[item, slot], across)))
        passed[item].append(
            remote(piece, piece, m_send.at[item, slot], m_recv.at[item, slot], mate))

    def relay(item):
        via = item % 2
        for k in (via, 1 - via):
            firsts[item][k].wait_recv()
            if k == via:
                piece = held(item, side_me[k], parity)
                relays[item] = remote(
                    piece, piece, r_send.at[item], r_recv.at[item], side[1 - k])
            hand_on(item, k, side_me[k])

    def reach(item):
        relays[item].wait_recv()
        hand_on(item, 2, far_me)

    def cross(item):
        for slot, shard, copy in crossed[item]:
            copy.wait_recv()
            piece = held(item, shard, 1 - parity)
            passed[item].append(
                remote(piece, piece, q_send.at[item, slot], q_recv.at[item, slot], mate))

    def settle(item):
        for copy in passed[item]:
            copy.wait_recv()
        owned[item].wait()

    small[...] = jnp.zeros_like(small)
    wide_small[...] = jnp.zeros_like(wide_small)
    for layer in range(layers):
        small[pl.ds(layer * GAIN_ROWS, GAIN_ROWS), pl.ds(0, rows_d)] = wide(gains[layer])
        small[pl.ds(layers * GAIN_ROWS + layer * BIAS_ROWS, BIAS_ROWS), pl.ds(0, rows_d)] = wide(
            biases[layer])
    wide_small[pl.ds(0, layers), :] = wide(up_bias[...])

    pl.semaphore_wait(barrier, 6 + jnp.where(inside, 1, 0))

    tinies = []
    for k, shard in enumerate(side_me + (far_me,)):
        tinies.append(remote(
            small, small_all.at[me], p_send.at[0, k], p_recv.at[0, k], (shard, rep)))
        tinies.append(remote(
            wide_small, wide_all.at[me], p_send.at[1, k], p_recv.at[1, k], (shard, rep)))
    tinies_own = [
        local(small, small_all.at[me], io_sem.at[2]),
        local(wide_small, wide_all.at[me], io_sem.at[3]),
    ]

    first(0)
    first(1)
    first(2)
    load_x.wait()
    stream[...] = jnp.zeros_like(stream)
    stream[pl.ds(0, tokens), :] = x_in[0]
    unit, inverse = standardize(stream[...])
    unit_one[0] = unit
    inv_one[0] = inverse
    live = jnp.where(counts[0] > 0, 1.0, 0.0).astype(FULL)
    load_cot.wait()
    grad[...] = jnp.zeros_like(grad)
    grad[pl.ds(0, tokens), :] = cot[0] * live

    for copy in tinies:
        copy.wait_recv()
    for copy in tinies_own:
        copy.wait()
    for s in range(shards):
        par[:, pl.ds(s * rows_d, rows_d)] = small_all[s][:, :rows_d]
        per = wide_small.shape[1]
        par_up[:, pl.ds(s * per, per)] = wide_all[s]

    def gain_of(layer, which):
        return par[pl.ds(layer * GAIN_ROWS + which, 1), :]

    def bias_row(layer, which):
        return layers * GAIN_ROWS + layer * BIAS_ROWS + which

    def bias_of(layer, which):
        return par[pl.ds(bias_row(layer, which), 1), :]

    key_mask = jnp.where(
        lax.broadcasted_iota(jnp.int32, (1, padded), 1) < tokens, 0.0, -1e30).astype(FULL)
    lane_half = lax.broadcasted_iota(jnp.int32, (padded, 2 * HD), 1) < HD

    def one_head(value, which):
        keep = lane_half if which == 0 else jnp.logical_not(lane_half)
        return jnp.where(keep, value, jnp.zeros_like(value))

    def pair(p):
        return pl.ds(p * 2 * HD, 2 * HD)

    def project(layer):
        normed = (unit_one[layer] * gain_of(layer, 0) + bias_of(layer, 0)).astype(LOW)
        normed_one[layer] = normed
        queries[layer] = (
            (product(normed, w_qkv[layer, :, pl.ds(0, width)]) + bias_of(layer, 1)) * factor
        ).astype(LOW)
        key_rows[layer] = product(normed, w_qkv[layer, :, pl.ds(width, width)]).astype(LOW)
        values[layer] = (
            product(normed, w_qkv[layer, :, pl.ds(2 * width, width)]) + bias_of(layer, 2)
        ).astype(LOW)

    def attend(layer, p):
        q, k, v = (ref[layer, :, pair(p)] for ref in (queries, key_rows, values))
        total = None
        for h in range(2):
            scores = product_right(one_head(q, h), k) + key_mask
            log_total = jnp.log(jnp.sum(jnp.exp(scores), -1, keepdims=True))
            prob = jnp.exp(scores - log_total)
            probs[layer, 2 * p + h] = prob
            term = product(prob.astype(LOW), one_head(v, h))
            total = term if total is None else total + term
        mixed[layer, :, pair(p)] = total.astype(LOW)

    def join(layer):
        middle = stream[...] + product(mixed[layer], w_out[layer]) + bias_of(layer, 3)
        stream[...] = middle
        unit, inverse = standardize(middle)
        unit_two[layer] = unit
        inv_two[layer] = inverse
        normed_two[layer] = (unit * gain_of(layer, 1) + bias_of(layer, 4)).astype(LOW)

    chunk = 256

    def expand(layer, j):
        cols = pl.ds(j * chunk, chunk)
        hidden = product(normed_two[layer], w_up[layer, :, cols]) + par_up[pl.ds(layer, 1), cols]
        below = 0.5 * (1.0 + lax.erf(hidden * INV_ROOT_TWO))
        activated[layer, :, cols] = (hidden * below).astype(LOW)
        dens = jnp.exp(-0.5 * hidden * hidden) * INV_ROOT_TWO_PI
        slope[layer, :, cols] = below + hidden * dens

    def contract(layer):
        result = stream[...] + product(activated[layer], w_down[layer]) + bias_of(layer, 5)
        stream[...] = result
        if layer + 1 < layers:
            unit, inverse = standardize(result)
            unit_one[layer + 1] = unit
            inv_one[layer + 1] = inverse

    subs = []
    for layer in reversed(range(layers)):
        total_cols = own_w[QKV].shape[2]
        cut = (total_cols + width) // 2
        subs += [
            (DOWN, layer, 0, width, 0),
            (UP, layer, 0, ff, 1),
            (OUT, layer, 0, width, 1),
            (QKV, layer, 0, cut, 0),
            (QKV, layer, cut, total_cols - cut, 1),
        ]
    stage_a, one, two, z_one, z_out, ends = {}, {}, {}, {}, {}, {}

    def mine(a, dest, half):
        kind, layer, start, cols, _ = subs[a]
        return own_g[kind].at[layer, dest, half, :, pl.ds(start, cols)]

    def swap(a):
        kind, layer, start, cols, _ = subs[a]
        stage_a[a] = remote(
            own_g[kind].at[layer, :, 1 - core, :, pl.ds(start, cols)], buf_a[a], a_send.at[a],
            a_recv.at[a], mate)

    def both(a, dest):
        return wide(mine(a, dest, core)[...]) + wide(buf_a[a][dest])

    def scatter_one(a):
        turn = subs[a][4]
        stage_a[a].wait_recv()
        near = side_me[turn]
        buf_s[a][0] = both(a, near).astype(LOW)
        buf_s[a][1] = both(a, far_me).astype(LOW)
        one[a] = remote(
            buf_s[a].at[pl.ds(0, 2)], buf_b[a].at[pl.ds(0, 2)], b_send.at[a], b_recv.at[a],
            side[turn])

    def scatter_two(a):
        turn = 1 - subs[a][4]
        one[a].wait_recv()
        buf_s[a][2] = (both(a, side_me[turn]) + wide(buf_b[a][1])).astype(LOW)
        two[a] = remote(buf_s[a].at[2], buf_b[a].at[2], c_send.at[a], c_recv.at[a], side[turn])

    def summed(a):
        if a == n_sub:
            return tiny[3]
        return both(a, me) + wide(buf_b[a][0]) + wide(buf_b[a][2])

    def z_first(a):
        if a < n_sub:
            two[a].wait_recv()
        z_own[a][...] = summed(a).astype(z_own[a].dtype)

        @pl.when(jnp.logical_and(jnp.logical_not(inside), jnp.logical_not(center)))
        def _():
            remote(z_own[a], z_in[a], z_send.at[a, 0], z_recv.at[a, 0], inner, keep=False)

    def described(src, dst, send_sem, recv_sem, device):
        return pltpu.make_async_remote_copy(
            src_ref=src, dst_ref=dst, send_sem=send_sem, recv_sem=recv_sem, device_id=device,
            device_id_type=MESH)

    def z_copy(a):
        return described(z_own[a], z_in[a], z_send.at[a, 0], z_recv.at[a, 0], inner)

    def x_copy(a):
        return described(z_own[a], z_cross[a], z_send.at[a, 1], z_recv.at[a, 1], inner)

    def o_copy(a):
        return described(z_fin[a], z_fin[a], z_send.at[a, 2], z_recv.at[a, 2], outer)

    def z_second(a):
        @pl.when(inside)
        def _():
            z_copy(a).wait_recv()
            z_own[a][...] = (summed(a) + wide(z_in[a][...])).astype(z_own[a].dtype)

            @pl.when(jnp.logical_not(center))
            def _():
                z_copy(a).start()

        @pl.when(center)
        def _():
            x_copy(a).start()

    def goal(a):
        kind, layer, start, cols, _ = subs[a]
        return totals[kind].at[layer, core, :, pl.ds(start, cols)]

    def z_third(a):
        @pl.when(center)
        def _():
            x_copy(a).wait_recv()
            z_fin[a][...] = (wide(z_own[a][...]) + wide(z_cross[a][...])).astype(z_fin[a].dtype)

        @pl.when(jnp.logical_not(center))
        def _():
            o_copy(a).wait_recv()

        @pl.when(inside)
        def _():
            o_copy(a).start()

        if a == n_sub:
            return
        ends[a] = (
            remote(z_fin[a], goal(a), e_send.at[a], e_recv.at[a], mate),
            local(z_fin[a], goal(a), fin_sem.at[a]),
        )

    def z_done(a):
        if a < n_sub:
            ends[a][0].wait_recv()
            ends[a][1].wait()

        @pl.when(jnp.logical_not(center))
        def _():
            z_copy(a).wait_send()

        @pl.when(center)
        def _():
            x_copy(a).wait_send()

        @pl.when(inside)
        def _():
            o_copy(a).wait_send()

    def shared(value):
        return value.reshape(shards, 2, value.shape[0] // shards // 2, value.shape[1]).astype(LOW)

    up_row = layers * (GAIN_ROWS + BIAS_ROWS)

    def put_up_bias(layer, start, value):
        for at in range(0, value.shape[1], 128):
            row, lane = divmod(start + at, width)
            tiny[0, pl.ds(up_row + layer * (ff // width) + row, 1), pl.ds(lane, 128)] = (
                value[:, at : at + 128])

    def put_gain(layer, which, value):
        tiny[0, pl.ds(layer * GAIN_ROWS + which, 1), :] = value

    def put_bias(layer, which, value):
        tiny[0, pl.ds(bias_row(layer, which), 1), :] = value

    def back_down(layer):
        low = grad[...].astype(LOW)
        per = ff // shards
        for s in range(shards):
            piece = product_left(activated[layer, :, pl.ds(s * per, per)], low)
            own_g[DOWN][layer, s] = piece.reshape(2, per // 2, width).astype(LOW)
        put_bias(layer, 5, column_sum(grad[...]))

    def back_expand(layer, j):
        low = grad[...].astype(LOW)
        cols = pl.ds(j * chunk, chunk)
        act_grad = product_right(low, w_down[layer, cols, :])
        hid_grad = act_grad * slope[layer, :, cols]
        put_up_bias(layer, j * chunk, column_sum(hid_grad))
        hid_low[:, cols] = hid_grad.astype(LOW)

    def back_up(layer, j):
        cols = pl.ds(j * 2 * chunk, 2 * chunk)
        own_g[UP][layer, :, :, :, cols] = shared(product_left(normed_two[layer], hid_low[:, cols]))

    def back_middle(layer):
        norm_grad = product_right(hid_low[...], w_up[layer])
        back, gain, shift = norm_back(
            norm_grad, unit_two[layer], inv_two[layer], gain_of(layer, 1))
        put_gain(layer, 1, gain)
        put_bias(layer, 4, shift)
        mid_grad = grad[...] + back
        grad[...] = mid_grad
        put_bias(layer, 3, column_sum(mid_grad))
        mid_low = mid_grad.astype(LOW)
        own_g[OUT][layer] = shared(product_left(mixed[layer], mid_low))
        mix_grad[...] = product_right(mid_low, w_out[layer]).astype(LOW)

    def back_attend(layer, p):
        q, k, v = (ref[layer, :, pair(p)] for ref in (queries, key_rows, values))
        up = mix_grad[:, pair(p)]
        sums = [None] * 3
        for h in range(2):
            up_h = one_head(up, h)
            prob = probs[layer, 2 * p + h]
            prob_grad = product_right(up_h, v)
            row_dot = jnp.sum(prob * prob_grad, -1, keepdims=True)
            score_grad = (prob * (prob_grad - row_dot)).astype(LOW)
            terms = (
                product(score_grad, one_head(k, h)),
                product_left(score_grad, one_head(q, h)),
                product_left(prob.astype(LOW), up_h),
            )
            sums = [t if s is None else s + t for s, t in zip(sums, terms)]
        query_grad = sums[0] * factor
        start = p * 2 * HD
        tiny[0, pl.ds(bias_row(layer, 1), 1), pair(p)] = column_sum(query_grad)
        tiny[0, pl.ds(bias_row(layer, 2), 1), pair(p)] = column_sum(sums[2])
        for n, value in enumerate((query_grad, sums[1], sums[2])):
            pgrad[:, pl.ds(n * width + start, 2 * HD)] = value.astype(LOW)

    def back_qkv(layer, n):
        cols = pl.ds(n * width, width)
        own_g[QKV][layer, :, :, :, cols] = shared(product_left(normed_one[layer], pgrad[:, cols]))

    def back_first(layer):
        first_grad = product_right(pgrad[...], w_qkv[layer])
        back, gain, shift = norm_back(
            first_grad, unit_one[layer], inv_one[layer], gain_of(layer, 0))
        put_gain(layer, 0, gain)
        put_bias(layer, 0, shift)
        grad[...] = grad[...] + back


    relay(0)
    first(3)
    relay(1)
    reach(0)
    first(4)
    relay(2)
    reach(1)
    settle(0)
    project(0)
    first(5)
    relay(3)
    reach(2)
    attend(0, 0)
    relay(4)
    first(6)
    reach(3)
    attend(0, 1)
    cross(2)
    attend(0, 2)
    settle(1)
    join(0)
    relay(5)
    first(7)
    reach(4)
    cross(3)
    settle(2)
    for j in range(ff // chunk):
        expand(0, j)
        if j == 1:
            relay(6)
            reach(5)
        if j == 3:
            relay(7)
            reach(6)
    settle(3)
    contract(0)
    settle(4)
    project(1)
    reach(7)
    attend(1, 0)
    cross(6)
    attend(1, 1)
    cross(7)
    attend(1, 2)
    settle(5)
    join(1)
    settle(6)
    for j in range(ff // chunk):
        expand(1, j)
    settle(7)
    contract(1)

    x_in[0] = stream[pl.ds(0, tokens), :] * live
    store_act = local(x_in, act_out, io_sem.at[0])

    back_down(1)
    swap(0)
    for j in range(3):
        back_expand(1, j)
    scatter_one(0)
    for j in range(3, 6):
        back_expand(1, j)
    for j in range(3):
        back_up(1, j)
    swap(1)
    back_middle(1)
    swap(2)
    scatter_one(1)
    back_attend(1, 0)
    scatter_one(2)
    back_attend(1, 1)
    back_attend(1, 2)
    for n in range(3):
        back_qkv(1, n)
    swap(3)
    swap(4)
    scatter_two(0)
    back_first(1)
    scatter_one(3)
    scatter_one(4)
    back_down(0)
    swap(5)
    scatter_two(1)
    for j in range(6):
        back_expand(0, j)
    z_first(0)
    scatter_one(5)
    scatter_two(2)
    for j in range(3):
        back_up(0, j)
    swap(6)
    z_first(1)
    back_middle(0)
    swap(7)
    scatter_two(3)
    scatter_one(6)
    z_second(0)
    back_attend(0, 0)
    scatter_two(4)
    scatter_one(7)
    z_first(2)
    z_second(1)
    back_attend(0, 1)
    z_third(0)
    z_first(3)
    back_attend(0, 2)
    for n in range(3):
        back_qkv(0, n)
    swap(8)
    swap(9)
    z_second(2)
    z_first(4)
    z_third(1)
    back_first(0)
    scatter_one(8)
    scatter_one(9)
    x_cot = cot
    x_cot[0] = grad[pl.ds(0, tokens), :]
    store_grad = local(x_cot, grad_out, io_sem.at[1])

    swaps = []

    def tiny_send(n):
        device = (mate, side[0], side[1])[n]
        swaps.append(remote(tiny.at[n], tiny_in.at[n], t_send.at[n], t_recv.at[n], device))

    def tiny_add(n):
        swaps[n].wait_recv()
        tiny[n + 1] = tiny[n] + tiny_in[n]

    tiny_send(0)
    z_second(3)
    z_second(4)
    z_third(2)
    tiny_add(0)
    tiny_send(1)
    scatter_two(5)
    z_third(3)
    z_third(4)
    scatter_two(6)
    scatter_two(7)
    tiny_add(1)
    tiny_send(2)
    z_first(5)
    scatter_two(8)
    z_first(6)
    z_second(5)
    z_first(7)
    tiny_add(2)
    z_first(n_sub)
    scatter_two(9)
    z_second(6)
    z_third(5)
    z_first(8)
    z_second(7)
    z_first(9)
    z_second(n_sub)
    z_third(6)
    z_third(7)
    z_second(8)
    z_second(9)
    z_third(n_sub)
    z_third(8)
    z_third(9)
    done = z_fin[n_sub][...]
    picked = None
    for s in range(shards):
        hit = jnp.where(me == s, 1.0, 0.0).astype(FULL)
        term = done[:up_row, s * rows_d : (s + 1) * rows_d] * hit
        picked = term if picked is None else picked + term
    for layer in range(layers):
        small_out[0][layer] = picked[layer * GAIN_ROWS : (layer + 1) * GAIN_ROWS]
        first_row = bias_row(layer, 0)
        small_out[1][layer] = picked[first_row : first_row + BIAS_ROWS]
        row = None
        for s in range(shards):
            at = up_row + layer * (ff // width) + s
            hit = jnp.where(me == s, 1.0, 0.0).astype(FULL)
            term = done[at : at + 1] * hit
            row = term if row is None else row + term
        small_out[2][pl.ds(layer, 1), :] = row
    for a in range(n_sub + 1):
        z_done(a)
    for copy in sent:
        copy.wait_send()
    store_act.wait()
    store_grad.wait()


def finish_kernel(*refs):
    half = len(refs) // 2
    for src, dst in zip(refs[:half], refs[half:]):
        dst[...] = src[...].astype(FULL)


def finish(arrays):
    layers = arrays[2].shape[0]

    def spec(n, x):
        if 2 <= n < 6:
            return pl.BlockSpec((1,) + x.shape[1:], lambda i: (i,) + (0,) * (x.ndim - 1))
        return pl.BlockSpec(x.shape, lambda i: (0,) * x.ndim)

    specs = [spec(n, x) for n, x in enumerate(arrays)]
    return pl.pallas_call(
        finish_kernel,
        grid=(layers,),
        out_shape=[jax.ShapeDtypeStruct(x.shape, FULL) for x in arrays],
        in_specs=specs,
        out_specs=specs,
        name="widen",
    )(*arrays)


def on_device(shards, replicas, images, cotangent, counts, *stacks):
    weights, (gains, biases, up_bias) = stacks[:4], stacks[4:]
    layers, rows_d, _ = weights[QKV].shape
    deep = replicas // 2
    tokens, width = images.shape[1:]
    padded = -(-tokens // 16) * 16
    ff = weights[UP].shape[2]
    heads = width // HD
    qkv = weights[QKV].shape[2]
    sems = pltpu.SemaphoreType.DMA
    low = lambda *s: pltpu.VMEM(s, LOW)
    full = lambda *s: pltpu.VMEM(s, FULL)
    small_rows = layers * (GAIN_ROWS + BIAS_ROWS)
    small_rows_pad = -(-small_rows // 8) * 8
    per_up = up_bias.shape[1]
    scratch = [
        full(1, tokens, width), full(1, tokens, width), full(padded, width), full(padded, width),
        low(layers, shards * rows_d, qkv), low(layers, shards * rows_d, width),
        low(layers, shards * rows_d, ff), low(layers, ff, width),
        full(small_rows_pad, width), full(8, ff),
        full(small_rows_pad, 128), full(shards, small_rows_pad, 128),
        full(8, per_up), full(shards, 8, per_up),
        full(layers, padded, width), full(layers, padded, 1), low(layers, padded, width),
        low(layers, padded, width), low(layers, padded, width), low(layers, padded, width),
        full(layers, heads, padded, padded), low(layers, padded, width),
        full(layers, padded, width), full(layers, padded, 1), low(layers, padded, width),
        low(layers, padded, ff), full(layers, padded, ff), low(padded, ff), low(padded, width),
        low(padded, qkv),
    ]
    halves = [w.shape[1] // 2 for w in weights]
    columns = [w.shape[2] for w in weights]
    scratch += [low(layers, shards, 2, h, c) for h, c in zip(halves, columns)]
    cut = (qkv + width) // 2
    shapes = [
        (halves[DOWN], width), (halves[UP], ff), (halves[OUT], width), (halves[QKV], cut),
        (halves[QKV], qkv - cut),
    ] * layers
    n_sub = len(shapes)
    scratch += [low(shards, *s) for s in shapes] + [low(3, *s) for s in shapes] * 2
    tiny_rows = small_rows + layers * (ff // width)
    scratch += ([low(*s) for s in shapes] + [full(tiny_rows, width)]) * 4
    scratch += [full(4, tiny_rows, width), full(3, tiny_rows, width)]
    n_items = 4 * layers
    scratch += [
        sems((n_items, 2)), sems((n_items, 2)), sems((n_items,)), sems((n_items,)),
        sems((n_items, 3)), sems((n_items, 3)), sems((n_items, 3)), sems((n_items, 3)),
        sems((n_items, 3)), sems((n_items, 3)), sems((2, 3)), sems((2, 3)),
        sems((n_items,)), sems((4,)), sems((n_sub,)), sems((n_sub,)), sems((n_sub,)),
        sems((n_sub,)), sems((n_sub,)), sems((n_sub,)), sems((n_sub + 1, 3)), sems((n_sub + 1, 3)),
        sems((n_sub,)), sems((n_sub,)), sems((n_sub,)), sems((3,)), sems((3,)),
    ]
    shape = jax.ShapeDtypeStruct
    outs = [shape(images.shape, FULL), shape(images.shape, FULL)]
    outs += [shape((layers, 2, h, c), LOW) for h, c in zip(halves, columns)]
    outs += [shape(x.shape, FULL) for x in (gains, biases, up_bias)]
    hbm, vmem = pl.BlockSpec(memory_space=pl.ANY), pl.BlockSpec(memory_space=pltpu.VMEM)
    done = pl.pallas_call(
        functools.partial(fused_kernel, shards, deep),
        out_shape=outs,
        in_specs=[hbm, hbm, pl.BlockSpec(memory_space=pltpu.SMEM)] + [hbm] * 4 + [vmem] * 3,
        out_specs=[hbm] * 6 + [vmem] * 3,
        scratch_shapes=scratch,
        compiler_params=pltpu.CompilerParams(
            collective_id=0, has_side_effects=True, vmem_limit_bytes=VMEM_LIMIT
        ),
        name="encoder_step",
    )(images, cotangent, counts, *weights, gains, biases, up_bias)
    done = list(done)
    for kind in range(4):
        done[2 + kind] = done[2 + kind].reshape(weights[kind].shape)
    return tuple(finish(done))


def solution(mesh):
    in_specs = (
        P(("shard", "replica"), None, None),
        P(("shard", "replica"), None, None),
        P(("shard", "replica")),
        P(None, "shard", None),
        P(None, "shard", None),
        P(None, "shard", None),
        P(None, "shard", None),
        P(None, None, "shard"),
        P(None, None, "shard"),
        P(None, "shard"),
    )
    out_specs = (
        P(("shard", "replica"), None, None),
        P(("shard", "replica"), None, None),
        P(None, "shard", None),
        P(None, "shard", None),
        P(None, "shard", None),
        P(None, "shard", None),
        P(None, None, "shard"),
        P(None, None, "shard"),
        P(None, "shard"),
    )
    return jax.shard_map(
        functools.partial(on_device, mesh.shape["shard"], mesh.shape["replica"]), mesh=mesh, in_specs=in_specs, out_specs=out_specs, check_vma=False
    )
```

```python
import functools

import jax
import jax.numpy as jnp
from jax import lax
from jax.experimental import pallas as pl
from jax.experimental.pallas import tpu as pltpu
from jax.sharding import PartitionSpec as P

HD = 64
EPS = 1e-06
INV_ROOT_TWO = 0.7071067811865476
INV_ROOT_TWO_PI = 0.3989422804014327
LOW = jnp.bfloat16
FULL = jnp.float32
MESH = pl.DeviceIdType.MESH
VMEM_LIMIT = 60 * 1024 * 1024

QKV, OUT, UP, DOWN = range(4)
GAIN_ROWS, BIAS_ROWS = 2, 6


def product(left, right):
    return jnp.dot(left, right, preferred_element_type=FULL)


def product_left(left, right):
    return lax.dot_general(
        left, right, (((0,), (0,)), ((), ())), preferred_element_type=FULL
    )


def product_right(left, right):
    return lax.dot_general(
        left, right, (((1,), (1,)), ((), ())), preferred_element_type=FULL
    )


def wide(value):
    return value.astype(FULL)


def column_sum(value):
    return jnp.sum(value, 0, keepdims=True)


def standardize(values):
    center = jnp.mean(values, -1, keepdims=True)
    centered = values - center
    spread = jnp.mean(centered * centered, -1, keepdims=True)
    inverse = lax.rsqrt(spread + EPS)
    return centered * inverse, inverse


def norm_back(upstream, unit, inverse, gain):
    scaled = upstream * gain
    inner = (
        scaled
        - jnp.mean(scaled, -1, keepdims=True)
        - unit * jnp.mean(scaled * unit, -1, keepdims=True)
    )
    return inverse * inner, column_sum(upstream * unit), column_sum(upstream)


SUBS = 7


def sub_items(layers, weights, shards):
    width, ff, qkv = (weights[kind].shape[2] for kind in (OUT, UP, QKV))
    half_d = weights[QKV].shape[1] // 2
    rows = weights[DOWN].shape[1] // 4
    cut = (qkv + width) // 2
    subs = []
    for layer in reversed(range(layers)):
        subs += [
            (DOWN, layer, 0, rows, 0, width, 0),
            (DOWN, layer, rows, rows, 0, width, 1),
            (UP, layer, 0, half_d, 0, ff // 2, 0),
            (UP, layer, 0, half_d, ff // 2, ff // 2, 1),
            (OUT, layer, 0, half_d, 0, width, 1),
            (QKV, layer, 0, half_d, 0, cut, 0),
            (QKV, layer, 0, half_d, cut, qkv - cut, 1),
        ]
    return subs


def fused_kernel(shards, deep, *refs):
    (images, cotangent, counts, *own_w), refs = refs[:7], refs[7:]
    (gains, biases, up_bias), refs = refs[:3], refs[3:]
    (act_out, grad_out), refs = refs[:2], refs[2:]
    totals, refs = refs[:4], refs[4:]
    small_out, refs = refs[:3], refs[3:]
    (x_in, cot, stream, grad, w_qkv, w_out, w_up, w_down, par, par_up, small, small_all, wide_small,
     wide_all), refs = refs[:14], refs[14:]
    (unit_one, inv_one, normed_one, queries, key_rows, values, probs, mixed, unit_two, inv_two,
     normed_two, activated, slope, hid_low, mix_grad, pgrad), refs = refs[:16], refs[16:]
    own_g, refs = refs[:4], refs[4:]
    n_sub = SUBS * own_w[0].shape[0]
    buf_a, refs = refs[:n_sub], refs[n_sub:]
    buf_s, refs = refs[:n_sub], refs[n_sub:]
    buf_b, refs = refs[:n_sub], refs[n_sub:]
    z_own, refs = refs[: n_sub + 1], refs[n_sub + 1 :]
    z_in, refs = refs[: n_sub + 1], refs[n_sub + 1 :]
    z_cross, refs = refs[: n_sub + 1], refs[n_sub + 1 :]
    z_fin, refs = refs[: n_sub + 1], refs[n_sub + 1 :]
    (tiny, tiny_in), refs = refs[:2], refs[2:]
    (f_send, f_recv, r_send, r_recv, m_send, m_recv, x_send, x_recv, q_send, q_recv, p_send, p_recv,
     own_sem, io_sem, a_send, a_recv, b_send, b_recv, c_send, c_recv, z_send, z_recv, e_send, e_recv,
     fin_sem, t_send, t_recv) = refs

    layers, rows_d, _ = own_w[QKV].shape
    width = x_in.shape[1]
    tokens = x_in.shape[0]
    padded = stream.shape[0]
    heads = width // HD
    ff = w_up.shape[2]
    factor = HD ** (-0.5)
    weights = (w_qkv, w_out, w_up, w_down)

    me = lax.axis_index("shard")
    rep = lax.axis_index("replica")
    core = lax.rem(rep, 2)
    depth = lax.div(rep, 2)
    parity = lax.rem(depth, 2)
    mid = deep // 2
    left = depth < mid
    place = jnp.where(left, depth, deep - 1 - depth)
    inner_depth = jnp.where(left, depth + 1, depth - 1)
    outer_depth = jnp.where(left, depth - 1, depth + 1)
    mate = (me, rep + 1 - 2 * core)
    across = (me, (depth + 1 - 2 * parity) * 2 + core)
    inner = (me, inner_depth * 2 + core)
    outer = (me, outer_depth * 2 + core)
    side_me = (me + 1 - 2 * lax.rem(me, 2), lax.rem(me + 2, shards))
    side = [(s, rep) for s in side_me]
    far_me = shards - 1 - me
    inside = place > 0
    center = place == mid - 1

    def local(src, dst, sem):
        copy = pltpu.make_async_copy(src, dst, sem)
        copy.start()
        return copy

    load_x = local(images.at[:, 0], x_in, io_sem.at[0])
    load_cot = local(cotangent.at[:, 0], cot, io_sem.at[1])

    barrier = pltpu.get_barrier_semaphore()
    for device in (mate, across, side[0], side[1], (far_me, rep), inner):
        pl.semaphore_signal(barrier, inc=1, device_id=device, device_id_type=MESH)

    @pl.when(inside)
    def _():
        pl.semaphore_signal(barrier, inc=1, device_id=outer, device_id_type=MESH)

    sent = []

    def remote(src, dst, send_sem, recv_sem, device, keep=True):
        copy = pltpu.make_async_remote_copy(
            src_ref=src, dst_ref=dst, send_sem=send_sem, recv_sem=recv_sem, device_id=device,
            device_id_type=MESH)
        copy.start()
        if keep:
            sent.append(copy)
        return copy

    items = [(kind, layer) for layer in range(layers) for kind in (UP, DOWN)]
    items += [(kind, layer) for layer in range(layers) for kind in (QKV, OUT)]
    via_of, loads = [], [0, 0]
    for kind, _ in items:
        via_of.append(0 if loads[1] <= loads[0] else 1)
        loads[1 - via_of[-1]] += own_w[kind].shape[1] * own_w[kind].shape[2] // (
            2 if kind in (UP, DOWN) else 1)

    def part(ref, kind, layer, first_row, rows, which):
        half = rows // 2
        start = first_row + core * half
        if kind == UP:
            cut = ff // 2
            return ref.at[layer, pl.ds(pl.multiple_of(start, 16), half),
                          pl.ds(pl.multiple_of(which * cut, 128), cut)]
        if kind == DOWN:
            return ref.at[layer, pl.ds(pl.multiple_of(start + which * (half // 2), 16), half // 2)]
        return ref.at[layer, pl.ds(pl.multiple_of(start, 16), half)]

    def held(item, shard, which):
        kind, layer = items[item]
        rows = own_w[kind].shape[1]
        return part(weights[kind], kind, layer, shard * rows, rows, which)

    firsts, relays, passed, crossed, again, owned = {}, {}, {}, {}, {}, {}

    def first(item):
        kind, layer = items[item]
        rows = own_w[kind].shape[1]
        src = part(own_w[kind], kind, layer, 0, rows, parity)
        firsts[item] = [
            remote(src, held(item, me, parity), f_send.at[item, k], f_recv.at[item, k], side[k])
            for k in range(2)
        ]
        owned[item] = local(
            own_w[kind].at[layer],
            weights[kind].at[layer, pl.ds(pl.multiple_of(me * rows, 16), rows)], own_sem.at[item])
        passed[item] = []
        crossed[item] = []

    def hand_on(item, slot, shard):
        piece = held(item, shard, parity)
        if items[item][0] in (UP, DOWN):
            crossed[item].append((slot, shard, remote(
                piece, piece, x_send.at[item, slot], x_recv.at[item, slot], across)))
        passed[item].append(
            remote(piece, piece, m_send.at[item, slot], m_recv.at[item, slot], mate))

    def relay(item):
        via = via_of[item]
        for k in (via, 1 - via):
            firsts[item][k].wait_recv()
            if k == via:
                piece = held(item, side_me[k], parity)
                relays[item] = remote(
                    piece, piece, r_send.at[item], r_recv.at[item], side[1 - k])
            hand_on(item, k, side_me[k])

    def reach(item):
        relays[item].wait_recv()
        hand_on(item, 2, far_me)

    def cross(item):
        for slot, shard, copy in crossed[item]:
            copy.wait_recv()
            piece = held(item, shard, 1 - parity)
            passed[item].append(
                remote(piece, piece, q_send.at[item, slot], q_recv.at[item, slot], mate))

    def settle(item):
        for copy in passed[item]:
            copy.wait_recv()
        owned[item].wait()

    small[...] = jnp.zeros_like(small)
    wide_small[...] = jnp.zeros_like(wide_small)
    for layer in range(layers):
        small[pl.ds(layer * GAIN_ROWS, GAIN_ROWS), pl.ds(0, rows_d)] = wide(gains[layer])
    for which in range(BIAS_ROWS):
        small[pl.ds((GAIN_ROWS + which) * layers, layers), pl.ds(0, rows_d)] = wide(biases[which])
    wide_small[pl.ds(0, layers), :] = wide(up_bias[...])

    pl.semaphore_wait(barrier, 6 + jnp.where(inside, 1, 0))

    tinies = []
    for k, shard in enumerate(side_me + (far_me,)):
        tinies.append(remote(
            small, small_all.at[me], p_send.at[0, k], p_recv.at[0, k], (shard, rep)))
        tinies.append(remote(
            wide_small, wide_all.at[me], p_send.at[1, k], p_recv.at[1, k], (shard, rep)))
    tinies_own = [
        local(small, small_all.at[me], io_sem.at[2]),
        local(wide_small, wide_all.at[me], io_sem.at[3]),
    ]

    for item in range(len(items)):
        first(item)
    load_x.wait()
    stream[...] = jnp.zeros_like(stream)
    stream[pl.ds(0, tokens), :] = x_in[...]
    unit, inverse = standardize(stream[...])
    unit_one[0] = unit
    inv_one[0] = inverse
    live = jnp.where(counts[0] > 0, 1.0, 0.0).astype(FULL)
    load_cot.wait()
    grad[...] = jnp.zeros_like(grad)
    grad[pl.ds(0, tokens), :] = cot[...] * live

    for copy in tinies:
        copy.wait_recv()
    for copy in tinies_own:
        copy.wait()
    for s in range(shards):
        par[:, pl.ds(s * rows_d, rows_d)] = small_all[s][:, :rows_d]
        per = wide_small.shape[1]
        par_up[:, pl.ds(s * per, per)] = wide_all[s]

    def gain_of(layer, which):
        return par[pl.ds(layer * GAIN_ROWS + which, 1), :]

    def bias_row(layer, which):
        return (GAIN_ROWS + which) * layers + layer

    def bias_of(layer, which):
        return par[pl.ds(bias_row(layer, which), 1), :]

    key_mask = jnp.where(
        lax.broadcasted_iota(jnp.int32, (1, padded), 1) < tokens, 0.0, -1e30).astype(FULL)
    lane_half = lax.broadcasted_iota(jnp.int32, (padded, 2 * HD), 1) < HD

    def one_head(value, which):
        keep = lane_half if which == 0 else jnp.logical_not(lane_half)
        return jnp.where(keep, value, jnp.zeros_like(value))

    def pair(p):
        return pl.ds(p * 2 * HD, 2 * HD)

    def project(layer):
        normed = (unit_one[layer] * gain_of(layer, 0) + bias_of(layer, 0)).astype(LOW)
        normed_one[layer] = normed
        queries[layer] = (
            (product(normed, w_qkv[layer, :, pl.ds(0, width)]) + bias_of(layer, 1)) * factor
        ).astype(LOW)
        key_rows[layer] = product(normed, w_qkv[layer, :, pl.ds(width, width)]).astype(LOW)
        values[layer] = (
            product(normed, w_qkv[layer, :, pl.ds(2 * width, width)]) + bias_of(layer, 2)
        ).astype(LOW)

    def attend(layer, p):
        q, k, v = (ref[layer, :, pair(p)] for ref in (queries, key_rows, values))
        total = None
        for h in range(2):
            scores = product_right(one_head(q, h), k) + key_mask
            log_total = jnp.log(jnp.sum(jnp.exp(scores), -1, keepdims=True))
            prob = jnp.exp(scores - log_total)
            probs[layer, 2 * p + h] = prob
            term = product(prob.astype(LOW), one_head(v, h))
            total = term if total is None else total + term
        mixed[layer, :, pair(p)] = total.astype(LOW)

    def join(layer):
        middle = stream[...] + product(mixed[layer], w_out[layer]) + bias_of(layer, 3)
        stream[...] = middle
        unit, inverse = standardize(middle)
        unit_two[layer] = unit
        inv_two[layer] = inverse
        normed_two[layer] = (unit * gain_of(layer, 1) + bias_of(layer, 4)).astype(LOW)

    chunk = 256

    def expand(layer, j):
        cols = pl.ds(j * chunk, chunk)
        hidden = product(normed_two[layer], w_up[layer, :, cols]) + par_up[pl.ds(layer, 1), cols]
        below = 0.5 * (1.0 + lax.erf(hidden * INV_ROOT_TWO))
        activated[layer, :, cols] = (hidden * below).astype(LOW)
        dens = jnp.exp(-0.5 * hidden * hidden) * INV_ROOT_TWO_PI
        slope[layer, :, cols] = below + hidden * dens

    def contract(layer):
        result = stream[...] + product(activated[layer], w_down[layer]) + bias_of(layer, 5)
        stream[...] = result
        if layer + 1 < layers:
            unit, inverse = standardize(result)
            unit_one[layer + 1] = unit
            inv_one[layer + 1] = inverse

    subs = sub_items(layers, own_w, shards)
    stage_a, one, two = {}, {}, {}

    def mine(a, dest, half):
        kind, layer, row, rows, start, cols, _ = subs[a]
        return own_g[kind].at[layer, dest, half, pl.ds(row, rows), pl.ds(start, cols)]

    def swap(a):
        kind, layer, row, rows, start, cols, _ = subs[a]
        stage_a[a] = remote(
            own_g[kind].at[layer, :, 1 - core, pl.ds(row, rows), pl.ds(start, cols)], buf_a[a],
            a_send.at[a], a_recv.at[a], mate)

    def both(a, dest):
        return wide(mine(a, dest, core)[...]) + wide(buf_a[a][dest])

    def scatter_one(a):
        turn = subs[a][-1]
        stage_a[a].wait_recv()
        near = side_me[turn]
        buf_s[a][0] = both(a, near).astype(LOW)
        buf_s[a][1] = both(a, far_me).astype(LOW)
        one[a] = remote(
            buf_s[a].at[pl.ds(0, 2)], buf_b[a].at[pl.ds(0, 2)], b_send.at[a], b_recv.at[a],
            side[turn])

    def scatter_two(a):
        turn = 1 - subs[a][-1]
        one[a].wait_recv()
        buf_s[a][2] = (both(a, side_me[turn]) + wide(buf_b[a][1])).astype(LOW)
        two[a] = remote(buf_s[a].at[2], buf_b[a].at[2], c_send.at[a], c_recv.at[a], side[turn])

    def summed(a):
        if a == n_sub:
            return tiny[3]
        return both(a, me) + wide(buf_b[a][0]) + wide(buf_b[a][2])

    def z_first(a):
        if a < n_sub:
            two[a].wait_recv()
        z_own[a][...] = summed(a).astype(z_own[a].dtype)

        @pl.when(jnp.logical_and(jnp.logical_not(inside), jnp.logical_not(center)))
        def _():
            remote(z_own[a], z_in[a], z_send.at[a, 0], z_recv.at[a, 0], inner, keep=False)

    def described(src, dst, send_sem, recv_sem, device):
        return pltpu.make_async_remote_copy(
            src_ref=src, dst_ref=dst, send_sem=send_sem, recv_sem=recv_sem, device_id=device,
            device_id_type=MESH)

    def z_copy(a):
        return described(z_own[a], z_in[a], z_send.at[a, 0], z_recv.at[a, 0], inner)

    def x_copy(a):
        return described(z_own[a], z_cross[a], z_send.at[a, 1], z_recv.at[a, 1], inner)

    def o_copy(a):
        return described(z_fin[a], z_fin[a], z_send.at[a, 2], z_recv.at[a, 2], outer)

    def z_second(a):
        @pl.when(inside)
        def _():
            z_copy(a).wait_recv()
            z_own[a][...] = (summed(a) + wide(z_in[a][...])).astype(z_own[a].dtype)

            @pl.when(jnp.logical_not(center))
            def _():
                z_copy(a).start()

        @pl.when(center)
        def _():
            x_copy(a).start()

    def goal(a):
        kind, layer, row, rows, start, cols, _ = subs[a]
        return totals[kind].at[layer, core, pl.ds(row, rows), pl.ds(start, cols)]

    def e_copy(a):
        return described(z_fin[a], goal(a), e_send.at[a], e_recv.at[a], mate)

    def fin_copy(a):
        return pltpu.make_async_copy(z_fin[a], goal(a), fin_sem.at[a])

    def spread(a):
        @pl.when(inside)
        def _():
            o_copy(a).start()

        if a < n_sub:
            e_copy(a).start()
            fin_copy(a).start()

    def z_third(a):
        @pl.when(center)
        def _():
            x_copy(a).wait_recv()
            z_fin[a][...] = (wide(z_own[a][...]) + wide(z_cross[a][...])).astype(z_fin[a].dtype)
            spread(a)

    def z_fourth(a):
        @pl.when(jnp.logical_not(center))
        def _():
            o_copy(a).wait_recv()
            spread(a)

    def z_done(a):
        if a < n_sub:
            e_copy(a).wait()
            fin_copy(a).wait()

        @pl.when(jnp.logical_not(center))
        def _():
            z_copy(a).wait_send()

        @pl.when(center)
        def _():
            x_copy(a).wait_send()

        @pl.when(inside)
        def _():
            o_copy(a).wait_send()

    def shared(value):
        return value.reshape(shards, 2, value.shape[0] // shards // 2, value.shape[1]).astype(LOW)

    up_row = layers * (GAIN_ROWS + BIAS_ROWS)

    def put_up_bias(layer, start, value):
        for at in range(0, value.shape[1], 128):
            row, lane = divmod(start + at, width)
            tiny[0, pl.ds(up_row + layer * (ff // width) + row, 1), pl.ds(lane, 128)] = (
                value[:, at : at + 128])

    def put_gain(layer, which, value):
        tiny[0, pl.ds(layer * GAIN_ROWS + which, 1), :] = value

    def put_bias(layer, which, value):
        tiny[0, pl.ds(bias_row(layer, which), 1), :] = value

    def back_down(layer):
        low = grad[...].astype(LOW)
        per = ff // shards
        for s in range(shards):
            piece = product_left(activated[layer, :, pl.ds(s * per, per)], low)
            own_g[DOWN][layer, s] = piece.reshape(2, per // 2, width).astype(LOW)
        put_bias(layer, 5, column_sum(grad[...]))

    def back_expand(layer, j):
        low = grad[...].astype(LOW)
        cols = pl.ds(j * chunk, chunk)
        act_grad = product_right(low, w_down[layer, cols, :])
        hid_grad = act_grad * slope[layer, :, cols]
        put_up_bias(layer, j * chunk, column_sum(hid_grad))
        hid_low[:, cols] = hid_grad.astype(LOW)

    def back_up(layer, j):
        cols = pl.ds(j * ff // 2, ff // 2)
        own_g[UP][layer, :, :, :, cols] = shared(product_left(normed_two[layer], hid_low[:, cols]))

    def back_middle(layer):
        norm_grad = product_right(hid_low[...], w_up[layer])
        back, gain, shift = norm_back(
            norm_grad, unit_two[layer], inv_two[layer], gain_of(layer, 1))
        put_gain(layer, 1, gain)
        put_bias(layer, 4, shift)
        mid_grad = grad[...] + back
        grad[...] = mid_grad
        put_bias(layer, 3, column_sum(mid_grad))
        mid_low = mid_grad.astype(LOW)
        own_g[OUT][layer] = shared(product_left(mixed[layer], mid_low))
        mix_grad[...] = product_right(mid_low, w_out[layer]).astype(LOW)

    def back_attend(layer, p):
        q, k, v = (ref[layer, :, pair(p)] for ref in (queries, key_rows, values))
        up = mix_grad[:, pair(p)]
        sums = [None] * 3
        for h in range(2):
            up_h = one_head(up, h)
            prob = probs[layer, 2 * p + h]
            prob_grad = product_right(up_h, v)
            row_dot = jnp.sum(prob * prob_grad, -1, keepdims=True)
            score_grad = (prob * (prob_grad - row_dot)).astype(LOW)
            terms = (
                product(score_grad, one_head(k, h)),
                product_left(score_grad, one_head(q, h)),
                product_left(prob.astype(LOW), up_h),
            )
            sums = [t if s is None else s + t for s, t in zip(sums, terms)]
        query_grad = sums[0] * factor
        start = p * 2 * HD
        tiny[0, pl.ds(bias_row(layer, 1), 1), pair(p)] = column_sum(query_grad)
        tiny[0, pl.ds(bias_row(layer, 2), 1), pair(p)] = column_sum(sums[2])
        for n, value in enumerate((query_grad, sums[1], sums[2])):
            pgrad[:, pl.ds(n * width + start, 2 * HD)] = value.astype(LOW)

    def back_qkv(layer, n):
        cols = pl.ds(n * width, width)
        own_g[QKV][layer, :, :, :, cols] = shared(product_left(normed_one[layer], pgrad[:, cols]))

    def back_first(layer):
        first_grad = product_right(pgrad[...], w_qkv[layer])
        back, gain, shift = norm_back(
            first_grad, unit_one[layer], inv_one[layer], gain_of(layer, 0))
        put_gain(layer, 0, gain)
        put_bias(layer, 0, shift)
        grad[...] = grad[...] + back


    def finish_forward():
        x_in[...] = stream[pl.ds(0, tokens), :] * live
        return local(x_in, act_out.at[:, 0], io_sem.at[0])

    swaps = []

    def tiny_send(n):
        device = (mate, side[0], side[1])[n]
        swaps.append(remote(tiny.at[n], tiny_in.at[n], t_send.at[n], t_recv.at[n], device))

    def tiny_add(n):
        swaps[n].wait_recv()
        tiny[n + 1] = tiny[n] + tiny_in[n]

    def finish_backward():
        cot[...] = grad[pl.ds(0, tokens), :]
        return local(cot, grad_out.at[:, 0], io_sem.at[1])

    relay(0)
    relay(1)
    relay(2)
    relay(3)
    relay(4)
    relay(5)
    relay(6)
    relay(7)
    reach(0)
    reach(1)
    reach(2)
    reach(3)
    cross(0)
    reach(4)
    reach(5)
    reach(6)
    reach(7)
    cross(1)
    settle(4)
    project(0)
    for j in range(0, 3):
        attend(0, j)
    cross(2)
    settle(5)
    join(0)
    settle(0)
    for j in range(0, 6):
        expand(0, j)
    settle(1)
    contract(0)
    cross(3)
    settle(6)
    project(1)
    for j in range(0, 3):
        attend(1, j)
    settle(7)
    join(1)
    settle(2)
    for j in range(0, 6):
        expand(1, j)
    settle(3)
    contract(1)
    store_act = finish_forward()
    back_down(1)
    swap(0)
    swap(1)
    for j in range(0, 6):
        back_expand(1, j)
    back_up(1, 0)
    swap(2)
    back_up(1, 1)
    swap(3)
    back_middle(1)
    swap(4)
    scatter_one(0)
    back_attend(1, 0)
    scatter_one(1)
    back_attend(1, 1)
    back_attend(1, 2)
    back_qkv(1, 0)
    back_qkv(1, 1)
    swap(5)
    back_qkv(1, 2)
    swap(6)
    back_first(1)
    back_down(0)
    swap(7)
    scatter_one(2)
    swap(8)
    scatter_one(3)
    for j in range(0, 6):
        back_expand(0, j)
    back_up(0, 0)
    swap(9)
    back_up(0, 1)
    swap(10)
    back_middle(0)
    swap(11)
    scatter_two(0)
    back_attend(0, 0)
    scatter_two(1)
    back_attend(0, 1)
    back_attend(0, 2)
    back_qkv(0, 0)
    back_qkv(0, 1)
    swap(12)
    back_qkv(0, 2)
    swap(13)
    scatter_one(5)
    back_first(0)
    store_grad = finish_backward()
    tiny_send(0)
    scatter_one(4)
    scatter_two(2)
    scatter_two(3)
    tiny_add(0)
    tiny_send(1)
    z_first(1)
    z_first(0)
    scatter_one(6)
    scatter_two(4)
    scatter_one(8)
    scatter_two(5)
    z_second(1)
    z_first(2)
    scatter_one(7)
    z_first(3)
    z_second(0)
    scatter_two(6)
    tiny_add(1)
    tiny_send(2)
    z_first(4)
    z_third(1)
    z_second(2)
    scatter_one(9)
    scatter_one(11)
    scatter_two(8)
    z_third(0)
    z_second(3)
    scatter_two(7)
    z_second(4)
    z_first(5)
    z_first(6)
    z_fourth(1)
    tiny_add(2)
    z_first(n_sub)
    z_third(2)
    scatter_one(10)
    z_fourth(0)
    scatter_two(11)
    z_third(3)
    z_third(4)
    scatter_one(12)
    scatter_two(9)
    z_second(5)
    z_first(7)
    z_second(6)
    z_fourth(2)
    z_first(8)
    z_second(n_sub)
    z_first(11)
    z_fourth(3)
    scatter_one(13)
    z_fourth(4)
    scatter_two(10)
    z_third(5)
    z_second(7)
    z_third(6)
    z_first(9)
    z_third(n_sub)
    scatter_two(12)
    z_second(8)
    z_second(11)
    scatter_two(13)
    z_first(10)
    z_fourth(5)
    z_third(7)
    z_fourth(6)
    z_second(9)
    z_fourth(n_sub)
    z_first(12)
    z_third(8)
    z_first(13)
    z_third(11)
    z_second(10)
    z_fourth(7)
    z_third(9)
    z_second(12)
    z_fourth(8)
    z_second(13)
    z_fourth(11)
    z_third(10)
    z_fourth(9)
    z_third(12)
    z_third(13)
    z_fourth(10)
    z_fourth(12)
    z_fourth(13)
    done = z_fin[n_sub][...]
    picked = None
    for s in range(shards):
        hit = jnp.where(me == s, 1.0, 0.0).astype(FULL)
        term = done[:up_row, s * rows_d : (s + 1) * rows_d] * hit
        picked = term if picked is None else picked + term
    for layer in range(layers):
        small_out[0][layer] = picked[layer * GAIN_ROWS : (layer + 1) * GAIN_ROWS]
        row = None
        for s in range(shards):
            at = up_row + layer * (ff // width) + s
            hit = jnp.where(me == s, 1.0, 0.0).astype(FULL)
            term = done[at : at + 1] * hit
            row = term if row is None else row + term
        small_out[2][pl.ds(layer, 1), :] = row
    for which in range(BIAS_ROWS):
        small_out[1][which] = picked[bias_row(0, which) : bias_row(0, which) + layers]
    for a in range(n_sub + 1):
        z_done(a)
    for copy in sent:
        copy.wait_send()
    store_act.wait()
    store_grad.wait()


def finish_kernel(steps, *refs):
    half = (len(refs) - 1) // 2
    sems = refs[-1]
    copies = [pltpu.make_async_copy(refs[n], refs[half + n], sems.at[n]) for n in range(2)]

    @pl.when(pl.program_id(0) == 0)
    def _():
        for copy in copies:
            copy.start()

    for src, dst in zip(refs[2:half], refs[half + 2 : -1]):
        dst[...] = src[...].astype(FULL)

    @pl.when(pl.program_id(0) == steps - 1)
    def _():
        for copy in copies:
            copy.wait()


def finish(arrays):
    layers = arrays[2].shape[0]
    cuts = 3
    steps = layers * cuts

    def spec(n, x):
        if n < 2:
            return pl.BlockSpec(memory_space=pl.ANY)
        if n < 6:
            block = (1, x.shape[1] // cuts) + x.shape[2:]
            return pl.BlockSpec(block, lambda i: (i // cuts, i % cuts, 0))
        return pl.BlockSpec(x.shape, lambda i: (0,) * x.ndim)

    specs = [spec(n, x) for n, x in enumerate(arrays)]
    return pl.pallas_call(
        functools.partial(finish_kernel, steps),
        grid=(steps,),
        out_shape=[jax.ShapeDtypeStruct(x.shape, FULL) for x in arrays],
        in_specs=specs,
        out_specs=specs,
        scratch_shapes=[pltpu.SemaphoreType.DMA((2,))],
        name="widen",
    )(*arrays)


def on_device(shards, replicas, images, cotangent, counts, *stacks):
    weights, (gains, biases, up_bias) = stacks[:4], stacks[4:]
    layers, rows_d, _ = weights[QKV].shape
    deep = replicas // 2
    tokens, width = images.shape[1:]
    padded = -(-tokens // 16) * 16
    ff = weights[UP].shape[2]
    heads = width // HD
    qkv = weights[QKV].shape[2]
    sems = pltpu.SemaphoreType.DMA
    low = lambda *s: pltpu.VMEM(s, LOW)
    full = lambda *s: pltpu.VMEM(s, FULL)
    small_rows = layers * (GAIN_ROWS + BIAS_ROWS)
    small_rows_pad = -(-small_rows // 8) * 8
    per_up = up_bias.shape[1]
    scratch = [
        full(tokens, width), full(tokens, width), full(padded, width), full(padded, width),
        low(layers, shards * rows_d, qkv), low(layers, shards * rows_d, width),
        low(layers, shards * rows_d, ff), low(layers, ff, width),
        full(small_rows_pad, width), full(8, ff),
        full(small_rows_pad, 128), full(shards, small_rows_pad, 128),
        full(8, per_up), full(shards, 8, per_up),
        full(layers, padded, width), full(layers, padded, 1), low(layers, padded, width),
        low(layers, padded, width), low(layers, padded, width), low(layers, padded, width),
        full(layers, heads, padded, padded), low(layers, padded, width),
        full(layers, padded, width), full(layers, padded, 1), low(layers, padded, width),
        low(layers, padded, ff), full(layers, padded, ff), low(padded, ff), low(padded, width),
        low(padded, qkv),
    ]
    halves = [w.shape[1] // 2 for w in weights]
    columns = [w.shape[2] for w in weights]
    scratch += [low(layers, shards, 2, h, c) for h, c in zip(halves, columns)]
    shapes = [(sub[3], sub[5]) for sub in sub_items(layers, weights, shards)]
    n_sub = len(shapes)
    scratch += [low(shards, *s) for s in shapes] + [low(3, *s) for s in shapes] * 2
    tiny_rows = small_rows + layers * (ff // width)
    scratch += ([low(*s) for s in shapes] + [full(tiny_rows, width)]) * 4
    scratch += [full(4, tiny_rows, width), full(3, tiny_rows, width)]
    n_items = 4 * layers
    scratch += [
        sems((n_items, 2)), sems((n_items, 2)), sems((n_items,)), sems((n_items,)),
        sems((n_items, 3)), sems((n_items, 3)), sems((n_items, 3)), sems((n_items, 3)),
        sems((n_items, 3)), sems((n_items, 3)), sems((2, 3)), sems((2, 3)),
        sems((n_items,)), sems((4,)), sems((n_sub,)), sems((n_sub,)), sems((n_sub,)),
        sems((n_sub,)), sems((n_sub,)), sems((n_sub,)), sems((n_sub + 1, 3)), sems((n_sub + 1, 3)),
        sems((n_sub,)), sems((n_sub,)), sems((n_sub,)), sems((3,)), sems((3,)),
    ]
    shape = jax.ShapeDtypeStruct
    images, cotangent, biases = (x.transpose(1, 0, 2) for x in (images, cotangent, biases))
    outs = [shape(images.shape, FULL), shape(images.shape, FULL)]
    outs += [shape((layers, 2, h, c), LOW) for h, c in zip(halves, columns)]
    outs += [shape(x.shape, FULL) for x in (gains, biases, up_bias)]
    hbm, vmem = pl.BlockSpec(memory_space=pl.ANY), pl.BlockSpec(memory_space=pltpu.VMEM)
    done = pl.pallas_call(
        functools.partial(fused_kernel, shards, deep),
        out_shape=outs,
        in_specs=[hbm, hbm, pl.BlockSpec(memory_space=pltpu.SMEM)] + [hbm] * 4 + [vmem] * 3,
        out_specs=[hbm] * 6 + [vmem] * 3,
        scratch_shapes=scratch,
        compiler_params=pltpu.CompilerParams(
            collective_id=0, has_side_effects=True, vmem_limit_bytes=VMEM_LIMIT
        ),
        name="encoder_step",
    )(images, cotangent, counts, *weights, gains, biases, up_bias)
    done = list(done)
    for kind in range(4):
        done[2 + kind] = done[2 + kind].reshape(weights[kind].shape)
    done = list(finish(done))
    for n in (0, 1, 7):
        done[n] = done[n].transpose(1, 0, 2)
    return tuple(done)


def solution(mesh):
    in_specs = (
        P(("shard", "replica"), None, None),
        P(("shard", "replica"), None, None),
        P(("shard", "replica")),
        P(None, "shard", None),
        P(None, "shard", None),
        P(None, "shard", None),
        P(None, "shard", None),
        P(None, None, "shard"),
        P(None, None, "shard"),
        P(None, "shard"),
    )
    out_specs = (
        P(("shard", "replica"), None, None),
        P(("shard", "replica"), None, None),
        P(None, "shard", None),
        P(None, "shard", None),
        P(None, "shard", None),
        P(None, "shard", None),
        P(None, None, "shard"),
        P(None, None, "shard"),
        P(None, "shard"),
    )
    return jax.shard_map(
        functools.partial(on_device, mesh.shape["shard"], mesh.shape["replica"]), mesh=mesh, in_specs=in_specs, out_specs=out_specs, check_vma=False
    )
```

```python
import functools

import jax
import jax.numpy as jnp
from jax import lax
from jax.experimental import pallas as pl
from jax.experimental.pallas import tpu as pltpu
from jax.sharding import PartitionSpec as P

HD = 64
EPS = 1e-06
INV_ROOT_TWO = 0.7071067811865476
INV_ROOT_TWO_PI = 0.3989422804014327
LOW = jnp.bfloat16
FULL = jnp.float32
MESH = pl.DeviceIdType.MESH
VMEM_LIMIT = 60 * 1024 * 1024

QKV, OUT, UP, DOWN = range(4)
GAIN_ROWS, BIAS_ROWS = 2, 6


def product(left, right):
    return jnp.dot(left, right, preferred_element_type=FULL)


def product_left(left, right):
    return lax.dot_general(
        left, right, (((0,), (0,)), ((), ())), preferred_element_type=FULL
    )


def product_right(left, right):
    return lax.dot_general(
        left, right, (((1,), (1,)), ((), ())), preferred_element_type=FULL
    )


def wide(value):
    return value.astype(FULL)


def column_sum(value):
    return jnp.sum(value, 0, keepdims=True)


def standardize(values):
    center = jnp.mean(values, -1, keepdims=True)
    centered = values - center
    spread = jnp.mean(centered * centered, -1, keepdims=True)
    inverse = lax.rsqrt(spread + EPS)
    return centered * inverse, inverse


def norm_back(upstream, unit, inverse, gain):
    scaled = upstream * gain
    inner = (
        scaled
        - jnp.mean(scaled, -1, keepdims=True)
        - unit * jnp.mean(scaled * unit, -1, keepdims=True)
    )
    return inverse * inner, column_sum(upstream * unit), column_sum(upstream)


SUBS = 7


def sub_items(layers, weights, shards):
    width, ff, qkv = (weights[kind].shape[2] for kind in (OUT, UP, QKV))
    half_d = weights[QKV].shape[1] // 2
    rows = weights[DOWN].shape[1] // 4
    cut = (qkv + width) // 2
    subs = []
    for layer in reversed(range(layers)):
        subs += [
            (DOWN, layer, 0, rows, 0, width, 0),
            (DOWN, layer, rows, rows, 0, width, 1),
            (UP, layer, 0, half_d, 0, ff // 2, 0),
            (UP, layer, 0, half_d, ff // 2, ff // 2, 1),
            (OUT, layer, 0, half_d, 0, width, 1),
            (QKV, layer, 0, half_d, 0, cut, 0),
            (QKV, layer, 0, half_d, cut, qkv - cut, 1),
        ]
    return subs


def fused_kernel(shards, deep, *refs):
    (images, cotangent, counts, *own_w), refs = refs[:7], refs[7:]
    (gains, biases, up_bias), refs = refs[:3], refs[3:]
    (act_out, grad_out), refs = refs[:2], refs[2:]
    totals, refs = refs[:4], refs[4:]
    small_out, refs = refs[:3], refs[3:]
    (x_in, cot, stream, grad, w_qkv, w_out, w_up, w_down, par, par_up, small, small_all, wide_small,
     wide_all), refs = refs[:14], refs[14:]
    (unit_one, inv_one, normed_one, queries, key_rows, values, probs, mixed, unit_two, inv_two,
     normed_two, activated, slope, hid_low, mix_grad, pgrad), refs = refs[:16], refs[16:]
    own_g, refs = refs[:4], refs[4:]
    n_sub = SUBS * own_w[0].shape[0]
    buf_a, refs = refs[:n_sub], refs[n_sub:]
    buf_s, refs = refs[:n_sub], refs[n_sub:]
    buf_b, refs = refs[:n_sub], refs[n_sub:]
    z_own, refs = refs[: n_sub + 1], refs[n_sub + 1 :]
    z_in, refs = refs[: n_sub + 1], refs[n_sub + 1 :]
    z_cross, refs = refs[: n_sub + 1], refs[n_sub + 1 :]
    z_fin, refs = refs[: n_sub + 1], refs[n_sub + 1 :]
    (tiny, tiny_in), refs = refs[:2], refs[2:]
    (f_send, f_recv, r_send, r_recv, m_send, m_recv, x_send, x_recv, q_send, q_recv, p_send, p_recv,
     own_sem, io_sem, a_send, a_recv, b_send, b_recv, c_send, c_recv, z_send, z_recv, e_send, e_recv,
     fin_sem, t_send, t_recv) = refs

    layers, rows_d, _ = own_w[QKV].shape
    width = x_in.shape[1]
    tokens = x_in.shape[0]
    padded = stream.shape[0]
    heads = width // HD
    ff = w_up.shape[2]
    factor = HD ** (-0.5)
    weights = (w_qkv, w_out, w_up, w_down)

    me = lax.axis_index("shard")
    rep = lax.axis_index("replica")
    core = lax.rem(rep, 2)
    depth = lax.div(rep, 2)
    parity = lax.rem(depth, 2)
    mid = deep // 2
    left = depth < mid
    place = jnp.where(left, depth, deep - 1 - depth)
    inner_depth = jnp.where(left, depth + 1, depth - 1)
    outer_depth = jnp.where(left, depth - 1, depth + 1)
    mate = (me, rep + 1 - 2 * core)
    across = (me, (depth + 1 - 2 * parity) * 2 + core)
    inner = (me, inner_depth * 2 + core)
    outer = (me, outer_depth * 2 + core)
    side_me = (me + 1 - 2 * lax.rem(me, 2), lax.rem(me + 2, shards))
    side = [(s, rep) for s in side_me]
    far_me = shards - 1 - me
    inside = place > 0
    center = place == mid - 1

    def local(src, dst, sem):
        copy = pltpu.make_async_copy(src, dst, sem)
        copy.start()
        return copy

    load_x = local(images.at[:, 0], x_in, io_sem.at[0])
    load_cot = local(cotangent.at[:, 0], cot, io_sem.at[1])

    barrier = pltpu.get_barrier_semaphore()
    for device in (mate, across, side[0], side[1], (far_me, rep), inner):
        pl.semaphore_signal(barrier, inc=1, device_id=device, device_id_type=MESH)

    @pl.when(inside)
    def _():
        pl.semaphore_signal(barrier, inc=1, device_id=outer, device_id_type=MESH)

    sent = []

    def remote(src, dst, send_sem, recv_sem, device, keep=True):
        copy = pltpu.make_async_remote_copy(
            src_ref=src, dst_ref=dst, send_sem=send_sem, recv_sem=recv_sem, device_id=device,
            device_id_type=MESH)
        copy.start()
        if keep:
            sent.append(copy)
        return copy

    items = [(kind, layer) for layer in range(layers) for kind in (UP, DOWN)]
    items += [(kind, layer) for layer in range(layers) for kind in (QKV, OUT)]
    via_of, loads = [], [0, 0]
    for kind, _ in items:
        via_of.append(0 if loads[1] <= loads[0] else 1)
        loads[1 - via_of[-1]] += own_w[kind].shape[1] * own_w[kind].shape[2] // (
            2 if kind in (UP, DOWN) else 1)

    def part(ref, kind, layer, first_row, rows, which):
        half = rows // 2
        start = first_row + core * half
        if kind == UP:
            cut = ff // 2
            return ref.at[layer, pl.ds(pl.multiple_of(start, 16), half),
                          pl.ds(pl.multiple_of(which * cut, 128), cut)]
        if kind == DOWN:
            return ref.at[layer, pl.ds(pl.multiple_of(start + which * (half // 2), 16), half // 2)]
        return ref.at[layer, pl.ds(pl.multiple_of(start, 16), half)]

    def held(item, shard, which):
        kind, layer = items[item]
        rows = own_w[kind].shape[1]
        return part(weights[kind], kind, layer, shard * rows, rows, which)

    firsts, relays, passed, crossed, again, owned = {}, {}, {}, {}, {}, {}

    def first(item):
        kind, layer = items[item]
        rows = own_w[kind].shape[1]
        src = part(own_w[kind], kind, layer, 0, rows, parity)
        firsts[item] = [
            remote(src, held(item, me, parity), f_send.at[item, k], f_recv.at[item, k], side[k])
            for k in range(2)
        ]
        owned[item] = local(
            own_w[kind].at[layer],
            weights[kind].at[layer, pl.ds(pl.multiple_of(me * rows, 16), rows)], own_sem.at[item])
        passed[item] = []
        crossed[item] = []

    def hand_on(item, slot, shard):
        piece = held(item, shard, parity)
        if items[item][0] in (UP, DOWN):
            crossed[item].append((slot, shard, remote(
                piece, piece, x_send.at[item, slot], x_recv.at[item, slot], across)))
        passed[item].append(
            remote(piece, piece, m_send.at[item, slot], m_recv.at[item, slot], mate))

    def relay(item):
        via = via_of[item]
        for k in (via, 1 - via):
            firsts[item][k].wait_recv()
            if k == via:
                piece = held(item, side_me[k], parity)
                relays[item] = remote(
                    piece, piece, r_send.at[item], r_recv.at[item], side[1 - k])
            hand_on(item, k, side_me[k])

    def reach(item):
        relays[item].wait_recv()
        hand_on(item, 2, far_me)

    def cross(item):
        for slot, shard, copy in crossed[item]:
            copy.wait_recv()
            piece = held(item, shard, 1 - parity)
            passed[item].append(
                remote(piece, piece, q_send.at[item, slot], q_recv.at[item, slot], mate))

    def settle(item):
        for copy in passed[item]:
            copy.wait_recv()
        owned[item].wait()

    small[...] = jnp.zeros_like(small)
    wide_small[...] = jnp.zeros_like(wide_small)
    for layer in range(layers):
        small[pl.ds(layer * GAIN_ROWS, GAIN_ROWS), pl.ds(0, rows_d)] = wide(gains[layer])
    for which in range(BIAS_ROWS):
        small[pl.ds((GAIN_ROWS + which) * layers, layers), pl.ds(0, rows_d)] = wide(biases[which])
    wide_small[pl.ds(0, layers), :] = wide(up_bias[...])

    pl.semaphore_wait(barrier, 6 + jnp.where(inside, 1, 0))

    tinies = []
    for k, shard in enumerate(side_me + (far_me,)):
        tinies.append(remote(
            small, small_all.at[me], p_send.at[0, k], p_recv.at[0, k], (shard, rep)))
        tinies.append(remote(
            wide_small, wide_all.at[me], p_send.at[1, k], p_recv.at[1, k], (shard, rep)))
    tinies_own = [
        local(small, small_all.at[me], io_sem.at[2]),
        local(wide_small, wide_all.at[me], io_sem.at[3]),
    ]

    for item in range(len(items)):
        first(item)
    load_x.wait()
    stream[...] = jnp.zeros_like(stream)
    stream[pl.ds(0, tokens), :] = x_in[...]
    unit, inverse = standardize(stream[...])
    unit_one[0] = unit
    inv_one[0] = inverse
    live = jnp.where(counts[0] > 0, 1.0, 0.0).astype(FULL)
    load_cot.wait()
    grad[...] = jnp.zeros_like(grad)
    grad[pl.ds(0, tokens), :] = cot[...] * live

    for copy in tinies:
        copy.wait_recv()
    for copy in tinies_own:
        copy.wait()
    for s in range(shards):
        par[:, pl.ds(s * rows_d, rows_d)] = small_all[s][:, :rows_d]
        per = wide_small.shape[1]
        par_up[:, pl.ds(s * per, per)] = wide_all[s]

    def gain_of(layer, which):
        return par[pl.ds(layer * GAIN_ROWS + which, 1), :]

    def bias_row(layer, which):
        return (GAIN_ROWS + which) * layers + layer

    def bias_of(layer, which):
        return par[pl.ds(bias_row(layer, which), 1), :]

    key_mask = jnp.where(
        lax.broadcasted_iota(jnp.int32, (1, padded), 1) < tokens, 0.0, -1e30).astype(FULL)
    lane_half = lax.broadcasted_iota(jnp.int32, (padded, 2 * HD), 1) < HD

    def one_head(value, which):
        keep = lane_half if which == 0 else jnp.logical_not(lane_half)
        return jnp.where(keep, value, jnp.zeros_like(value))

    def pair(p):
        return pl.ds(p * 2 * HD, 2 * HD)

    def project(layer):
        normed = (unit_one[layer] * gain_of(layer, 0) + bias_of(layer, 0)).astype(LOW)
        normed_one[layer] = normed
        queries[layer] = (
            (product(normed, w_qkv[layer, :, pl.ds(0, width)]) + bias_of(layer, 1)) * factor
        ).astype(LOW)
        key_rows[layer] = product(normed, w_qkv[layer, :, pl.ds(width, width)]).astype(LOW)
        values[layer] = (
            product(normed, w_qkv[layer, :, pl.ds(2 * width, width)]) + bias_of(layer, 2)
        ).astype(LOW)

    def attend(layer, p):
        q, k, v = (ref[layer, :, pair(p)] for ref in (queries, key_rows, values))
        total = None
        for h in range(2):
            scores = product_right(one_head(q, h), k) + key_mask
            log_total = jnp.log(jnp.sum(jnp.exp(scores), -1, keepdims=True))
            prob = jnp.exp(scores - log_total)
            probs[layer, 2 * p + h] = prob
            term = product(prob.astype(LOW), one_head(v, h))
            total = term if total is None else total + term
        mixed[layer, :, pair(p)] = total.astype(LOW)

    def join(layer):
        middle = stream[...] + product(mixed[layer], w_out[layer]) + bias_of(layer, 3)
        stream[...] = middle
        unit, inverse = standardize(middle)
        unit_two[layer] = unit
        inv_two[layer] = inverse
        normed_two[layer] = (unit * gain_of(layer, 1) + bias_of(layer, 4)).astype(LOW)

    chunk = 256

    def expand(layer, j):
        cols = pl.ds(j * chunk, chunk)
        hidden = product(normed_two[layer], w_up[layer, :, cols]) + par_up[pl.ds(layer, 1), cols]
        below = 0.5 * (1.0 + lax.erf(hidden * INV_ROOT_TWO))
        activated[layer, :, cols] = (hidden * below).astype(LOW)
        dens = jnp.exp(-0.5 * hidden * hidden) * INV_ROOT_TWO_PI
        slope[layer, :, cols] = below + hidden * dens

    def contract(layer):
        result = stream[...] + product(activated[layer], w_down[layer]) + bias_of(layer, 5)
        stream[...] = result
        if layer + 1 < layers:
            unit, inverse = standardize(result)
            unit_one[layer + 1] = unit
            inv_one[layer + 1] = inverse

    subs = sub_items(layers, own_w, shards)
    stage_a, one, two = {}, {}, {}

    def mine(a, dest, half):
        kind, layer, row, rows, start, cols, _ = subs[a]
        return own_g[kind].at[layer, dest, half, pl.ds(row, rows), pl.ds(start, cols)]

    def swap(a):
        kind, layer, row, rows, start, cols, _ = subs[a]
        stage_a[a] = remote(
            own_g[kind].at[layer, :, 1 - core, pl.ds(row, rows), pl.ds(start, cols)], buf_a[a],
            a_send.at[a], a_recv.at[a], mate)

    def both(a, dest):
        return wide(mine(a, dest, core)[...]) + wide(buf_a[a][dest])

    def scatter_one(a):
        turn = subs[a][-1]
        stage_a[a].wait_recv()
        near = side_me[turn]
        buf_s[a][0] = both(a, near).astype(LOW)
        buf_s[a][1] = both(a, far_me).astype(LOW)
        one[a] = remote(
            buf_s[a].at[pl.ds(0, 2)], buf_b[a].at[pl.ds(0, 2)], b_send.at[a], b_recv.at[a],
            side[turn])

    def scatter_two(a):
        turn = 1 - subs[a][-1]
        one[a].wait_recv()
        buf_s[a][2] = (both(a, side_me[turn]) + wide(buf_b[a][1])).astype(LOW)
        two[a] = remote(buf_s[a].at[2], buf_b[a].at[2], c_send.at[a], c_recv.at[a], side[turn])

    def summed(a):
        if a == n_sub:
            return tiny[3]
        return both(a, me) + wide(buf_b[a][0]) + wide(buf_b[a][2])

    def z_first(a):
        if a < n_sub:
            two[a].wait_recv()
        z_own[a][...] = summed(a).astype(z_own[a].dtype)

        @pl.when(jnp.logical_and(jnp.logical_not(inside), jnp.logical_not(center)))
        def _():
            remote(z_own[a], z_in[a], z_send.at[a, 0], z_recv.at[a, 0], inner, keep=False)

    def described(src, dst, send_sem, recv_sem, device):
        return pltpu.make_async_remote_copy(
            src_ref=src, dst_ref=dst, send_sem=send_sem, recv_sem=recv_sem, device_id=device,
            device_id_type=MESH)

    def z_copy(a):
        return described(z_own[a], z_in[a], z_send.at[a, 0], z_recv.at[a, 0], inner)

    def x_copy(a):
        return described(z_own[a], z_cross[a], z_send.at[a, 1], z_recv.at[a, 1], inner)

    def o_copy(a):
        return described(z_fin[a], z_fin[a], z_send.at[a, 2], z_recv.at[a, 2], outer)

    def z_second(a):
        @pl.when(inside)
        def _():
            z_copy(a).wait_recv()
            z_own[a][...] = (summed(a) + wide(z_in[a][...])).astype(z_own[a].dtype)

            @pl.when(jnp.logical_not(center))
            def _():
                z_copy(a).start()

        @pl.when(center)
        def _():
            x_copy(a).start()

    def goal(a):
        kind, layer, row, rows, start, cols, _ = subs[a]
        return totals[kind].at[layer, core, pl.ds(row, rows), pl.ds(start, cols)]

    def e_copy(a):
        return described(z_fin[a], goal(a), e_send.at[a], e_recv.at[a], mate)

    def fin_copy(a):
        return pltpu.make_async_copy(z_fin[a], goal(a), fin_sem.at[a])

    def spread(a):
        @pl.when(inside)
        def _():
            o_copy(a).start()

        if a < n_sub:
            e_copy(a).start()
            fin_copy(a).start()

    def z_third(a):
        @pl.when(center)
        def _():
            x_copy(a).wait_recv()
            z_fin[a][...] = (wide(z_own[a][...]) + wide(z_cross[a][...])).astype(z_fin[a].dtype)
            spread(a)

    def z_fourth(a):
        @pl.when(jnp.logical_not(center))
        def _():
            o_copy(a).wait_recv()
            spread(a)

    def z_done(a):
        if a < n_sub:
            e_copy(a).wait()
            fin_copy(a).wait()

        @pl.when(jnp.logical_not(center))
        def _():
            z_copy(a).wait_send()

        @pl.when(center)
        def _():
            x_copy(a).wait_send()

        @pl.when(inside)
        def _():
            o_copy(a).wait_send()

    def shared(value):
        return value.reshape(shards, 2, value.shape[0] // shards // 2, value.shape[1]).astype(LOW)

    up_row = layers * (GAIN_ROWS + BIAS_ROWS)

    def put_up_bias(layer, start, value):
        for at in range(0, value.shape[1], 128):
            row, lane = divmod(start + at, width)
            tiny[0, pl.ds(up_row + layer * (ff // width) + row, 1), pl.ds(lane, 128)] = (
                value[:, at : at + 128])

    def put_gain(layer, which, value):
        tiny[0, pl.ds(layer * GAIN_ROWS + which, 1), :] = value

    def put_bias(layer, which, value):
        tiny[0, pl.ds(bias_row(layer, which), 1), :] = value

    def back_down(layer):
        low = grad[...].astype(LOW)
        per = ff // shards
        for s in range(shards):
            piece = product_left(activated[layer, :, pl.ds(s * per, per)], low)
            own_g[DOWN][layer, s] = piece.reshape(2, per // 2, width).astype(LOW)
        put_bias(layer, 5, column_sum(grad[...]))

    def back_expand(layer, j):
        low = grad[...].astype(LOW)
        cols = pl.ds(j * chunk, chunk)
        act_grad = product_right(low, w_down[layer, cols, :])
        hid_grad = act_grad * slope[layer, :, cols]
        put_up_bias(layer, j * chunk, column_sum(hid_grad))
        hid_low[:, cols] = hid_grad.astype(LOW)

    def back_up(layer, j):
        cols = pl.ds(j * ff // 2, ff // 2)
        own_g[UP][layer, :, :, :, cols] = shared(product_left(normed_two[layer], hid_low[:, cols]))

    def back_middle(layer):
        norm_grad = product_right(hid_low[...], w_up[layer])
        back, gain, shift = norm_back(
            norm_grad, unit_two[layer], inv_two[layer], gain_of(layer, 1))
        put_gain(layer, 1, gain)
        put_bias(layer, 4, shift)
        mid_grad = grad[...] + back
        grad[...] = mid_grad
        put_bias(layer, 3, column_sum(mid_grad))
        mid_low = mid_grad.astype(LOW)
        own_g[OUT][layer] = shared(product_left(mixed[layer], mid_low))
        mix_grad[...] = product_right(mid_low, w_out[layer]).astype(LOW)

    def back_attend(layer, p):
        q, k, v = (ref[layer, :, pair(p)] for ref in (queries, key_rows, values))
        up = mix_grad[:, pair(p)]
        sums = [None] * 3
        for h in range(2):
            up_h = one_head(up, h)
            prob = probs[layer, 2 * p + h]
            prob_grad = product_right(up_h, v)
            row_dot = jnp.sum(prob * prob_grad, -1, keepdims=True)
            score_grad = (prob * (prob_grad - row_dot)).astype(LOW)
            terms = (
                product(score_grad, one_head(k, h)),
                product_left(score_grad, one_head(q, h)),
                product_left(prob.astype(LOW), up_h),
            )
            sums = [t if s is None else s + t for s, t in zip(sums, terms)]
        query_grad = sums[0] * factor
        start = p * 2 * HD
        tiny[0, pl.ds(bias_row(layer, 1), 1), pair(p)] = column_sum(query_grad)
        tiny[0, pl.ds(bias_row(layer, 2), 1), pair(p)] = column_sum(sums[2])
        for n, value in enumerate((query_grad, sums[1], sums[2])):
            pgrad[:, pl.ds(n * width + start, 2 * HD)] = value.astype(LOW)

    def back_qkv(layer, n):
        cols = pl.ds(n * width, width)
        own_g[QKV][layer, :, :, :, cols] = shared(product_left(normed_one[layer], pgrad[:, cols]))

    def back_first(layer):
        first_grad = product_right(pgrad[...], w_qkv[layer])
        back, gain, shift = norm_back(
            first_grad, unit_one[layer], inv_one[layer], gain_of(layer, 0))
        put_gain(layer, 0, gain)
        put_bias(layer, 0, shift)
        grad[...] = grad[...] + back


    def finish_forward():
        x_in[...] = stream[pl.ds(0, tokens), :] * live
        return local(x_in, act_out.at[:, 0], io_sem.at[0])

    swaps = []

    def tiny_send(n):
        device = (mate, side[0], side[1])[n]
        swaps.append(remote(tiny.at[n], tiny_in.at[n], t_send.at[n], t_recv.at[n], device))

    def tiny_add(n):
        swaps[n].wait_recv()
        tiny[n + 1] = tiny[n] + tiny_in[n]

    def finish_backward():
        cot[...] = grad[pl.ds(0, tokens), :]
        return local(cot, grad_out.at[:, 0], io_sem.at[1])

    relay(0)
    relay(1)
    relay(2)
    relay(3)
    relay(4)
    relay(5)
    relay(6)
    relay(7)
    reach(0)
    reach(1)
    reach(2)
    reach(3)
    cross(0)
    reach(4)
    reach(5)
    reach(6)
    reach(7)
    cross(1)
    settle(4)
    project(0)
    for j in range(0, 3):
        attend(0, j)
    cross(2)
    settle(5)
    join(0)
    settle(0)
    for j in range(0, 6):
        expand(0, j)
    settle(1)
    contract(0)
    cross(3)
    settle(6)
    project(1)
    for j in range(0, 3):
        attend(1, j)
    settle(7)
    join(1)
    settle(2)
    for j in range(0, 6):
        expand(1, j)
    settle(3)
    contract(1)
    store_act = finish_forward()
    back_down(1)
    swap(0)
    swap(1)
    for j in range(0, 6):
        back_expand(1, j)
    back_up(1, 0)
    swap(2)
    back_up(1, 1)
    swap(3)
    back_middle(1)
    swap(4)
    scatter_one(0)
    back_attend(1, 0)
    scatter_one(1)
    back_attend(1, 1)
    back_attend(1, 2)
    back_qkv(1, 0)
    back_qkv(1, 1)
    swap(5)
    back_qkv(1, 2)
    swap(6)
    back_first(1)
    back_down(0)
    swap(7)
    scatter_one(2)
    swap(8)
    scatter_one(3)
    for j in range(0, 6):
        back_expand(0, j)
    back_up(0, 0)
    swap(9)
    back_up(0, 1)
    swap(10)
    back_middle(0)
    swap(11)
    scatter_two(0)
    back_attend(0, 0)
    scatter_two(1)
    back_attend(0, 1)
    back_attend(0, 2)
    back_qkv(0, 0)
    back_qkv(0, 1)
    swap(12)
    back_qkv(0, 2)
    swap(13)
    scatter_one(5)
    back_first(0)
    store_grad = finish_backward()
    tiny_send(0)
    scatter_one(4)
    scatter_two(2)
    scatter_two(3)
    tiny_add(0)
    tiny_send(1)
    z_first(1)
    z_first(0)
    scatter_one(6)
    scatter_two(4)
    scatter_one(8)
    scatter_two(5)
    z_second(1)
    z_first(2)
    scatter_one(7)
    z_first(3)
    z_second(0)
    scatter_two(6)
    tiny_add(1)
    tiny_send(2)
    z_first(4)
    z_third(1)
    z_second(2)
    scatter_one(9)
    scatter_one(11)
    scatter_two(8)
    z_third(0)
    z_second(3)
    scatter_two(7)
    z_second(4)
    z_first(5)
    z_first(6)
    z_fourth(1)
    tiny_add(2)
    z_first(n_sub)
    z_third(2)
    scatter_one(10)
    z_fourth(0)
    scatter_two(11)
    z_third(3)
    z_third(4)
    scatter_one(12)
    scatter_two(9)
    z_second(5)
    z_first(7)
    z_second(6)
    z_fourth(2)
    z_first(8)
    z_second(n_sub)
    z_first(11)
    z_fourth(3)
    scatter_one(13)
    z_fourth(4)
    scatter_two(10)
    z_third(5)
    z_second(7)
    z_third(6)
    z_first(9)
    z_third(n_sub)
    scatter_two(12)
    z_second(8)
    z_second(11)
    scatter_two(13)
    z_first(10)
    z_fourth(5)
    z_third(7)
    z_fourth(6)
    z_second(9)
    z_fourth(n_sub)
    z_first(12)
    z_third(8)
    z_first(13)
    z_third(11)
    z_second(10)
    z_fourth(7)
    z_third(9)
    z_second(12)
    z_fourth(8)
    z_second(13)
    z_fourth(11)
    z_third(10)
    z_fourth(9)
    z_third(12)
    z_third(13)
    z_fourth(10)
    z_fourth(12)
    z_fourth(13)
    done = z_fin[n_sub][...]
    picked = None
    for s in range(shards):
        hit = jnp.where(me == s, 1.0, 0.0).astype(FULL)
        term = done[:up_row, s * rows_d : (s + 1) * rows_d] * hit
        picked = term if picked is None else picked + term
    for layer in range(layers):
        small_out[0][layer] = picked[layer * GAIN_ROWS : (layer + 1) * GAIN_ROWS]
        row = None
        for s in range(shards):
            at = up_row + layer * (ff // width) + s
            hit = jnp.where(me == s, 1.0, 0.0).astype(FULL)
            term = done[at : at + 1] * hit
            row = term if row is None else row + term
        small_out[2][pl.ds(layer, 1), :] = row
    for which in range(BIAS_ROWS):
        small_out[1][which] = picked[bias_row(0, which) : bias_row(0, which) + layers]
    for a in range(n_sub + 1):
        z_done(a)
    for copy in sent:
        copy.wait_send()
    store_act.wait()
    store_grad.wait()


def finish_kernel(count, *refs):
    ins, outs, refs = refs[:count], refs[count : 2 * count], refs[2 * count :]
    held, refs = refs[:count], refs[count:]
    wides, (load_sem, store_sem) = refs[:-2], refs[-2:]
    parts = []
    for n in range(2, 6):
        parts += [(n, layer) for layer in range(ins[n].shape[0])]
    parts += [(n, None) for n in range(count) if not 2 <= n < 6]

    def view(ref, layer):
        return ref if layer is None else ref.at[layer]

    loads, stores = [], []
    for at, (n, layer) in enumerate(parts):
        copy = pltpu.make_async_copy(view(ins[n], layer), view(held[n], layer), load_sem.at[at])
        copy.start()
        loads.append(copy)
    for at, (n, layer) in enumerate(parts):
        loads[at].wait()
        src = held[n]
        if layer is not None:
            src = wides[n - 2]
            src[layer] = held[n][layer].astype(FULL)
        copy = pltpu.make_async_copy(view(src, layer), view(outs[n], layer), store_sem.at[at])
        copy.start()
        stores.append(copy)
    for copy in stores:
        copy.wait()


def finish(arrays):
    count = len(arrays)
    parts = count - 4 + 4 * arrays[2].shape[0]
    specs = [pl.BlockSpec(memory_space=pl.ANY)] * count
    return pl.pallas_call(
        functools.partial(finish_kernel, count),
        out_shape=[jax.ShapeDtypeStruct(x.shape, FULL) for x in arrays],
        in_specs=specs,
        out_specs=specs,
        scratch_shapes=[pltpu.VMEM(x.shape, x.dtype) for x in arrays]
        + [pltpu.VMEM(x.shape, FULL) for x in arrays[2:6]]
        + [pltpu.SemaphoreType.DMA((parts,))] * 2,
        compiler_params=pltpu.CompilerParams(vmem_limit_bytes=VMEM_LIMIT),
        name="widen",
    )(*arrays)


def on_device(shards, replicas, images, cotangent, counts, *stacks):
    weights, (gains, biases, up_bias) = stacks[:4], stacks[4:]
    layers, rows_d, _ = weights[QKV].shape
    deep = replicas // 2
    tokens, width = images.shape[1:]
    padded = -(-tokens // 16) * 16
    ff = weights[UP].shape[2]
    heads = width // HD
    qkv = weights[QKV].shape[2]
    sems = pltpu.SemaphoreType.DMA
    low = lambda *s: pltpu.VMEM(s, LOW)
    full = lambda *s: pltpu.VMEM(s, FULL)
    small_rows = layers * (GAIN_ROWS + BIAS_ROWS)
    small_rows_pad = -(-small_rows // 8) * 8
    per_up = up_bias.shape[1]
    scratch = [
        full(tokens, width), full(tokens, width), full(padded, width), full(padded, width),
        low(layers, shards * rows_d, qkv), low(layers, shards * rows_d, width),
        low(layers, shards * rows_d, ff), low(layers, ff, width),
        full(small_rows_pad, width), full(8, ff),
        full(small_rows_pad, 128), full(shards, small_rows_pad, 128),
        full(8, per_up), full(shards, 8, per_up),
        full(layers, padded, width), full(layers, padded, 1), low(layers, padded, width),
        low(layers, padded, width), low(layers, padded, width), low(layers, padded, width),
        full(layers, heads, padded, padded), low(layers, padded, width),
        full(layers, padded, width), full(layers, padded, 1), low(layers, padded, width),
        low(layers, padded, ff), full(layers, padded, ff), low(padded, ff), low(padded, width),
        low(padded, qkv),
    ]
    halves = [w.shape[1] // 2 for w in weights]
    columns = [w.shape[2] for w in weights]
    scratch += [low(layers, shards, 2, h, c) for h, c in zip(halves, columns)]
    shapes = [(sub[3], sub[5]) for sub in sub_items(layers, weights, shards)]
    n_sub = len(shapes)
    scratch += [low(shards, *s) for s in shapes] + [low(3, *s) for s in shapes] * 2
    tiny_rows = small_rows + layers * (ff // width)
    scratch += ([low(*s) for s in shapes] + [full(tiny_rows, width)]) * 4
    scratch += [full(4, tiny_rows, width), full(3, tiny_rows, width)]
    n_items = 4 * layers
    scratch += [
        sems((n_items, 2)), sems((n_items, 2)), sems((n_items,)), sems((n_items,)),
        sems((n_items, 3)), sems((n_items, 3)), sems((n_items, 3)), sems((n_items, 3)),
        sems((n_items, 3)), sems((n_items, 3)), sems((2, 3)), sems((2, 3)),
        sems((n_items,)), sems((4,)), sems((n_sub,)), sems((n_sub,)), sems((n_sub,)),
        sems((n_sub,)), sems((n_sub,)), sems((n_sub,)), sems((n_sub + 1, 3)), sems((n_sub + 1, 3)),
        sems((n_sub,)), sems((n_sub,)), sems((n_sub,)), sems((3,)), sems((3,)),
    ]
    shape = jax.ShapeDtypeStruct
    images, cotangent, biases = (x.transpose(1, 0, 2) for x in (images, cotangent, biases))
    outs = [shape(images.shape, FULL), shape(images.shape, FULL)]
    outs += [shape((layers, 2, h, c), LOW) for h, c in zip(halves, columns)]
    outs += [shape(x.shape, FULL) for x in (gains, biases, up_bias)]
    hbm, vmem = pl.BlockSpec(memory_space=pl.ANY), pl.BlockSpec(memory_space=pltpu.VMEM)
    done = pl.pallas_call(
        functools.partial(fused_kernel, shards, deep),
        out_shape=outs,
        in_specs=[hbm, hbm, pl.BlockSpec(memory_space=pltpu.SMEM)] + [hbm] * 4 + [vmem] * 3,
        out_specs=[hbm] * 6 + [vmem] * 3,
        scratch_shapes=scratch,
        compiler_params=pltpu.CompilerParams(
            collective_id=0, has_side_effects=True, vmem_limit_bytes=VMEM_LIMIT
        ),
        name="encoder_step",
    )(images, cotangent, counts, *weights, gains, biases, up_bias)
    done = list(done)
    for kind in range(4):
        done[2 + kind] = done[2 + kind].reshape(weights[kind].shape)
    done = list(finish(done))
    for n in (0, 1, 7):
        done[n] = done[n].transpose(1, 0, 2)
    return tuple(done)


def solution(mesh):
    in_specs = (
        P(("shard", "replica"), None, None),
        P(("shard", "replica"), None, None),
        P(("shard", "replica")),
        P(None, "shard", None),
        P(None, "shard", None),
        P(None, "shard", None),
        P(None, "shard", None),
        P(None, None, "shard"),
        P(None, None, "shard"),
        P(None, "shard"),
    )
    out_specs = (
        P(("shard", "replica"), None, None),
        P(("shard", "replica"), None, None),
        P(None, "shard", None),
        P(None, "shard", None),
        P(None, "shard", None),
        P(None, "shard", None),
        P(None, None, "shard"),
        P(None, None, "shard"),
        P(None, "shard"),
    )
    return jax.shard_map(
        functools.partial(on_device, mesh.shape["shard"], mesh.shape["replica"]), mesh=mesh, in_specs=in_specs, out_specs=out_specs, check_vma=False
    )
```

```python
import functools

import jax
import jax.numpy as jnp
from jax import lax
from jax.experimental import pallas as pl
from jax.experimental.pallas import tpu as pltpu
from jax.sharding import PartitionSpec as P

HD = 64
EPS = 1e-06
INV_ROOT_TWO = 0.7071067811865476
INV_ROOT_TWO_PI = 0.3989422804014327
LOW = jnp.bfloat16
FULL = jnp.float32
MESH = pl.DeviceIdType.MESH
VMEM_LIMIT = 60 * 1024 * 1024

QKV, OUT, UP, DOWN = range(4)
GAIN_ROWS, BIAS_ROWS = 2, 6


def product(left, right):
    return jnp.dot(left, right, preferred_element_type=FULL)


def product_left(left, right):
    return lax.dot_general(
        left, right, (((0,), (0,)), ((), ())), preferred_element_type=FULL
    )


def product_right(left, right):
    return lax.dot_general(
        left, right, (((1,), (1,)), ((), ())), preferred_element_type=FULL
    )


def wide(value):
    return value.astype(FULL)


def column_sum(value):
    return jnp.sum(value, 0, keepdims=True)


def standardize(values):
    center = jnp.mean(values, -1, keepdims=True)
    centered = values - center
    spread = jnp.mean(centered * centered, -1, keepdims=True)
    inverse = lax.rsqrt(spread + EPS)
    return centered * inverse, inverse


def norm_back(upstream, unit, inverse, gain):
    scaled = upstream * gain
    inner = (
        scaled
        - jnp.mean(scaled, -1, keepdims=True)
        - unit * jnp.mean(scaled * unit, -1, keepdims=True)
    )
    return inverse * inner, column_sum(upstream * unit), column_sum(upstream)


SUBS = 7


def sub_items(layers, weights, shards):
    width, ff, qkv = (weights[kind].shape[2] for kind in (OUT, UP, QKV))
    half_d = weights[QKV].shape[1] // 2
    rows = weights[DOWN].shape[1] // 4
    cut = (qkv + width) // 2
    subs = []
    for layer in reversed(range(layers)):
        subs += [
            (DOWN, layer, 0, rows, 0, width, 0),
            (DOWN, layer, rows, rows, 0, width, 1),
            (UP, layer, 0, half_d, 0, ff // 2, 0),
            (UP, layer, 0, half_d, ff // 2, ff // 2, 1),
            (OUT, layer, 0, half_d, 0, width, 1),
            (QKV, layer, 0, half_d, 0, cut, 0),
            (QKV, layer, 0, half_d, cut, qkv - cut, 1),
        ]
    return subs


def fused_kernel(shards, deep, *refs):
    (images, cotangent, counts, *own_w), refs = refs[:7], refs[7:]
    (gains, biases, up_bias), refs = refs[:3], refs[3:]
    (act_out, grad_out), refs = refs[:2], refs[2:]
    totals, refs = refs[:4], refs[4:]
    small_out, refs = refs[:3], refs[3:]
    (x_in, cot, stream, grad, w_qkv, w_out, w_up, w_down, par, par_up, small, small_all, wide_small,
     wide_all), refs = refs[:14], refs[14:]
    (unit_one, inv_one, normed_one, queries, key_rows, values, probs, mixed, unit_two, inv_two,
     normed_two, activated, slope, hid_low, mix_grad, pgrad), refs = refs[:16], refs[16:]
    own_g, refs = refs[:4], refs[4:]
    n_sub = SUBS * own_w[0].shape[0]
    buf_a, refs = refs[:n_sub], refs[n_sub:]
    buf_s, refs = refs[:n_sub], refs[n_sub:]
    buf_b, refs = refs[:n_sub], refs[n_sub:]
    z_own, refs = refs[: n_sub + 1], refs[n_sub + 1 :]
    z_in, refs = refs[: n_sub + 1], refs[n_sub + 1 :]
    z_cross, refs = refs[: n_sub + 1], refs[n_sub + 1 :]
    z_fin, refs = refs[: n_sub + 1], refs[n_sub + 1 :]
    (tiny, tiny_in), refs = refs[:2], refs[2:]
    (f_send, f_recv, r_send, r_recv, m_send, m_recv, x_send, x_recv, q_send, q_recv, p_send, p_recv,
     own_sem, io_sem, a_send, a_recv, b_send, b_recv, c_send, c_recv, z_send, z_recv, e_send, e_recv,
     fin_sem, t_send, t_recv) = refs

    layers, rows_d, _ = own_w[QKV].shape
    width = x_in.shape[1]
    tokens = x_in.shape[0]
    padded = stream.shape[0]
    heads = width // HD
    ff = w_up.shape[2]
    factor = HD ** (-0.5)
    weights = (w_qkv, w_out, w_up, w_down)

    me = lax.axis_index("shard")
    rep = lax.axis_index("replica")
    core = lax.rem(rep, 2)
    depth = lax.div(rep, 2)
    parity = lax.rem(depth, 2)
    mid = deep // 2
    left = depth < mid
    place = jnp.where(left, depth, deep - 1 - depth)
    inner_depth = jnp.where(left, depth + 1, depth - 1)
    outer_depth = jnp.where(left, depth - 1, depth + 1)
    mate = (me, rep + 1 - 2 * core)
    across = (me, (depth + 1 - 2 * parity) * 2 + core)
    inner = (me, inner_depth * 2 + core)
    outer = (me, outer_depth * 2 + core)
    side_me = (me + 1 - 2 * lax.rem(me, 2), lax.rem(me + 2, shards))
    side = [(s, rep) for s in side_me]
    far_me = shards - 1 - me
    inside = place > 0
    center = place == mid - 1

    def local(src, dst, sem):
        copy = pltpu.make_async_copy(src, dst, sem)
        copy.start()
        return copy

    load_x = local(images.at[:, 0], x_in, io_sem.at[0])
    load_cot = local(cotangent.at[:, 0], cot, io_sem.at[1])

    barrier = pltpu.get_barrier_semaphore()
    for device in (mate, across, side[0], side[1], (far_me, rep), inner):
        pl.semaphore_signal(barrier, inc=1, device_id=device, device_id_type=MESH)

    @pl.when(inside)
    def _():
        pl.semaphore_signal(barrier, inc=1, device_id=outer, device_id_type=MESH)

    sent = []

    def remote(src, dst, send_sem, recv_sem, device, keep=True):
        copy = pltpu.make_async_remote_copy(
            src_ref=src, dst_ref=dst, send_sem=send_sem, recv_sem=recv_sem, device_id=device,
            device_id_type=MESH)
        copy.start()
        if keep:
            sent.append(copy)
        return copy

    items = [
        (UP, 0), (DOWN, 0), (QKV, 0), (OUT, 1),
        (DOWN, 1), (OUT, 0), (UP, 1), (QKV, 1),
    ]
    via_of, loads = [], [0, 0]
    for kind, _ in items:
        via_of.append(0 if loads[1] <= loads[0] else 1)
        loads[1 - via_of[-1]] += own_w[kind].shape[1] * own_w[kind].shape[2] // (
            2 if kind in (UP, DOWN) else 1)

    def part(ref, kind, layer, first_row, rows, which):
        half = rows // 2
        start = first_row + core * half
        if kind == UP:
            cut = ff // 2
            return ref.at[layer, pl.ds(pl.multiple_of(start, 16), half),
                          pl.ds(pl.multiple_of(which * cut, 128), cut)]
        if kind == DOWN:
            return ref.at[layer, pl.ds(pl.multiple_of(start + which * (half // 2), 16), half // 2)]
        return ref.at[layer, pl.ds(pl.multiple_of(start, 16), half)]

    def held(item, shard, which):
        kind, layer = items[item]
        rows = own_w[kind].shape[1]
        return part(weights[kind], kind, layer, shard * rows, rows, which)

    firsts, relays, passed, crossed, again, owned = {}, {}, {}, {}, {}, {}

    def first(item):
        kind, layer = items[item]
        rows = own_w[kind].shape[1]
        src = part(own_w[kind], kind, layer, 0, rows, parity)
        firsts[item] = [
            remote(src, held(item, me, parity), f_send.at[item, k], f_recv.at[item, k], side[k])
            for k in range(2)
        ]
        owned[item] = local(
            own_w[kind].at[layer],
            weights[kind].at[layer, pl.ds(pl.multiple_of(me * rows, 16), rows)], own_sem.at[item])
        passed[item] = []
        crossed[item] = []

    def hand_on(item, slot, shard):
        piece = held(item, shard, parity)
        if items[item][0] in (UP, DOWN):
            crossed[item].append((slot, shard, remote(
                piece, piece, x_send.at[item, slot], x_recv.at[item, slot], across)))
        passed[item].append(
            remote(piece, piece, m_send.at[item, slot], m_recv.at[item, slot], mate))

    def relay(item):
        via = via_of[item]
        for k in (via, 1 - via):
            firsts[item][k].wait_recv()
            if k == via:
                piece = held(item, side_me[k], parity)
                relays[item] = remote(
                    piece, piece, r_send.at[item], r_recv.at[item], side[1 - k])
            hand_on(item, k, side_me[k])

    def reach(item):
        relays[item].wait_recv()
        hand_on(item, 2, far_me)

    def cross(item):
        for slot, shard, copy in crossed[item]:
            copy.wait_recv()
            piece = held(item, shard, 1 - parity)
            passed[item].append(
                remote(piece, piece, q_send.at[item, slot], q_recv.at[item, slot], mate))

    def settle(item):
        for copy in passed[item]:
            copy.wait_recv()
        owned[item].wait()

    small[...] = jnp.zeros_like(small)
    wide_small[...] = jnp.zeros_like(wide_small)
    for layer in range(layers):
        small[pl.ds(layer * GAIN_ROWS, GAIN_ROWS), pl.ds(0, rows_d)] = wide(gains[layer])
    for which in range(BIAS_ROWS):
        small[pl.ds((GAIN_ROWS + which) * layers, layers), pl.ds(0, rows_d)] = wide(biases[which])
    wide_small[pl.ds(0, layers), :] = wide(up_bias[...])

    pl.semaphore_wait(barrier, 6 + jnp.where(inside, 1, 0))

    tinies = []
    for k, shard in enumerate(side_me + (far_me,)):
        tinies.append(remote(
            small, small_all.at[me], p_send.at[0, k], p_recv.at[0, k], (shard, rep)))
        tinies.append(remote(
            wide_small, wide_all.at[me], p_send.at[1, k], p_recv.at[1, k], (shard, rep)))
    tinies_own = [
        local(small, small_all.at[me], io_sem.at[2]),
        local(wide_small, wide_all.at[me], io_sem.at[3]),
    ]

    for item in range(len(items)):
        first(item)
    load_x.wait()
    stream[...] = jnp.zeros_like(stream)
    stream[pl.ds(0, tokens), :] = x_in[...]
    unit, inverse = standardize(stream[...])
    unit_one[0] = unit
    inv_one[0] = inverse
    live = jnp.where(counts[0] > 0, 1.0, 0.0).astype(FULL)
    load_cot.wait()
    grad[...] = jnp.zeros_like(grad)
    grad[pl.ds(0, tokens), :] = cot[...] * live

    for copy in tinies:
        copy.wait_recv()
    for copy in tinies_own:
        copy.wait()
    for s in range(shards):
        par[:, pl.ds(s * rows_d, rows_d)] = small_all[s][:, :rows_d]
        per = wide_small.shape[1]
        par_up[:, pl.ds(s * per, per)] = wide_all[s]

    def gain_of(layer, which):
        return par[pl.ds(layer * GAIN_ROWS + which, 1), :]

    def bias_row(layer, which):
        return (GAIN_ROWS + which) * layers + layer

    def bias_of(layer, which):
        return par[pl.ds(bias_row(layer, which), 1), :]

    key_mask = jnp.where(
        lax.broadcasted_iota(jnp.int32, (1, padded), 1) < tokens, 0.0, -1e30).astype(FULL)
    lane_half = lax.broadcasted_iota(jnp.int32, (padded, 2 * HD), 1) < HD

    def one_head(value, which):
        keep = lane_half if which == 0 else jnp.logical_not(lane_half)
        return jnp.where(keep, value, jnp.zeros_like(value))

    def pair(p):
        return pl.ds(p * 2 * HD, 2 * HD)

    def project(layer):
        normed = (unit_one[layer] * gain_of(layer, 0) + bias_of(layer, 0)).astype(LOW)
        normed_one[layer] = normed
        queries[layer] = (
            (product(normed, w_qkv[layer, :, pl.ds(0, width)]) + bias_of(layer, 1)) * factor
        ).astype(LOW)
        key_rows[layer] = product(normed, w_qkv[layer, :, pl.ds(width, width)]).astype(LOW)
        values[layer] = (
            product(normed, w_qkv[layer, :, pl.ds(2 * width, width)]) + bias_of(layer, 2)
        ).astype(LOW)

    def attend(layer, p):
        q, k, v = (ref[layer, :, pair(p)] for ref in (queries, key_rows, values))
        total = None
        for h in range(2):
            scores = product_right(one_head(q, h), k) + key_mask
            log_total = jnp.log(jnp.sum(jnp.exp(scores), -1, keepdims=True))
            prob = jnp.exp(scores - log_total)
            probs[layer, 2 * p + h] = prob
            term = product(prob.astype(LOW), one_head(v, h))
            total = term if total is None else total + term
        mixed[layer, :, pair(p)] = total.astype(LOW)

    def join(layer):
        middle = stream[...] + product(mixed[layer], w_out[layer]) + bias_of(layer, 3)
        stream[...] = middle
        unit, inverse = standardize(middle)
        unit_two[layer] = unit
        inv_two[layer] = inverse
        normed_two[layer] = (unit * gain_of(layer, 1) + bias_of(layer, 4)).astype(LOW)

    chunk = 256

    def expand(layer, j):
        cols = pl.ds(j * chunk, chunk)
        hidden = product(normed_two[layer], w_up[layer, :, cols]) + par_up[pl.ds(layer, 1), cols]
        below = 0.5 * (1.0 + lax.erf(hidden * INV_ROOT_TWO))
        activated[layer, :, cols] = (hidden * below).astype(LOW)
        dens = jnp.exp(-0.5 * hidden * hidden) * INV_ROOT_TWO_PI
        slope[layer, :, cols] = below + hidden * dens

    def contract(layer):
        result = stream[...] + product(activated[layer], w_down[layer]) + bias_of(layer, 5)
        stream[...] = result
        if layer + 1 < layers:
            unit, inverse = standardize(result)
            unit_one[layer + 1] = unit
            inv_one[layer + 1] = inverse

    subs = sub_items(layers, own_w, shards)
    stage_a, one, two = {}, {}, {}

    def mine(a, dest, half):
        kind, layer, row, rows, start, cols, _ = subs[a]
        return own_g[kind].at[layer, dest, half, pl.ds(row, rows), pl.ds(start, cols)]

    def swap(a):
        kind, layer, row, rows, start, cols, _ = subs[a]
        stage_a[a] = remote(
            own_g[kind].at[layer, :, 1 - core, pl.ds(row, rows), pl.ds(start, cols)], buf_a[a],
            a_send.at[a], a_recv.at[a], mate)

    def both(a, dest):
        return wide(mine(a, dest, core)[...]) + wide(buf_a[a][dest])

    def scatter_one(a):
        turn = subs[a][-1]
        stage_a[a].wait_recv()
        near = side_me[turn]
        buf_s[a][0] = both(a, near).astype(LOW)
        buf_s[a][1] = both(a, far_me).astype(LOW)
        one[a] = remote(
            buf_s[a].at[pl.ds(0, 2)], buf_b[a].at[pl.ds(0, 2)], b_send.at[a], b_recv.at[a],
            side[turn])

    def scatter_two(a):
        turn = 1 - subs[a][-1]
        one[a].wait_recv()
        buf_s[a][2] = (both(a, side_me[turn]) + wide(buf_b[a][1])).astype(LOW)
        two[a] = remote(buf_s[a].at[2], buf_b[a].at[2], c_send.at[a], c_recv.at[a], side[turn])

    def summed(a):
        if a == n_sub:
            return tiny[3]
        return both(a, me) + wide(buf_b[a][0]) + wide(buf_b[a][2])

    def z_first(a):
        if a < n_sub:
            two[a].wait_recv()
        z_own[a][...] = summed(a).astype(z_own[a].dtype)

        @pl.when(jnp.logical_and(jnp.logical_not(inside), jnp.logical_not(center)))
        def _():
            remote(z_own[a], z_in[a], z_send.at[a, 0], z_recv.at[a, 0], inner, keep=False)

    def described(src, dst, send_sem, recv_sem, device):
        return pltpu.make_async_remote_copy(
            src_ref=src, dst_ref=dst, send_sem=send_sem, recv_sem=recv_sem, device_id=device,
            device_id_type=MESH)

    def z_copy(a):
        return described(z_own[a], z_in[a], z_send.at[a, 0], z_recv.at[a, 0], inner)

    def x_copy(a):
        return described(z_own[a], z_cross[a], z_send.at[a, 1], z_recv.at[a, 1], inner)

    def o_copy(a):
        return described(z_fin[a], z_fin[a], z_send.at[a, 2], z_recv.at[a, 2], outer)

    def z_second(a):
        @pl.when(inside)
        def _():
            z_copy(a).wait_recv()
            z_own[a][...] = (summed(a) + wide(z_in[a][...])).astype(z_own[a].dtype)

            @pl.when(jnp.logical_not(center))
            def _():
                z_copy(a).start()

        @pl.when(center)
        def _():
            x_copy(a).start()

    def goal(a):
        kind, layer, row, rows, start, cols, _ = subs[a]
        return totals[kind].at[layer, core, pl.ds(row, rows), pl.ds(start, cols)]

    def e_copy(a):
        return described(z_fin[a], goal(a), e_send.at[a], e_recv.at[a], mate)

    def fin_copy(a):
        return pltpu.make_async_copy(z_fin[a], goal(a), fin_sem.at[a])

    def spread(a):
        @pl.when(inside)
        def _():
            o_copy(a).start()

        if a < n_sub:
            e_copy(a).start()
            fin_copy(a).start()

    def z_third(a):
        @pl.when(center)
        def _():
            x_copy(a).wait_recv()
            z_fin[a][...] = (wide(z_own[a][...]) + wide(z_cross[a][...])).astype(z_fin[a].dtype)
            spread(a)

    def z_fourth(a):
        @pl.when(jnp.logical_not(center))
        def _():
            o_copy(a).wait_recv()
            spread(a)

    def z_done(a):
        if a < n_sub:
            e_copy(a).wait()
            fin_copy(a).wait()

        @pl.when(jnp.logical_not(center))
        def _():
            z_copy(a).wait_send()

        @pl.when(center)
        def _():
            x_copy(a).wait_send()

        @pl.when(inside)
        def _():
            o_copy(a).wait_send()

    def shared(value):
        return value.reshape(shards, 2, value.shape[0] // shards // 2, value.shape[1]).astype(LOW)

    up_row = layers * (GAIN_ROWS + BIAS_ROWS)

    def put_up_bias(layer, start, value):
        for at in range(0, value.shape[1], 128):
            row, lane = divmod(start + at, width)
            tiny[0, pl.ds(up_row + layer * (ff // width) + row, 1), pl.ds(lane, 128)] = (
                value[:, at : at + 128])

    def put_gain(layer, which, value):
        tiny[0, pl.ds(layer * GAIN_ROWS + which, 1), :] = value

    def put_bias(layer, which, value):
        tiny[0, pl.ds(bias_row(layer, which), 1), :] = value

    def back_down(layer):
        low = grad[...].astype(LOW)
        per = ff // shards
        for s in range(shards):
            piece = product_left(activated[layer, :, pl.ds(s * per, per)], low)
            own_g[DOWN][layer, s] = piece.reshape(2, per // 2, width).astype(LOW)
        put_bias(layer, 5, column_sum(grad[...]))

    def back_expand(layer, j):
        low = grad[...].astype(LOW)
        cols = pl.ds(j * chunk, chunk)
        act_grad = product_right(low, w_down[layer, cols, :])
        hid_grad = act_grad * slope[layer, :, cols]
        put_up_bias(layer, j * chunk, column_sum(hid_grad))
        hid_low[:, cols] = hid_grad.astype(LOW)

    def back_up(layer, j):
        cols = pl.ds(j * ff // 2, ff // 2)
        own_g[UP][layer, :, :, :, cols] = shared(product_left(normed_two[layer], hid_low[:, cols]))

    def back_middle(layer):
        norm_grad = product_right(hid_low[...], w_up[layer])
        back, gain, shift = norm_back(
            norm_grad, unit_two[layer], inv_two[layer], gain_of(layer, 1))
        put_gain(layer, 1, gain)
        put_bias(layer, 4, shift)
        mid_grad = grad[...] + back
        grad[...] = mid_grad
        put_bias(layer, 3, column_sum(mid_grad))
        mid_low = mid_grad.astype(LOW)
        own_g[OUT][layer] = shared(product_left(mixed[layer], mid_low))
        mix_grad[...] = product_right(mid_low, w_out[layer]).astype(LOW)

    def back_attend(layer, p):
        q, k, v = (ref[layer, :, pair(p)] for ref in (queries, key_rows, values))
        up = mix_grad[:, pair(p)]
        sums = [None] * 3
        for h in range(2):
            up_h = one_head(up, h)
            prob = probs[layer, 2 * p + h]
            prob_grad = product_right(up_h, v)
            row_dot = jnp.sum(prob * prob_grad, -1, keepdims=True)
            score_grad = (prob * (prob_grad - row_dot)).astype(LOW)
            terms = (
                product(score_grad, one_head(k, h)),
                product_left(score_grad, one_head(q, h)),
                product_left(prob.astype(LOW), up_h),
            )
            sums = [t if s is None else s + t for s, t in zip(sums, terms)]
        query_grad = sums[0] * factor
        start = p * 2 * HD
        tiny[0, pl.ds(bias_row(layer, 1), 1), pair(p)] = column_sum(query_grad)
        tiny[0, pl.ds(bias_row(layer, 2), 1), pair(p)] = column_sum(sums[2])
        for n, value in enumerate((query_grad, sums[1], sums[2])):
            pgrad[:, pl.ds(n * width + start, 2 * HD)] = value.astype(LOW)

    def back_qkv(layer, n):
        cols = pl.ds(n * width, width)
        own_g[QKV][layer, :, :, :, cols] = shared(product_left(normed_one[layer], pgrad[:, cols]))

    def back_first(layer):
        first_grad = product_right(pgrad[...], w_qkv[layer])
        back, gain, shift = norm_back(
            first_grad, unit_one[layer], inv_one[layer], gain_of(layer, 0))
        put_gain(layer, 0, gain)
        put_bias(layer, 0, shift)
        grad[...] = grad[...] + back


    def finish_forward():
        x_in[...] = stream[pl.ds(0, tokens), :] * live
        return local(x_in, act_out.at[:, 0], io_sem.at[0])

    swaps = []

    def tiny_send(n):
        device = (mate, side[0], side[1])[n]
        swaps.append(remote(tiny.at[n], tiny_in.at[n], t_send.at[n], t_recv.at[n], device))

    def tiny_add(n):
        swaps[n].wait_recv()
        tiny[n + 1] = tiny[n] + tiny_in[n]

    def finish_backward():
        cot[...] = grad[pl.ds(0, tokens), :]
        return local(cot, grad_out.at[:, 0], io_sem.at[1])

    relay(0)
    relay(1)
    relay(2)
    relay(3)
    relay(4)
    relay(5)
    relay(6)
    relay(7)
    reach(0)
    reach(1)
    reach(2)
    reach(3)
    reach(4)
    reach(5)
    cross(0)
    settle(2)
    project(0)
    reach(6)
    attend(0, 0)
    attend(0, 1)
    reach(7)
    cross(1)
    attend(0, 2)
    settle(5)
    join(0)
    settle(0)
    expand(0, 0)
    expand(0, 1)
    cross(4)
    for j in range(2, 6):
        expand(0, j)
    settle(1)
    contract(0)
    settle(7)
    project(1)
    cross(6)
    for j in range(0, 3):
        attend(1, j)
    settle(3)
    join(1)
    settle(6)
    for j in range(0, 6):
        expand(1, j)
    back_down(1)
    swap(0)
    swap(1)
    settle(4)
    for j in range(0, 6):
        back_expand(1, j)
    back_up(1, 0)
    swap(2)
    back_up(1, 1)
    swap(3)
    scatter_one(0)
    back_middle(1)
    swap(4)
    scatter_one(1)
    back_attend(1, 0)
    back_attend(1, 1)
    scatter_one(2)
    back_attend(1, 2)
    back_qkv(1, 0)
    back_qkv(1, 1)
    swap(5)
    scatter_one(3)
    back_qkv(1, 2)
    swap(6)
    back_first(1)
    scatter_two(0)
    back_down(0)
    swap(7)
    swap(8)
    scatter_one(5)
    back_expand(0, 0)
    scatter_two(1)
    for j in range(1, 6):
        back_expand(0, j)
    back_up(0, 0)
    swap(9)
    back_up(0, 1)
    swap(10)
    back_middle(0)
    swap(11)
    scatter_two(2)
    back_attend(0, 0)
    scatter_two(3)
    scatter_one(8)
    back_attend(0, 1)
    back_attend(0, 2)
    z_first(0)
    scatter_two(5)
    back_qkv(0, 0)
    scatter_one(9)
    back_qkv(0, 1)
    swap(12)
    back_qkv(0, 2)
    swap(13)
    z_first(2)
    back_first(0)
    store_grad = finish_backward()
    tiny_send(0)
    z_first(1)
    contract(1)
    store_act = finish_forward()
    z_first(3)
    scatter_one(10)
    scatter_one(12)
    tiny_add(0)
    tiny_send(1)
    z_second(0)
    scatter_two(8)
    z_second(2)
    z_first(5)
    scatter_two(9)
    z_second(1)
    z_third(0)
    scatter_one(13)
    z_second(3)
    scatter_one(7)
    z_third(2)
    scatter_two(10)
    scatter_two(12)
    z_second(5)
    tiny_add(1)
    tiny_send(2)
    z_third(1)
    z_first(9)
    z_fourth(0)
    z_first(8)
    scatter_one(6)
    z_third(3)
    scatter_two(13)
    z_fourth(2)
    scatter_one(11)
    z_third(5)
    z_first(12)
    z_second(9)
    z_fourth(1)
    tiny_add(2)
    z_first(n_sub)
    scatter_two(7)
    z_second(8)
    z_fourth(3)
    scatter_two(6)
    z_first(10)
    scatter_one(4)
    z_first(13)
    z_second(12)
    z_fourth(5)
    scatter_two(11)
    z_third(9)
    z_second(n_sub)
    z_first(6)
    z_first(7)
    z_third(8)
    z_second(10)
    z_first(11)
    scatter_two(4)
    z_second(13)
    z_third(12)
    z_fourth(9)
    z_second(6)
    z_third(n_sub)
    z_fourth(8)
    z_second(7)
    z_first(4)
    z_third(10)
    z_second(11)
    z_third(13)
    z_fourth(12)
    z_third(6)
    z_fourth(n_sub)
    z_second(4)
    z_third(7)
    z_fourth(10)
    z_third(11)
    z_fourth(13)
    z_fourth(6)
    z_third(4)
    z_fourth(7)
    z_fourth(11)
    z_fourth(4)
    done = z_fin[n_sub][...]
    picked = None
    for s in range(shards):
        hit = jnp.where(me == s, 1.0, 0.0).astype(FULL)
        term = done[:up_row, s * rows_d : (s + 1) * rows_d] * hit
        picked = term if picked is None else picked + term
    for layer in range(layers):
        small_out[0][layer] = picked[layer * GAIN_ROWS : (layer + 1) * GAIN_ROWS]
        row = None
        for s in range(shards):
            at = up_row + layer * (ff // width) + s
            hit = jnp.where(me == s, 1.0, 0.0).astype(FULL)
            term = done[at : at + 1] * hit
            row = term if row is None else row + term
        small_out[2][pl.ds(layer, 1), :] = row
    for which in range(BIAS_ROWS):
        small_out[1][which] = picked[bias_row(0, which) : bias_row(0, which) + layers]
    for a in range(n_sub + 1):
        z_done(a)
    for copy in sent:
        copy.wait_send()
    store_act.wait()
    store_grad.wait()


def finish_kernel(count, *refs):
    ins, outs, refs = refs[:count], refs[count : 2 * count], refs[2 * count :]
    held, refs = refs[:count], refs[count:]
    wides, (load_sem, store_sem) = refs[:-2], refs[-2:]
    parts = []
    for n in range(2, 6):
        parts += [(n, layer) for layer in range(ins[n].shape[0])]
    parts += [(n, None) for n in range(count) if not 2 <= n < 6]

    def view(ref, layer):
        return ref if layer is None else ref.at[layer]

    loads, stores = [], []
    for at, (n, layer) in enumerate(parts):
        copy = pltpu.make_async_copy(view(ins[n], layer), view(held[n], layer), load_sem.at[at])
        copy.start()
        loads.append(copy)
    for at, (n, layer) in enumerate(parts):
        loads[at].wait()
        src = held[n]
        if layer is not None:
            src = wides[n - 2]
            src[layer] = held[n][layer].astype(FULL)
        copy = pltpu.make_async_copy(view(src, layer), view(outs[n], layer), store_sem.at[at])
        copy.start()
        stores.append(copy)
    for copy in stores:
        copy.wait()


def finish(arrays):
    count = len(arrays)
    parts = count - 4 + 4 * arrays[2].shape[0]
    specs = [pl.BlockSpec(memory_space=pl.ANY)] * count
    return pl.pallas_call(
        functools.partial(finish_kernel, count),
        out_shape=[jax.ShapeDtypeStruct(x.shape, FULL) for x in arrays],
        in_specs=specs,
        out_specs=specs,
        scratch_shapes=[pltpu.VMEM(x.shape, x.dtype) for x in arrays]
        + [pltpu.VMEM(x.shape, FULL) for x in arrays[2:6]]
        + [pltpu.SemaphoreType.DMA((parts,))] * 2,
        compiler_params=pltpu.CompilerParams(vmem_limit_bytes=VMEM_LIMIT),
        name="widen",
    )(*arrays)


def on_device(shards, replicas, images, cotangent, counts, *stacks):
    weights, (gains, biases, up_bias) = stacks[:4], stacks[4:]
    layers, rows_d, _ = weights[QKV].shape
    deep = replicas // 2
    tokens, width = images.shape[1:]
    padded = -(-tokens // 16) * 16
    ff = weights[UP].shape[2]
    heads = width // HD
    qkv = weights[QKV].shape[2]
    sems = pltpu.SemaphoreType.DMA
    low = lambda *s: pltpu.VMEM(s, LOW)
    full = lambda *s: pltpu.VMEM(s, FULL)
    small_rows = layers * (GAIN_ROWS + BIAS_ROWS)
    small_rows_pad = -(-small_rows // 8) * 8
    per_up = up_bias.shape[1]
    scratch = [
        full(tokens, width), full(tokens, width), full(padded, width), full(padded, width),
        low(layers, shards * rows_d, qkv), low(layers, shards * rows_d, width),
        low(layers, shards * rows_d, ff), low(layers, ff, width),
        full(small_rows_pad, width), full(8, ff),
        full(small_rows_pad, 128), full(shards, small_rows_pad, 128),
        full(8, per_up), full(shards, 8, per_up),
        full(layers, padded, width), full(layers, padded, 1), low(layers, padded, width),
        low(layers, padded, width), low(layers, padded, width), low(layers, padded, width),
        full(layers, heads, padded, padded), low(layers, padded, width),
        full(layers, padded, width), full(layers, padded, 1), low(layers, padded, width),
        low(layers, padded, ff), full(layers, padded, ff), low(padded, ff), low(padded, width),
        low(padded, qkv),
    ]
    halves = [w.shape[1] // 2 for w in weights]
    columns = [w.shape[2] for w in weights]
    scratch += [low(layers, shards, 2, h, c) for h, c in zip(halves, columns)]
    shapes = [(sub[3], sub[5]) for sub in sub_items(layers, weights, shards)]
    n_sub = len(shapes)
    scratch += [low(shards, *s) for s in shapes] + [low(3, *s) for s in shapes] * 2
    tiny_rows = small_rows + layers * (ff // width)
    scratch += ([low(*s) for s in shapes] + [full(tiny_rows, width)]) * 4
    scratch += [full(4, tiny_rows, width), full(3, tiny_rows, width)]
    n_items = 4 * layers
    scratch += [
        sems((n_items, 2)), sems((n_items, 2)), sems((n_items,)), sems((n_items,)),
        sems((n_items, 3)), sems((n_items, 3)), sems((n_items, 3)), sems((n_items, 3)),
        sems((n_items, 3)), sems((n_items, 3)), sems((2, 3)), sems((2, 3)),
        sems((n_items,)), sems((4,)), sems((n_sub,)), sems((n_sub,)), sems((n_sub,)),
        sems((n_sub,)), sems((n_sub,)), sems((n_sub,)), sems((n_sub + 1, 3)), sems((n_sub + 1, 3)),
        sems((n_sub,)), sems((n_sub,)), sems((n_sub,)), sems((3,)), sems((3,)),
    ]
    shape = jax.ShapeDtypeStruct
    images, cotangent, biases = (x.transpose(1, 0, 2) for x in (images, cotangent, biases))
    outs = [shape(images.shape, FULL), shape(images.shape, FULL)]
    outs += [shape((layers, 2, h, c), LOW) for h, c in zip(halves, columns)]
    outs += [shape(x.shape, FULL) for x in (gains, biases, up_bias)]
    hbm, vmem = pl.BlockSpec(memory_space=pl.ANY), pl.BlockSpec(memory_space=pltpu.VMEM)
    done = pl.pallas_call(
        functools.partial(fused_kernel, shards, deep),
        out_shape=outs,
        in_specs=[hbm, hbm, pl.BlockSpec(memory_space=pltpu.SMEM)] + [hbm] * 4 + [vmem] * 3,
        out_specs=[hbm] * 6 + [vmem] * 3,
        scratch_shapes=scratch,
        compiler_params=pltpu.CompilerParams(
            collective_id=0, has_side_effects=True, vmem_limit_bytes=VMEM_LIMIT
        ),
        name="encoder_step",
    )(images, cotangent, counts, *weights, gains, biases, up_bias)
    done = list(done)
    for kind in range(4):
        done[2 + kind] = done[2 + kind].reshape(weights[kind].shape)
    done = list(finish(done))
    for n in (0, 1, 7):
        done[n] = done[n].transpose(1, 0, 2)
    return tuple(done)


def solution(mesh):
    in_specs = (
        P(("shard", "replica"), None, None),
        P(("shard", "replica"), None, None),
        P(("shard", "replica")),
        P(None, "shard", None),
        P(None, "shard", None),
        P(None, "shard", None),
        P(None, "shard", None),
        P(None, None, "shard"),
        P(None, None, "shard"),
        P(None, "shard"),
    )
    out_specs = (
        P(("shard", "replica"), None, None),
        P(("shard", "replica"), None, None),
        P(None, "shard", None),
        P(None, "shard", None),
        P(None, "shard", None),
        P(None, "shard", None),
        P(None, None, "shard"),
        P(None, None, "shard"),
        P(None, "shard"),
    )
    return jax.shard_map(
        functools.partial(on_device, mesh.shape["shard"], mesh.shape["replica"]), mesh=mesh, in_specs=in_specs, out_specs=out_specs, check_vma=False
    )
```

```python
import functools

import jax
import jax.numpy as jnp
from jax import lax
from jax.experimental import pallas as pl
from jax.experimental.pallas import tpu as pltpu
from jax.sharding import PartitionSpec as P

HD = 64
EPS = 1e-06
INV_ROOT_TWO = 0.7071067811865476
INV_ROOT_TWO_PI = 0.3989422804014327
LOW = jnp.bfloat16
FULL = jnp.float32
MESH = pl.DeviceIdType.MESH
VMEM_LIMIT = 60 * 1024 * 1024

QKV, OUT, UP, DOWN = range(4)
GAIN_ROWS, BIAS_ROWS = 2, 6


def product(left, right):
    return jnp.dot(left, right, preferred_element_type=FULL)


def product_left(left, right):
    return lax.dot_general(
        left, right, (((0,), (0,)), ((), ())), preferred_element_type=FULL
    )


def product_right(left, right):
    return lax.dot_general(
        left, right, (((1,), (1,)), ((), ())), preferred_element_type=FULL
    )


def wide(value):
    return value.astype(FULL)


def column_sum(value):
    return jnp.sum(value, 0, keepdims=True)


def standardize(values):
    center = jnp.mean(values, -1, keepdims=True)
    centered = values - center
    spread = jnp.mean(centered * centered, -1, keepdims=True)
    inverse = lax.rsqrt(spread + EPS)
    return centered * inverse, inverse


def norm_back(upstream, unit, inverse, gain):
    scaled = upstream * gain
    inner = (
        scaled
        - jnp.mean(scaled, -1, keepdims=True)
        - unit * jnp.mean(scaled * unit, -1, keepdims=True)
    )
    return inverse * inner, column_sum(upstream * unit), column_sum(upstream)


SUBS = 7


def sub_items(layers, weights, shards):
    width, ff, qkv = (weights[kind].shape[2] for kind in (OUT, UP, QKV))
    half_d = weights[QKV].shape[1] // 2
    rows = weights[DOWN].shape[1] // 4
    cut = (qkv + width) // 2
    subs = []
    for layer in reversed(range(layers)):
        subs += [
            (DOWN, layer, 0, rows, 0, width, 0),
            (DOWN, layer, rows, rows, 0, width, 1),
            (UP, layer, 0, half_d, 0, ff // 2, 0),
            (UP, layer, 0, half_d, ff // 2, ff // 2, 1),
            (OUT, layer, 0, half_d, 0, width, 1),
            (QKV, layer, 0, half_d, 0, cut, 0),
            (QKV, layer, 0, half_d, cut, qkv - cut, 1),
        ]
    return subs


def fused_kernel(shards, deep, *refs):
    (images, cotangent, counts, *own_w), refs = refs[:7], refs[7:]
    (gains, biases, up_bias), refs = refs[:3], refs[3:]
    (act_out, grad_out), refs = refs[:2], refs[2:]
    totals, refs = refs[:4], refs[4:]
    small_out, refs = refs[:3], refs[3:]
    (x_in, cot, stream, grad, w_qkv, w_out, w_up, w_down, par, par_up, small, small_all, wide_small,
     wide_all), refs = refs[:14], refs[14:]
    (unit_one, inv_one, normed_one, queries, key_rows, values, probs, mixed, unit_two, inv_two,
     normed_two, activated, slope, hid_low, mix_grad, pgrad), refs = refs[:16], refs[16:]
    own_g, refs = refs[:4], refs[4:]
    n_sub = SUBS * own_w[0].shape[0]
    buf_a, refs = refs[:n_sub], refs[n_sub:]
    buf_s, refs = refs[:n_sub], refs[n_sub:]
    buf_b, refs = refs[:n_sub], refs[n_sub:]
    z_own, refs = refs[: n_sub + 1], refs[n_sub + 1 :]
    z_in, refs = refs[: n_sub + 1], refs[n_sub + 1 :]
    z_cross, refs = refs[: n_sub + 1], refs[n_sub + 1 :]
    z_fin, refs = refs[: n_sub + 1], refs[n_sub + 1 :]
    (tiny, tiny_in), refs = refs[:2], refs[2:]
    (f_send, f_recv, r_send, r_recv, m_send, m_recv, x_send, x_recv, q_send, q_recv, p_send, p_recv,
     own_sem, io_sem, a_send, a_recv, b_send, b_recv, c_send, c_recv, z_send, z_recv, e_send, e_recv,
     fin_sem, t_send, t_recv, s_sem, *small_held) = refs

    layers, rows_d, _ = own_w[QKV].shape
    width = x_in.shape[1]
    tokens = x_in.shape[0]
    padded = stream.shape[0]
    heads = width // HD
    ff = w_up.shape[2]
    factor = HD ** (-0.5)
    weights = (w_qkv, w_out, w_up, w_down)

    me = lax.axis_index("shard")
    rep = lax.axis_index("replica")
    core = lax.rem(rep, 2)
    depth = lax.div(rep, 2)
    parity = lax.rem(depth, 2)
    mid = deep // 2
    left = depth < mid
    place = jnp.where(left, depth, deep - 1 - depth)
    inner_depth = jnp.where(left, depth + 1, depth - 1)
    outer_depth = jnp.where(left, depth - 1, depth + 1)
    mate = (me, rep + 1 - 2 * core)
    across = (me, (depth + 1 - 2 * parity) * 2 + core)
    inner = (me, inner_depth * 2 + core)
    outer = (me, outer_depth * 2 + core)
    side_me = (me + 1 - 2 * lax.rem(me, 2), lax.rem(me + 2, shards))
    side = [(s, rep) for s in side_me]
    far_me = shards - 1 - me
    inside = place > 0
    center = place == mid - 1

    def local(src, dst, sem):
        copy = pltpu.make_async_copy(src, dst, sem)
        copy.start()
        return copy

    load_x = local(images.at[:, 0], x_in, io_sem.at[0])
    load_cot = local(cotangent.at[:, 0], cot, io_sem.at[1])

    barrier = pltpu.get_barrier_semaphore()
    for device in (mate, across, side[0], side[1], (far_me, rep), inner):
        pl.semaphore_signal(barrier, inc=1, device_id=device, device_id_type=MESH)

    @pl.when(inside)
    def _():
        pl.semaphore_signal(barrier, inc=1, device_id=outer, device_id_type=MESH)

    sent = []

    def remote(src, dst, send_sem, recv_sem, device, keep=True):
        copy = pltpu.make_async_remote_copy(
            src_ref=src, dst_ref=dst, send_sem=send_sem, recv_sem=recv_sem, device_id=device,
            device_id_type=MESH)
        copy.start()
        if keep:
            sent.append(copy)
        return copy

    items = [
        (UP, 0), (UP, 1), (QKV, 0), (DOWN, 0),
        (OUT, 0), (QKV, 1), (DOWN, 1), (OUT, 1),
    ]
    via_of, loads = [], [0, 0]
    for kind, _ in items:
        via_of.append(0 if loads[1] <= loads[0] else 1)
        loads[1 - via_of[-1]] += own_w[kind].shape[1] * own_w[kind].shape[2] // (
            2 if kind in (UP, DOWN) else 1)

    def part(ref, kind, layer, first_row, rows, which):
        half = rows // 2
        start = first_row + core * half
        if kind == UP:
            cut = ff // 2
            return ref.at[layer, pl.ds(pl.multiple_of(start, 16), half),
                          pl.ds(pl.multiple_of(which * cut, 128), cut)]
        if kind == DOWN:
            return ref.at[layer, pl.ds(pl.multiple_of(start + which * (half // 2), 16), half // 2)]
        return ref.at[layer, pl.ds(pl.multiple_of(start, 16), half)]

    def held(item, shard, which):
        kind, layer = items[item]
        rows = own_w[kind].shape[1]
        return part(weights[kind], kind, layer, shard * rows, rows, which)

    firsts, relays, passed, crossed, again, owned = {}, {}, {}, {}, {}, {}

    def first(item):
        kind, layer = items[item]
        rows = own_w[kind].shape[1]
        src = part(own_w[kind], kind, layer, 0, rows, parity)
        firsts[item] = [
            remote(src, held(item, me, parity), f_send.at[item, k], f_recv.at[item, k], side[k])
            for k in range(2)
        ]
        owned[item] = local(
            own_w[kind].at[layer],
            weights[kind].at[layer, pl.ds(pl.multiple_of(me * rows, 16), rows)], own_sem.at[item])
        passed[item] = []
        crossed[item] = []

    def hand_on(item, slot, shard):
        piece = held(item, shard, parity)
        if items[item][0] in (UP, DOWN):
            crossed[item].append((slot, shard, remote(
                piece, piece, x_send.at[item, slot], x_recv.at[item, slot], across)))
        passed[item].append(
            remote(piece, piece, m_send.at[item, slot], m_recv.at[item, slot], mate))

    def relay(item):
        via = via_of[item]
        for k in (via, 1 - via):
            firsts[item][k].wait_recv()
            if k == via:
                piece = held(item, side_me[k], parity)
                relays[item] = remote(
                    piece, piece, r_send.at[item], r_recv.at[item], side[1 - k])
            hand_on(item, k, side_me[k])

    def reach(item):
        relays[item].wait_recv()
        hand_on(item, 2, far_me)

    def cross(item):
        for slot, shard, copy in crossed[item]:
            copy.wait_recv()
            piece = held(item, shard, 1 - parity)
            passed[item].append(
                remote(piece, piece, q_send.at[item, slot], q_recv.at[item, slot], mate))

    def settle(item):
        for copy in passed[item]:
            copy.wait_recv()
        owned[item].wait()

    pl.semaphore_wait(barrier, 6 + jnp.where(inside, 1, 0))

    for item in range(3):
        first(item)

    small[...] = jnp.zeros_like(small)
    wide_small[...] = jnp.zeros_like(wide_small)
    for layer in range(layers):
        small[pl.ds(layer * GAIN_ROWS, GAIN_ROWS), pl.ds(0, rows_d)] = wide(gains[layer])
    for which in range(BIAS_ROWS):
        small[pl.ds((GAIN_ROWS + which) * layers, layers), pl.ds(0, rows_d)] = wide(biases[which])
    wide_small[pl.ds(0, layers), :] = wide(up_bias[...])

    tinies = []
    for k, shard in enumerate(side_me + (far_me,)):
        tinies.append(remote(
            small, small_all.at[me], p_send.at[0, k], p_recv.at[0, k], (shard, rep)))
        tinies.append(remote(
            wide_small, wide_all.at[me], p_send.at[1, k], p_recv.at[1, k], (shard, rep)))
    tinies_own = [
        local(small, small_all.at[me], io_sem.at[2]),
        local(wide_small, wide_all.at[me], io_sem.at[3]),
    ]

    load_x.wait()
    stream[...] = jnp.zeros_like(stream)
    stream[pl.ds(0, tokens), :] = x_in[...]
    unit, inverse = standardize(stream[...])
    unit_one[0] = unit
    inv_one[0] = inverse
    live = jnp.where(counts[0] > 0, 1.0, 0.0).astype(FULL)
    load_cot.wait()
    grad[...] = jnp.zeros_like(grad)
    grad[pl.ds(0, tokens), :] = cot[...] * live

    for copy in tinies:
        copy.wait_recv()
    for copy in tinies_own:
        copy.wait()
    for s in range(shards):
        par[:, pl.ds(s * rows_d, rows_d)] = small_all[s][:, :rows_d]
        per = wide_small.shape[1]
        par_up[:, pl.ds(s * per, per)] = wide_all[s]

    def gain_of(layer, which):
        return par[pl.ds(layer * GAIN_ROWS + which, 1), :]

    def bias_row(layer, which):
        return (GAIN_ROWS + which) * layers + layer

    def bias_of(layer, which):
        return par[pl.ds(bias_row(layer, which), 1), :]

    key_mask = jnp.where(
        lax.broadcasted_iota(jnp.int32, (1, padded), 1) < tokens, 0.0, -1e30).astype(FULL)
    lane_half = lax.broadcasted_iota(jnp.int32, (padded, 2 * HD), 1) < HD

    def one_head(value, which):
        keep = lane_half if which == 0 else jnp.logical_not(lane_half)
        return jnp.where(keep, value, jnp.zeros_like(value))

    def pair(p):
        return pl.ds(p * 2 * HD, 2 * HD)

    def project(layer):
        normed = (unit_one[layer] * gain_of(layer, 0) + bias_of(layer, 0)).astype(LOW)
        normed_one[layer] = normed
        queries[layer] = (
            (product(normed, w_qkv[layer, :, pl.ds(0, width)]) + bias_of(layer, 1)) * factor
        ).astype(LOW)
        key_rows[layer] = product(normed, w_qkv[layer, :, pl.ds(width, width)]).astype(LOW)
        values[layer] = (
            product(normed, w_qkv[layer, :, pl.ds(2 * width, width)]) + bias_of(layer, 2)
        ).astype(LOW)

    def attend(layer, p):
        q, k, v = (ref[layer, :, pair(p)] for ref in (queries, key_rows, values))
        total = None
        for h in range(2):
            scores = product_right(one_head(q, h), k) + key_mask
            log_total = jnp.log(jnp.sum(jnp.exp(scores), -1, keepdims=True))
            prob = jnp.exp(scores - log_total)
            probs[layer, 2 * p + h] = prob
            term = product(prob.astype(LOW), one_head(v, h))
            total = term if total is None else total + term
        mixed[layer, :, pair(p)] = total.astype(LOW)

    def join(layer):
        middle = stream[...] + product(mixed[layer], w_out[layer]) + bias_of(layer, 3)
        stream[...] = middle
        unit, inverse = standardize(middle)
        unit_two[layer] = unit
        inv_two[layer] = inverse
        normed_two[layer] = (unit * gain_of(layer, 1) + bias_of(layer, 4)).astype(LOW)

    chunk = 256

    def expand(layer, j):
        cols = pl.ds(j * chunk, chunk)
        hidden = product(normed_two[layer], w_up[layer, :, cols]) + par_up[pl.ds(layer, 1), cols]
        below = 0.5 * (1.0 + lax.erf(hidden * INV_ROOT_TWO))
        activated[layer, :, cols] = (hidden * below).astype(LOW)
        dens = jnp.exp(-0.5 * hidden * hidden) * INV_ROOT_TWO_PI
        slope[layer, :, cols] = below + hidden * dens

    def contract(layer):
        result = stream[...] + product(activated[layer], w_down[layer]) + bias_of(layer, 5)
        stream[...] = result
        if layer + 1 < layers:
            unit, inverse = standardize(result)
            unit_one[layer + 1] = unit
            inv_one[layer + 1] = inverse

    subs = sub_items(layers, own_w, shards)
    stage_a, one, two = {}, {}, {}

    def mine(a, dest, half):
        kind, layer, row, rows, start, cols, _ = subs[a]
        return own_g[kind].at[layer, dest, half, pl.ds(row, rows), pl.ds(start, cols)]

    def swap(a):
        kind, layer, row, rows, start, cols, _ = subs[a]
        stage_a[a] = remote(
            own_g[kind].at[layer, :, 1 - core, pl.ds(row, rows), pl.ds(start, cols)], buf_a[a],
            a_send.at[a], a_recv.at[a], mate)

    def both(a, dest):
        return wide(mine(a, dest, core)[...]) + wide(buf_a[a][dest])

    def scatter_one(a):
        turn = subs[a][-1]
        stage_a[a].wait_recv()
        near = side_me[turn]
        buf_s[a][0] = both(a, near).astype(LOW)
        buf_s[a][1] = both(a, far_me).astype(LOW)
        one[a] = remote(
            buf_s[a].at[pl.ds(0, 2)], buf_b[a].at[pl.ds(0, 2)], b_send.at[a], b_recv.at[a],
            side[turn])

    def scatter_two(a):
        turn = 1 - subs[a][-1]
        one[a].wait_recv()
        buf_s[a][2] = (both(a, side_me[turn]) + wide(buf_b[a][1])).astype(LOW)
        two[a] = remote(buf_s[a].at[2], buf_b[a].at[2], c_send.at[a], c_recv.at[a], side[turn])

    def summed(a):
        if a == n_sub:
            return tiny[3]
        return both(a, me) + wide(buf_b[a][0]) + wide(buf_b[a][2])

    def z_first(a):
        if a < n_sub:
            two[a].wait_recv()
        z_own[a][...] = summed(a).astype(z_own[a].dtype)

        @pl.when(jnp.logical_and(jnp.logical_not(inside), jnp.logical_not(center)))
        def _():
            remote(z_own[a], z_in[a], z_send.at[a, 0], z_recv.at[a, 0], inner, keep=False)

    def described(src, dst, send_sem, recv_sem, device):
        return pltpu.make_async_remote_copy(
            src_ref=src, dst_ref=dst, send_sem=send_sem, recv_sem=recv_sem, device_id=device,
            device_id_type=MESH)

    def z_copy(a):
        return described(z_own[a], z_in[a], z_send.at[a, 0], z_recv.at[a, 0], inner)

    def x_copy(a):
        return described(z_own[a], z_cross[a], z_send.at[a, 1], z_recv.at[a, 1], inner)

    def o_copy(a):
        return described(z_fin[a], z_fin[a], z_send.at[a, 2], z_recv.at[a, 2], outer)

    def z_second(a):
        @pl.when(inside)
        def _():
            z_copy(a).wait_recv()
            z_own[a][...] = (summed(a) + wide(z_in[a][...])).astype(z_own[a].dtype)

            @pl.when(jnp.logical_not(center))
            def _():
                z_copy(a).start()

        @pl.when(center)
        def _():
            x_copy(a).start()

    def goal(a):
        kind, layer, row, rows, start, cols, _ = subs[a]
        return totals[kind].at[layer, core, pl.ds(row, rows), pl.ds(start, cols)]

    def e_copy(a):
        return described(z_fin[a], goal(a), e_send.at[a], e_recv.at[a], mate)

    def fin_copy(a):
        return pltpu.make_async_copy(z_fin[a], goal(a), fin_sem.at[a])

    def spread(a):
        @pl.when(inside)
        def _():
            o_copy(a).start()

        if a < n_sub:
            e_copy(a).start()
            fin_copy(a).start()

    def z_third(a):
        @pl.when(center)
        def _():
            x_copy(a).wait_recv()
            z_fin[a][...] = (wide(z_own[a][...]) + wide(z_cross[a][...])).astype(z_fin[a].dtype)
            spread(a)

    def z_fourth(a):
        @pl.when(jnp.logical_not(center))
        def _():
            o_copy(a).wait_recv()
            spread(a)

    def z_done(a):
        if a < n_sub:
            e_copy(a).wait()
            fin_copy(a).wait()

        @pl.when(jnp.logical_not(center))
        def _():
            z_copy(a).wait_send()

        @pl.when(center)
        def _():
            x_copy(a).wait_send()

        @pl.when(inside)
        def _():
            o_copy(a).wait_send()

    def shared(value):
        return value.reshape(shards, 2, value.shape[0] // shards // 2, value.shape[1]).astype(LOW)

    up_row = layers * (GAIN_ROWS + BIAS_ROWS)

    def put_up_bias(layer, start, value):
        for at in range(0, value.shape[1], 128):
            row, lane = divmod(start + at, width)
            tiny[0, pl.ds(up_row + layer * (ff // width) + row, 1), pl.ds(lane, 128)] = (
                value[:, at : at + 128])

    def put_gain(layer, which, value):
        tiny[0, pl.ds(layer * GAIN_ROWS + which, 1), :] = value

    def put_bias(layer, which, value):
        tiny[0, pl.ds(bias_row(layer, which), 1), :] = value

    def back_down(layer):
        low = grad[...].astype(LOW)
        per = ff // shards
        for s in range(shards):
            piece = product_left(activated[layer, :, pl.ds(s * per, per)], low)
            own_g[DOWN][layer, s] = piece.reshape(2, per // 2, width).astype(LOW)
        put_bias(layer, 5, column_sum(grad[...]))

    def back_expand(layer, j):
        low = grad[...].astype(LOW)
        cols = pl.ds(j * chunk, chunk)
        act_grad = product_right(low, w_down[layer, cols, :])
        hid_grad = act_grad * slope[layer, :, cols]
        put_up_bias(layer, j * chunk, column_sum(hid_grad))
        hid_low[:, cols] = hid_grad.astype(LOW)

    def back_up(layer, j):
        cols = pl.ds(j * ff // 2, ff // 2)
        own_g[UP][layer, :, :, :, cols] = shared(product_left(normed_two[layer], hid_low[:, cols]))

    def back_middle(layer):
        norm_grad = product_right(hid_low[...], w_up[layer])
        back, gain, shift = norm_back(
            norm_grad, unit_two[layer], inv_two[layer], gain_of(layer, 1))
        put_gain(layer, 1, gain)
        put_bias(layer, 4, shift)
        mid_grad = grad[...] + back
        grad[...] = mid_grad
        put_bias(layer, 3, column_sum(mid_grad))
        mid_low = mid_grad.astype(LOW)
        own_g[OUT][layer] = shared(product_left(mixed[layer], mid_low))

    def back_mix(layer):
        mix_grad[...] = product_right(grad[...].astype(LOW), w_out[layer]).astype(LOW)

    def back_attend(layer, p):
        q, k, v = (ref[layer, :, pair(p)] for ref in (queries, key_rows, values))
        up = mix_grad[:, pair(p)]
        sums = [None] * 3
        for h in range(2):
            up_h = one_head(up, h)
            prob = probs[layer, 2 * p + h]
            prob_grad = product_right(up_h, v)
            row_dot = jnp.sum(prob * prob_grad, -1, keepdims=True)
            score_grad = (prob * (prob_grad - row_dot)).astype(LOW)
            terms = (
                product(score_grad, one_head(k, h)),
                product_left(score_grad, one_head(q, h)),
                product_left(prob.astype(LOW), up_h),
            )
            sums = [t if s is None else s + t for s, t in zip(sums, terms)]
        query_grad = sums[0] * factor
        start = p * 2 * HD
        tiny[0, pl.ds(bias_row(layer, 1), 1), pair(p)] = column_sum(query_grad)
        tiny[0, pl.ds(bias_row(layer, 2), 1), pair(p)] = column_sum(sums[2])
        for n, value in enumerate((query_grad, sums[1], sums[2])):
            pgrad[:, pl.ds(n * width + start, 2 * HD)] = value.astype(LOW)

    def back_qkv(layer, n):
        cols = pl.ds(n * width, width)
        own_g[QKV][layer, :, :, :, cols] = shared(product_left(normed_one[layer], pgrad[:, cols]))

    def back_first(layer):
        first_grad = product_right(pgrad[...], w_qkv[layer])
        back, gain, shift = norm_back(
            first_grad, unit_one[layer], inv_one[layer], gain_of(layer, 0))
        put_gain(layer, 0, gain)
        put_bias(layer, 0, shift)
        grad[...] = grad[...] + back


    def finish_forward():
        x_in[...] = stream[pl.ds(0, tokens), :] * live
        return local(x_in, act_out.at[:, 0], io_sem.at[0])

    swaps = []

    def tiny_send(n):
        device = (mate, side[0], side[1])[n]
        swaps.append(remote(tiny.at[n], tiny_in.at[n], t_send.at[n], t_recv.at[n], device))

    def tiny_add(n):
        swaps[n].wait_recv()
        tiny[n + 1] = tiny[n] + tiny_in[n]

    def finish_backward():
        cot[...] = grad[pl.ds(0, tokens), :]
        return local(cot, grad_out.at[:, 0], io_sem.at[1])

    relay(0)
    first(3)
    relay(1)
    first(4)
    relay(2)
    first(5)
    reach(0)
    relay(3)
    first(6)
    reach(1)
    relay(4)
    first(7)
    cross(0)
    reach(2)
    reach(3)
    settle(2)
    project(0)
    relay(5)
    for j in range(0, 3):
        attend(0, j)
    reach(4)
    relay(6)
    cross(1)
    relay(7)
    settle(4)
    join(0)
    settle(0)
    for j in range(0, 4):
        expand(0, j)
    cross(3)
    expand(0, 4)
    expand(0, 5)
    reach(5)
    reach(6)
    settle(3)
    contract(0)
    reach(7)
    settle(5)
    project(1)
    for j in range(0, 3):
        attend(1, j)
    settle(7)
    join(1)
    settle(1)
    for j in range(0, 6):
        expand(1, j)
    back_down(1)
    swap(0)
    cross(6)
    swap(1)
    scatter_one(0)
    settle(6)
    for j in range(0, 6):
        back_expand(1, j)
    back_up(1, 0)
    swap(2)
    scatter_one(1)
    back_up(1, 1)
    swap(3)
    back_middle(1)
    swap(4)
    back_mix(1)
    back_attend(1, 0)
    scatter_one(2)
    scatter_one(3)
    back_attend(1, 1)
    back_attend(1, 2)
    back_qkv(1, 0)
    scatter_two(0)
    back_qkv(1, 1)
    swap(5)
    back_qkv(1, 2)
    swap(6)
    back_first(1)
    scatter_two(1)
    back_down(0)
    swap(7)
    swap(8)
    back_expand(0, 0)
    back_expand(0, 1)
    scatter_one(5)
    for j in range(2, 6):
        back_expand(0, j)
    back_up(0, 0)
    swap(9)
    scatter_one(6)
    scatter_two(2)
    back_up(0, 1)
    swap(10)
    back_middle(0)
    swap(11)
    scatter_two(3)
    z_first(1)
    back_mix(0)
    back_attend(0, 0)
    z_first(0)
    scatter_one(4)
    back_attend(0, 1)
    scatter_one(9)
    scatter_two(6)
    back_attend(0, 2)
    scatter_two(5)
    back_qkv(0, 0)
    back_qkv(0, 1)
    swap(12)
    back_qkv(0, 2)
    swap(13)
    z_second(1)
    z_first(2)
    scatter_one(8)
    z_first(3)
    back_first(0)
    store_grad = finish_backward()
    tiny_send(0)
    z_second(0)
    scatter_two(4)
    contract(1)
    store_act = finish_forward()
    scatter_one(12)
    z_first(5)
    tiny_add(0)
    tiny_send(1)
    scatter_one(13)
    z_third(1)
    z_second(2)
    scatter_two(9)
    z_first(6)
    z_first(4)
    z_third(0)
    z_second(3)
    scatter_two(8)
    scatter_one(10)
    z_second(5)
    z_fourth(1)
    z_third(2)
    scatter_two(13)
    z_second(6)
    scatter_two(12)
    z_second(4)
    scatter_one(7)
    z_fourth(0)
    tiny_add(1)
    tiny_send(2)
    z_third(3)
    z_first(9)
    z_first(8)
    z_third(5)
    z_fourth(2)
    z_first(13)
    z_third(6)
    scatter_one(11)
    scatter_two(10)
    z_third(4)
    z_fourth(3)
    z_second(9)
    z_first(12)
    scatter_two(7)
    tiny_add(2)
    z_first(n_sub)
    z_fourth(5)
    z_second(8)
    z_fourth(6)
    z_second(13)
    z_first(10)
    z_fourth(4)
    scatter_two(11)
    z_third(9)
    z_second(12)
    z_first(7)
    z_second(n_sub)
    z_third(8)
    z_first(11)
    z_third(13)
    z_second(10)
    z_fourth(9)
    z_third(12)
    z_second(7)
    z_third(n_sub)
    z_fourth(8)
    z_second(11)
    z_fourth(13)
    z_third(10)
    z_fourth(12)
    z_third(7)
    z_fourth(n_sub)
    z_third(11)
    z_fourth(10)
    z_fourth(7)
    z_fourth(11)
    done = z_fin[n_sub][...]
    picked = None
    for s in range(shards):
        hit = jnp.where(me == s, 1.0, 0.0).astype(FULL)
        term = done[:up_row, s * rows_d : (s + 1) * rows_d] * hit
        picked = term if picked is None else picked + term
    for layer in range(layers):
        small_held[0][layer] = picked[layer * GAIN_ROWS : (layer + 1) * GAIN_ROWS]
        row = None
        for s in range(shards):
            at = up_row + layer * (ff // width) + s
            hit = jnp.where(me == s, 1.0, 0.0).astype(FULL)
            term = done[at : at + 1] * hit
            row = term if row is None else row + term
        small_held[2][pl.ds(layer, 1), :] = row
    for which in range(BIAS_ROWS):
        small_held[1][which] = picked[bias_row(0, which) : bias_row(0, which) + layers]
    store_small = [local(small_held[n], small_out[n], s_sem.at[n]) for n in range(3)]
    for a in range(n_sub + 1):
        z_done(a)
    for copy in store_small:
        copy.wait()
    for copy in sent:
        copy.wait_send()
    store_act.wait()
    store_grad.wait()


def finish_kernel(count, *refs):
    ins, outs, refs = refs[:count], refs[count : 2 * count], refs[2 * count :]
    held, refs = refs[:count], refs[count:]
    wides, (load_sem, store_sem) = refs[:-2], refs[-2:]
    parts = []
    for n in range(2, 6):
        parts += [(n, layer) for layer in range(ins[n].shape[0])]
    parts += [(n, None) for n in range(count) if not 2 <= n < 6]

    def view(ref, layer):
        return ref if layer is None else ref.at[layer]

    loads, stores = [], []
    for at, (n, layer) in enumerate(parts):
        copy = pltpu.make_async_copy(view(ins[n], layer), view(held[n], layer), load_sem.at[at])
        copy.start()
        loads.append(copy)
    for at, (n, layer) in enumerate(parts):
        loads[at].wait()
        src = held[n]
        if layer is not None:
            src = wides[n - 2]
            src[layer] = held[n][layer].astype(FULL)
        copy = pltpu.make_async_copy(view(src, layer), view(outs[n], layer), store_sem.at[at])
        copy.start()
        stores.append(copy)
    for copy in stores:
        copy.wait()


def finish(arrays):
    count = len(arrays)
    parts = count - 4 + 4 * arrays[2].shape[0]
    specs = [pl.BlockSpec(memory_space=pl.ANY)] * count
    return pl.pallas_call(
        functools.partial(finish_kernel, count),
        out_shape=[jax.ShapeDtypeStruct(x.shape, FULL) for x in arrays],
        in_specs=specs,
        out_specs=specs,
        scratch_shapes=[pltpu.VMEM(x.shape, x.dtype) for x in arrays]
        + [pltpu.VMEM(x.shape, FULL) for x in arrays[2:6]]
        + [pltpu.SemaphoreType.DMA((parts,))] * 2,
        compiler_params=pltpu.CompilerParams(vmem_limit_bytes=VMEM_LIMIT),
        name="widen",
    )(*arrays)


def on_device(shards, replicas, images, cotangent, counts, *stacks):
    weights, (gains, biases, up_bias) = stacks[:4], stacks[4:]
    layers, rows_d, _ = weights[QKV].shape
    deep = replicas // 2
    tokens, width = images.shape[1:]
    padded = -(-tokens // 16) * 16
    ff = weights[UP].shape[2]
    heads = width // HD
    qkv = weights[QKV].shape[2]
    sems = pltpu.SemaphoreType.DMA
    low = lambda *s: pltpu.VMEM(s, LOW)
    full = lambda *s: pltpu.VMEM(s, FULL)
    small_rows = layers * (GAIN_ROWS + BIAS_ROWS)
    small_rows_pad = -(-small_rows // 8) * 8
    per_up = up_bias.shape[1]
    scratch = [
        full(tokens, width), full(tokens, width), full(padded, width), full(padded, width),
        low(layers, shards * rows_d, qkv), low(layers, shards * rows_d, width),
        low(layers, shards * rows_d, ff), low(layers, ff, width),
        full(small_rows_pad, width), full(8, ff),
        full(small_rows_pad, 128), full(shards, small_rows_pad, 128),
        full(8, per_up), full(shards, 8, per_up),
        full(layers, padded, width), full(layers, padded, 1), low(layers, padded, width),
        low(layers, padded, width), low(layers, padded, width), low(layers, padded, width),
        full(layers, heads, padded, padded), low(layers, padded, width),
        full(layers, padded, width), full(layers, padded, 1), low(layers, padded, width),
        low(layers, padded, ff), full(layers, padded, ff), low(padded, ff), low(padded, width),
        low(padded, qkv),
    ]
    halves = [w.shape[1] // 2 for w in weights]
    columns = [w.shape[2] for w in weights]
    scratch += [low(layers, shards, 2, h, c) for h, c in zip(halves, columns)]
    shapes = [(sub[3], sub[5]) for sub in sub_items(layers, weights, shards)]
    n_sub = len(shapes)
    scratch += [low(shards, *s) for s in shapes] + [low(3, *s) for s in shapes] * 2
    tiny_rows = small_rows + layers * (ff // width)
    scratch += ([low(*s) for s in shapes] + [full(tiny_rows, width)]) * 4
    scratch += [full(4, tiny_rows, width), full(3, tiny_rows, width)]
    n_items = 4 * layers
    scratch += [
        sems((n_items, 2)), sems((n_items, 2)), sems((n_items,)), sems((n_items,)),
        sems((n_items, 3)), sems((n_items, 3)), sems((n_items, 3)), sems((n_items, 3)),
        sems((n_items, 3)), sems((n_items, 3)), sems((2, 3)), sems((2, 3)),
        sems((n_items,)), sems((4,)), sems((n_sub,)), sems((n_sub,)), sems((n_sub,)),
        sems((n_sub,)), sems((n_sub,)), sems((n_sub,)), sems((n_sub + 1, 3)), sems((n_sub + 1, 3)),
        sems((n_sub,)), sems((n_sub,)), sems((n_sub,)), sems((3,)), sems((3,)),
    ]
    shape = jax.ShapeDtypeStruct
    images, cotangent, biases = (x.transpose(1, 0, 2) for x in (images, cotangent, biases))
    scratch += [sems((3,))] + [full(*x.shape) for x in (gains, biases, up_bias)]
    outs = [shape(images.shape, FULL), shape(images.shape, FULL)]
    outs += [shape((layers, 2, h, c), LOW) for h, c in zip(halves, columns)]
    outs += [shape(x.shape, FULL) for x in (gains, biases, up_bias)]
    hbm, vmem = pl.BlockSpec(memory_space=pl.ANY), pl.BlockSpec(memory_space=pltpu.VMEM)
    done = pl.pallas_call(
        functools.partial(fused_kernel, shards, deep),
        out_shape=outs,
        in_specs=[hbm, hbm, pl.BlockSpec(memory_space=pltpu.SMEM)] + [hbm] * 4 + [vmem] * 3,
        out_specs=[hbm] * 9,
        scratch_shapes=scratch,
        compiler_params=pltpu.CompilerParams(
            collective_id=0, has_side_effects=True, vmem_limit_bytes=VMEM_LIMIT
        ),
        name="encoder_step",
    )(images, cotangent, counts, *weights, gains, biases, up_bias)
    done = list(done)
    for kind in range(4):
        done[2 + kind] = done[2 + kind].reshape(weights[kind].shape)
    done = list(finish(done))
    for n in (0, 1, 7):
        done[n] = done[n].transpose(1, 0, 2)
    return tuple(done)


def solution(mesh):
    in_specs = (
        P(("shard", "replica"), None, None),
        P(("shard", "replica"), None, None),
        P(("shard", "replica")),
        P(None, "shard", None),
        P(None, "shard", None),
        P(None, "shard", None),
        P(None, "shard", None),
        P(None, None, "shard"),
        P(None, None, "shard"),
        P(None, "shard"),
    )
    out_specs = (
        P(("shard", "replica"), None, None),
        P(("shard", "replica"), None, None),
        P(None, "shard", None),
        P(None, "shard", None),
        P(None, "shard", None),
        P(None, "shard", None),
        P(None, None, "shard"),
        P(None, None, "shard"),
        P(None, "shard"),
    )
    return jax.shard_map(
        functools.partial(on_device, mesh.shape["shard"], mesh.shape["replica"]), mesh=mesh, in_specs=in_specs, out_specs=out_specs, check_vma=False
    )
```

```python
import functools

import jax
import jax.numpy as jnp
from jax import lax
from jax.experimental import pallas as pl
from jax.experimental.pallas import tpu as pltpu
from jax.sharding import PartitionSpec as P

HD = 64
EPS = 1e-06
INV_ROOT_TWO = 0.7071067811865476
INV_ROOT_TWO_PI = 0.3989422804014327
LOW = jnp.bfloat16
FULL = jnp.float32
MESH = pl.DeviceIdType.MESH
VMEM_LIMIT = 60 * 1024 * 1024

QKV, OUT, UP, DOWN = range(4)
GAIN_ROWS, BIAS_ROWS = 2, 6


def product(left, right):
    return jnp.dot(left, right, preferred_element_type=FULL)


def product_left(left, right):
    return lax.dot_general(
        left, right, (((0,), (0,)), ((), ())), preferred_element_type=FULL
    )


def product_right(left, right):
    return lax.dot_general(
        left, right, (((1,), (1,)), ((), ())), preferred_element_type=FULL
    )


def wide(value):
    return value.astype(FULL)


def column_sum(value):
    return jnp.sum(value, 0, keepdims=True)


def standardize(values):
    center = jnp.mean(values, -1, keepdims=True)
    centered = values - center
    spread = jnp.mean(centered * centered, -1, keepdims=True)
    inverse = lax.rsqrt(spread + EPS)
    return centered * inverse, inverse


def norm_back(upstream, unit, inverse, gain):
    scaled = upstream * gain
    inner = (
        scaled
        - jnp.mean(scaled, -1, keepdims=True)
        - unit * jnp.mean(scaled * unit, -1, keepdims=True)
    )
    return inverse * inner, column_sum(upstream * unit), column_sum(upstream)


SUBS = 7


def sub_items(layers, weights, shards):
    width, ff, qkv = (weights[kind].shape[2] for kind in (OUT, UP, QKV))
    half_d = weights[QKV].shape[1] // 2
    rows = weights[DOWN].shape[1] // 4
    cut = (qkv + width) // 2
    subs = []
    for layer in reversed(range(layers)):
        subs += [
            (DOWN, layer, 0, rows, 0, width, 0),
            (DOWN, layer, rows, rows, 0, width, 1),
            (UP, layer, 0, half_d, 0, ff // 2, 0),
            (UP, layer, 0, half_d, ff // 2, ff // 2, 1),
            (OUT, layer, 0, half_d, 0, width, 1),
            (QKV, layer, 0, half_d, 0, cut, 0),
            (QKV, layer, 0, half_d, cut, qkv - cut, 1),
        ]
    return subs


def fused_kernel(shards, deep, *refs):
    (images, cotangent, counts, *own_w), refs = refs[:7], refs[7:]
    (gains, biases, up_bias), refs = refs[:3], refs[3:]
    (act_out, grad_out), refs = refs[:2], refs[2:]
    totals, refs = refs[:4], refs[4:]
    small_out, refs = refs[:3], refs[3:]
    (x_in, cot, stream, grad, w_qkv, w_out, w_up, w_down, par, par_up, small, small_all, wide_small,
     wide_all), refs = refs[:14], refs[14:]
    (unit_one, inv_one, normed_one, queries, key_rows, values, probs, mixed, unit_two, inv_two,
     normed_two, activated, slope, hid_low, mix_grad, pgrad), refs = refs[:16], refs[16:]
    own_g, refs = refs[:4], refs[4:]
    n_sub = SUBS * own_w[0].shape[0]
    buf_a, refs = refs[:n_sub], refs[n_sub:]
    buf_s, refs = refs[:n_sub], refs[n_sub:]
    buf_b, refs = refs[:n_sub], refs[n_sub:]
    z_own, refs = refs[: n_sub + 1], refs[n_sub + 1 :]
    z_in, refs = refs[: n_sub + 1], refs[n_sub + 1 :]
    z_cross, refs = refs[: n_sub + 1], refs[n_sub + 1 :]
    z_fin, refs = refs[: n_sub + 1], refs[n_sub + 1 :]
    (tiny, tiny_in), refs = refs[:2], refs[2:]
    (f_send, f_recv, r_send, r_recv, m_send, m_recv, x_send, x_recv, q_send, q_recv, p_send, p_recv,
     own_sem, io_sem, a_send, a_recv, b_send, b_recv, c_send, c_recv, z_send, z_recv, e_send, e_recv,
     fin_sem, t_send, t_recv, s_sem, *small_held) = refs

    layers, rows_d, _ = own_w[QKV].shape
    width = x_in.shape[1]
    tokens = x_in.shape[0]
    padded = stream.shape[0]
    heads = width // HD
    ff = w_up.shape[2]
    factor = HD ** (-0.5)
    weights = (w_qkv, w_out, w_up, w_down)

    me = lax.axis_index("shard")
    rep = lax.axis_index("replica")
    core = lax.rem(rep, 2)
    depth = lax.div(rep, 2)
    parity = lax.rem(depth, 2)
    mid = deep // 2
    left = depth < mid
    place = jnp.where(left, depth, deep - 1 - depth)
    inner_depth = jnp.where(left, depth + 1, depth - 1)
    outer_depth = jnp.where(left, depth - 1, depth + 1)
    mate = (me, rep + 1 - 2 * core)
    across = (me, (depth + 1 - 2 * parity) * 2 + core)
    inner = (me, inner_depth * 2 + core)
    outer = (me, outer_depth * 2 + core)
    side_me = (me + 1 - 2 * lax.rem(me, 2), lax.rem(me + 2, shards))
    side = [(s, rep) for s in side_me]
    far_me = shards - 1 - me
    inside = place > 0
    center = place == mid - 1

    def local(src, dst, sem):
        copy = pltpu.make_async_copy(src, dst, sem)
        copy.start()
        return copy

    load_x = local(images.at[:, 0], x_in, io_sem.at[0])
    load_cot = local(cotangent.at[:, 0], cot, io_sem.at[1])

    barrier = pltpu.get_barrier_semaphore()
    for device in (mate, across, side[0], side[1], (far_me, rep), inner):
        pl.semaphore_signal(barrier, inc=1, device_id=device, device_id_type=MESH)

    @pl.when(inside)
    def _():
        pl.semaphore_signal(barrier, inc=1, device_id=outer, device_id_type=MESH)

    sent = []

    def remote(src, dst, send_sem, recv_sem, device, keep=True):
        copy = pltpu.make_async_remote_copy(
            src_ref=src, dst_ref=dst, send_sem=send_sem, recv_sem=recv_sem, device_id=device,
            device_id_type=MESH)
        copy.start()
        if keep:
            sent.append(copy)
        return copy

    items = [
        (UP, 0), (UP, 1), (QKV, 0), (DOWN, 0),
        (OUT, 0), (QKV, 1), (DOWN, 1), (OUT, 1),
    ]
    via_of, loads = [], [0, 0]
    for kind, _ in items:
        via_of.append(0 if loads[1] <= loads[0] else 1)
        loads[1 - via_of[-1]] += own_w[kind].shape[1] * own_w[kind].shape[2] // (
            2 if kind in (UP, DOWN) else 1)

    def part(ref, kind, layer, first_row, rows, which):
        half = rows // 2
        start = first_row + core * half
        if kind == UP:
            cut = ff // 2
            return ref.at[layer, pl.ds(pl.multiple_of(start, 16), half),
                          pl.ds(pl.multiple_of(which * cut, 128), cut)]
        if kind == DOWN:
            return ref.at[layer, pl.ds(pl.multiple_of(start + which * (half // 2), 16), half // 2)]
        return ref.at[layer, pl.ds(pl.multiple_of(start, 16), half)]

    def held(item, shard, which):
        kind, layer = items[item]
        rows = own_w[kind].shape[1]
        return part(weights[kind], kind, layer, shard * rows, rows, which)

    firsts, relays, passed, crossed, again, owned = {}, {}, {}, {}, {}, {}

    def first(item):
        kind, layer = items[item]
        rows = own_w[kind].shape[1]
        src = part(own_w[kind], kind, layer, 0, rows, parity)
        firsts[item] = [
            remote(src, held(item, me, parity), f_send.at[item, k], f_recv.at[item, k], side[k])
            for k in range(2)
        ]
        owned[item] = local(
            own_w[kind].at[layer],
            weights[kind].at[layer, pl.ds(pl.multiple_of(me * rows, 16), rows)], own_sem.at[item])
        passed[item] = []
        crossed[item] = []

    def hand_on(item, slot, shard):
        piece = held(item, shard, parity)
        if items[item][0] in (UP, DOWN):
            crossed[item].append((slot, shard, remote(
                piece, piece, x_send.at[item, slot], x_recv.at[item, slot], across)))
        passed[item].append(
            remote(piece, piece, m_send.at[item, slot], m_recv.at[item, slot], mate))

    def relay(item):
        via = via_of[item]
        for k in (via, 1 - via):
            firsts[item][k].wait_recv()
            if k == via:
                piece = held(item, side_me[k], parity)
                relays[item] = remote(
                    piece, piece, r_send.at[item], r_recv.at[item], side[1 - k])
            hand_on(item, k, side_me[k])

    def reach(item):
        relays[item].wait_recv()
        hand_on(item, 2, far_me)

    def cross(item):
        for slot, shard, copy in crossed[item]:
            copy.wait_recv()
            piece = held(item, shard, 1 - parity)
            passed[item].append(
                remote(piece, piece, q_send.at[item, slot], q_recv.at[item, slot], mate))

    def settle(item):
        for copy in passed[item]:
            copy.wait_recv()
        owned[item].wait()

    pl.semaphore_wait(barrier, 6 + jnp.where(inside, 1, 0))

    for item in range(3):
        first(item)

    small[...] = jnp.zeros_like(small)
    wide_small[...] = jnp.zeros_like(wide_small)
    for layer in range(layers):
        small[pl.ds(layer * GAIN_ROWS, GAIN_ROWS), pl.ds(0, rows_d)] = wide(gains[layer])
    for which in range(BIAS_ROWS):
        small[pl.ds((GAIN_ROWS + which) * layers, layers), pl.ds(0, rows_d)] = wide(biases[which])
    wide_small[pl.ds(0, layers), :] = wide(up_bias[...])

    tinies = []
    for k, shard in enumerate(side_me + (far_me,)):
        tinies.append(remote(
            small, small_all.at[me], p_send.at[0, k], p_recv.at[0, k], (shard, rep)))
        tinies.append(remote(
            wide_small, wide_all.at[me], p_send.at[1, k], p_recv.at[1, k], (shard, rep)))
    tinies_own = [
        local(small, small_all.at[me], io_sem.at[2]),
        local(wide_small, wide_all.at[me], io_sem.at[3]),
    ]

    load_x.wait()
    stream[...] = jnp.zeros_like(stream)
    stream[pl.ds(0, tokens), :] = x_in[...]
    unit, inverse = standardize(stream[...])
    unit_one[0] = unit
    inv_one[0] = inverse
    live = jnp.where(counts[0] > 0, 1.0, 0.0).astype(FULL)
    load_cot.wait()
    grad[...] = jnp.zeros_like(grad)
    grad[pl.ds(0, tokens), :] = cot[...] * live

    for copy in tinies:
        copy.wait_recv()
    for copy in tinies_own:
        copy.wait()
    for s in range(shards):
        par[:, pl.ds(s * rows_d, rows_d)] = small_all[s][:, :rows_d]
        per = wide_small.shape[1]
        par_up[:, pl.ds(s * per, per)] = wide_all[s]

    def gain_of(layer, which):
        return par[pl.ds(layer * GAIN_ROWS + which, 1), :]

    def bias_row(layer, which):
        return (GAIN_ROWS + which) * layers + layer

    def bias_of(layer, which):
        return par[pl.ds(bias_row(layer, which), 1), :]

    key_mask = jnp.where(
        lax.broadcasted_iota(jnp.int32, (1, padded), 1) < tokens, 0.0, -1e30).astype(FULL)
    lane_half = lax.broadcasted_iota(jnp.int32, (padded, 2 * HD), 1) < HD

    def one_head(value, which):
        keep = lane_half if which == 0 else jnp.logical_not(lane_half)
        return jnp.where(keep, value, jnp.zeros_like(value))

    def pair(p):
        return pl.ds(p * 2 * HD, 2 * HD)

    def project(layer):
        normed = (unit_one[layer] * gain_of(layer, 0) + bias_of(layer, 0)).astype(LOW)
        normed_one[layer] = normed
        queries[layer] = (
            (product(normed, w_qkv[layer, :, pl.ds(0, width)]) + bias_of(layer, 1)) * factor
        ).astype(LOW)
        key_rows[layer] = product(normed, w_qkv[layer, :, pl.ds(width, width)]).astype(LOW)
        values[layer] = (
            product(normed, w_qkv[layer, :, pl.ds(2 * width, width)]) + bias_of(layer, 2)
        ).astype(LOW)

    def attend(layer, p):
        q, k, v = (ref[layer, :, pair(p)] for ref in (queries, key_rows, values))
        total = None
        for h in range(2):
            scores = product_right(one_head(q, h), k) + key_mask
            log_total = jnp.log(jnp.sum(jnp.exp(scores), -1, keepdims=True))
            prob = jnp.exp(scores - log_total)
            probs[layer, 2 * p + h] = prob
            term = product(prob.astype(LOW), one_head(v, h))
            total = term if total is None else total + term
        mixed[layer, :, pair(p)] = total.astype(LOW)

    def join(layer):
        middle = stream[...] + product(mixed[layer], w_out[layer]) + bias_of(layer, 3)
        stream[...] = middle
        unit, inverse = standardize(middle)
        unit_two[layer] = unit
        inv_two[layer] = inverse
        normed_two[layer] = (unit * gain_of(layer, 1) + bias_of(layer, 4)).astype(LOW)

    chunk = 256

    def expand(layer, j):
        cols = pl.ds(j * chunk, chunk)
        hidden = product(normed_two[layer], w_up[layer, :, cols]) + par_up[pl.ds(layer, 1), cols]
        below = 0.5 * (1.0 + lax.erf(hidden * INV_ROOT_TWO))
        activated[layer, :, cols] = (hidden * below).astype(LOW)
        dens = jnp.exp(-0.5 * hidden * hidden) * INV_ROOT_TWO_PI
        slope[layer, :, cols] = below + hidden * dens

    def contract(layer):
        result = stream[...] + product(activated[layer], w_down[layer]) + bias_of(layer, 5)
        stream[...] = result
        if layer + 1 < layers:
            unit, inverse = standardize(result)
            unit_one[layer + 1] = unit
            inv_one[layer + 1] = inverse

    subs = sub_items(layers, own_w, shards)
    stage_a, one, two = {}, {}, {}

    def mine(a, dest, half):
        kind, layer, row, rows, start, cols, _ = subs[a]
        return own_g[kind].at[layer, dest, half, pl.ds(row, rows), pl.ds(start, cols)]

    def swap(a):
        kind, layer, row, rows, start, cols, _ = subs[a]
        stage_a[a] = remote(
            own_g[kind].at[layer, :, 1 - core, pl.ds(row, rows), pl.ds(start, cols)], buf_a[a],
            a_send.at[a], a_recv.at[a], mate)

    def both(a, dest):
        return wide(mine(a, dest, core)[...]) + wide(buf_a[a][dest])

    def scatter_one(a):
        turn = subs[a][-1]
        stage_a[a].wait_recv()
        near = side_me[turn]
        buf_s[a][0] = both(a, near).astype(LOW)
        buf_s[a][1] = both(a, far_me).astype(LOW)
        one[a] = remote(
            buf_s[a].at[pl.ds(0, 2)], buf_b[a].at[pl.ds(0, 2)], b_send.at[a], b_recv.at[a],
            side[turn])

    def scatter_two(a):
        turn = 1 - subs[a][-1]
        one[a].wait_recv()
        buf_s[a][2] = (both(a, side_me[turn]) + wide(buf_b[a][1])).astype(LOW)
        two[a] = remote(buf_s[a].at[2], buf_b[a].at[2], c_send.at[a], c_recv.at[a], side[turn])

    def summed(a):
        if a == n_sub:
            return tiny[3]
        return both(a, me) + wide(buf_b[a][0]) + wide(buf_b[a][2])

    def z_first(a):
        if a < n_sub:
            two[a].wait_recv()
        z_own[a][...] = summed(a).astype(z_own[a].dtype)

        @pl.when(jnp.logical_and(jnp.logical_not(inside), jnp.logical_not(center)))
        def _():
            remote(z_own[a], z_in[a], z_send.at[a, 0], z_recv.at[a, 0], inner, keep=False)

    def described(src, dst, send_sem, recv_sem, device):
        return pltpu.make_async_remote_copy(
            src_ref=src, dst_ref=dst, send_sem=send_sem, recv_sem=recv_sem, device_id=device,
            device_id_type=MESH)

    def z_copy(a):
        return described(z_own[a], z_in[a], z_send.at[a, 0], z_recv.at[a, 0], inner)

    def x_copy(a):
        return described(z_own[a], z_cross[a], z_send.at[a, 1], z_recv.at[a, 1], inner)

    def o_copy(a):
        return described(z_fin[a], z_fin[a], z_send.at[a, 2], z_recv.at[a, 2], outer)

    def z_second(a):
        @pl.when(inside)
        def _():
            z_copy(a).wait_recv()
            z_own[a][...] = (summed(a) + wide(z_in[a][...])).astype(z_own[a].dtype)

            @pl.when(jnp.logical_not(center))
            def _():
                z_copy(a).start()

        @pl.when(center)
        def _():
            x_copy(a).start()

    def goal(a):
        kind, layer, row, rows, start, cols, _ = subs[a]
        return totals[kind].at[layer, core, pl.ds(row, rows), pl.ds(start, cols)]

    def e_copy(a):
        return described(z_fin[a], goal(a), e_send.at[a], e_recv.at[a], mate)

    def fin_copy(a):
        return pltpu.make_async_copy(z_fin[a], goal(a), fin_sem.at[a])

    def spread(a):
        @pl.when(inside)
        def _():
            o_copy(a).start()

        if a < n_sub:
            e_copy(a).start()
            fin_copy(a).start()

    def z_third(a):
        @pl.when(center)
        def _():
            x_copy(a).wait_recv()
            z_fin[a][...] = (wide(z_own[a][...]) + wide(z_cross[a][...])).astype(z_fin[a].dtype)
            spread(a)

    def z_fourth(a):
        @pl.when(jnp.logical_not(center))
        def _():
            o_copy(a).wait_recv()
            spread(a)

    def z_done(a):
        if a < n_sub:
            e_copy(a).wait()
            fin_copy(a).wait()

        @pl.when(jnp.logical_not(center))
        def _():
            z_copy(a).wait_send()

        @pl.when(center)
        def _():
            x_copy(a).wait_send()

        @pl.when(inside)
        def _():
            o_copy(a).wait_send()

    def shared(value):
        return value.reshape(shards, 2, value.shape[0] // shards // 2, value.shape[1]).astype(LOW)

    up_row = layers * (GAIN_ROWS + BIAS_ROWS)

    def put_up_bias(layer, start, value):
        for at in range(0, value.shape[1], 128):
            row, lane = divmod(start + at, width)
            tiny[0, pl.ds(up_row + layer * (ff // width) + row, 1), pl.ds(lane, 128)] = (
                value[:, at : at + 128])

    def put_gain(layer, which, value):
        tiny[0, pl.ds(layer * GAIN_ROWS + which, 1), :] = value

    def put_bias(layer, which, value):
        tiny[0, pl.ds(bias_row(layer, which), 1), :] = value

    def back_down(layer):
        low = grad[...].astype(LOW)
        per = ff // shards
        for s in range(shards):
            piece = product_left(activated[layer, :, pl.ds(s * per, per)], low)
            own_g[DOWN][layer, s] = piece.reshape(2, per // 2, width).astype(LOW)
        put_bias(layer, 5, column_sum(grad[...]))

    def back_expand(layer, j):
        low = grad[...].astype(LOW)
        cols = pl.ds(j * chunk, chunk)
        act_grad = product_right(low, w_down[layer, cols, :])
        hid_grad = act_grad * slope[layer, :, cols]
        put_up_bias(layer, j * chunk, column_sum(hid_grad))
        hid_low[:, cols] = hid_grad.astype(LOW)

    def back_up(layer, j):
        cols = pl.ds(j * ff // 2, ff // 2)
        own_g[UP][layer, :, :, :, cols] = shared(product_left(normed_two[layer], hid_low[:, cols]))

    def back_middle(layer):
        norm_grad = product_right(hid_low[...], w_up[layer])
        back, gain, shift = norm_back(
            norm_grad, unit_two[layer], inv_two[layer], gain_of(layer, 1))
        put_gain(layer, 1, gain)
        put_bias(layer, 4, shift)
        mid_grad = grad[...] + back
        grad[...] = mid_grad
        put_bias(layer, 3, column_sum(mid_grad))
        mid_low = mid_grad.astype(LOW)
        own_g[OUT][layer] = shared(product_left(mixed[layer], mid_low))

    def back_mix(layer):
        mix_grad[...] = product_right(grad[...].astype(LOW), w_out[layer]).astype(LOW)

    def back_attend(layer, p):
        q, k, v = (ref[layer, :, pair(p)] for ref in (queries, key_rows, values))
        up = mix_grad[:, pair(p)]
        sums = [None] * 3
        for h in range(2):
            up_h = one_head(up, h)
            prob = probs[layer, 2 * p + h]
            prob_grad = product_right(up_h, v)
            row_dot = jnp.sum(prob * prob_grad, -1, keepdims=True)
            score_grad = (prob * (prob_grad - row_dot)).astype(LOW)
            terms = (
                product(score_grad, one_head(k, h)),
                product_left(score_grad, one_head(q, h)),
                product_left(prob.astype(LOW), up_h),
            )
            sums = [t if s is None else s + t for s, t in zip(sums, terms)]
        query_grad = sums[0] * factor
        start = p * 2 * HD
        tiny[0, pl.ds(bias_row(layer, 1), 1), pair(p)] = column_sum(query_grad)
        tiny[0, pl.ds(bias_row(layer, 2), 1), pair(p)] = column_sum(sums[2])
        for n, value in enumerate((query_grad, sums[1], sums[2])):
            pgrad[:, pl.ds(n * width + start, 2 * HD)] = value.astype(LOW)

    def back_qkv(layer, n):
        cols = pl.ds(n * width, width)
        own_g[QKV][layer, :, :, :, cols] = shared(product_left(normed_one[layer], pgrad[:, cols]))

    def back_first(layer):
        first_grad = product_right(pgrad[...], w_qkv[layer])
        back, gain, shift = norm_back(
            first_grad, unit_one[layer], inv_one[layer], gain_of(layer, 0))
        put_gain(layer, 0, gain)
        put_bias(layer, 0, shift)
        grad[...] = grad[...] + back


    def finish_forward():
        x_in[...] = stream[pl.ds(0, tokens), :] * live
        return local(x_in, act_out.at[:, 0], io_sem.at[0])

    swaps = []

    def tiny_send(n):
        device = (mate, side[0], side[1])[n]
        swaps.append(remote(tiny.at[n], tiny_in.at[n], t_send.at[n], t_recv.at[n], device))

    def tiny_add(n):
        swaps[n].wait_recv()
        tiny[n + 1] = tiny[n] + tiny_in[n]

    def finish_backward():
        cot[...] = grad[pl.ds(0, tokens), :]
        return local(cot, grad_out.at[:, 0], io_sem.at[1])

    relay(0)
    first(3)
    relay(1)
    first(4)
    relay(2)
    first(5)
    reach(0)
    relay(3)
    first(6)
    reach(1)
    relay(4)
    first(7)
    cross(0)
    reach(2)
    reach(3)
    settle(2)
    project(0)
    relay(5)
    for j in range(0, 3):
        attend(0, j)
    reach(4)
    relay(6)
    cross(1)
    relay(7)
    settle(4)
    join(0)
    settle(0)
    for j in range(0, 4):
        expand(0, j)
    cross(3)
    expand(0, 4)
    expand(0, 5)
    reach(5)
    reach(6)
    settle(3)
    contract(0)
    reach(7)
    settle(5)
    project(1)
    for j in range(0, 3):
        attend(1, j)
    settle(7)
    join(1)
    settle(1)
    for j in range(0, 6):
        expand(1, j)
    back_down(1)
    swap(0)
    cross(6)
    swap(1)
    scatter_one(0)
    settle(6)
    for j in range(0, 6):
        back_expand(1, j)
    back_up(1, 0)
    swap(2)
    scatter_one(1)
    back_up(1, 1)
    swap(3)
    back_middle(1)
    swap(4)
    back_mix(1)
    back_attend(1, 0)
    scatter_one(2)
    scatter_one(3)
    back_attend(1, 1)
    back_attend(1, 2)
    back_qkv(1, 0)
    scatter_two(0)
    back_qkv(1, 1)
    swap(5)
    back_qkv(1, 2)
    swap(6)
    back_first(1)
    scatter_two(1)
    back_down(0)
    swap(7)
    swap(8)
    back_expand(0, 0)
    back_expand(0, 1)
    scatter_one(5)
    for j in range(2, 6):
        back_expand(0, j)
    back_up(0, 0)
    swap(9)
    scatter_one(6)
    scatter_two(2)
    back_up(0, 1)
    swap(10)
    back_middle(0)
    swap(11)
    scatter_two(3)
    z_first(1)
    back_mix(0)
    back_attend(0, 0)
    z_first(0)
    scatter_one(4)
    back_attend(0, 1)
    scatter_one(9)
    scatter_two(6)
    back_attend(0, 2)
    scatter_two(5)
    back_qkv(0, 0)
    back_qkv(0, 1)
    swap(12)
    back_qkv(0, 2)
    swap(13)
    z_second(1)
    z_first(2)
    scatter_one(8)
    z_first(3)
    back_first(0)
    store_grad = finish_backward()
    tiny_send(0)
    z_second(0)
    scatter_two(4)
    contract(1)
    store_act = finish_forward()
    scatter_one(12)
    z_first(5)
    tiny_add(0)
    tiny_send(1)
    scatter_one(13)
    z_third(1)
    z_second(2)
    scatter_two(9)
    z_first(6)
    z_first(4)
    z_third(0)
    z_second(3)
    scatter_two(8)
    scatter_one(10)
    z_second(5)
    z_fourth(1)
    z_third(2)
    scatter_two(13)
    z_second(6)
    scatter_two(12)
    z_second(4)
    scatter_one(7)
    z_fourth(0)
    tiny_add(1)
    tiny_send(2)
    z_third(3)
    z_first(9)
    z_first(8)
    z_third(5)
    z_fourth(2)
    z_first(13)
    z_third(6)
    scatter_one(11)
    scatter_two(10)
    z_third(4)
    z_fourth(3)
    z_second(9)
    z_first(12)
    scatter_two(7)
    tiny_add(2)
    z_first(n_sub)
    z_fourth(5)
    z_second(8)
    z_fourth(6)
    z_second(13)
    z_first(10)
    z_fourth(4)
    scatter_two(11)
    z_third(9)
    z_second(12)
    z_first(7)
    z_second(n_sub)
    z_third(8)
    z_first(11)
    z_third(13)
    z_second(10)
    z_fourth(9)
    z_third(12)
    z_second(7)
    z_third(n_sub)
    z_fourth(8)
    z_second(11)
    z_fourth(13)
    z_third(10)
    z_fourth(12)
    z_third(7)
    z_fourth(n_sub)
    z_third(11)
    z_fourth(10)
    z_fourth(7)
    z_fourth(11)
    done = z_fin[n_sub][...]
    picked = None
    for s in range(shards):
        hit = jnp.where(me == s, 1.0, 0.0).astype(FULL)
        term = done[:up_row, s * rows_d : (s + 1) * rows_d] * hit
        picked = term if picked is None else picked + term
    for layer in range(layers):
        small_held[0][layer] = picked[layer * GAIN_ROWS : (layer + 1) * GAIN_ROWS]
        row = None
        for s in range(shards):
            at = up_row + layer * (ff // width) + s
            hit = jnp.where(me == s, 1.0, 0.0).astype(FULL)
            term = done[at : at + 1] * hit
            row = term if row is None else row + term
        small_held[2][pl.ds(layer, 1), :] = row
    for which in range(BIAS_ROWS):
        small_held[1][which] = picked[bias_row(0, which) : bias_row(0, which) + layers]
    store_small = [local(small_held[n], small_out[n], s_sem.at[n]) for n in range(3)]
    for a in range(n_sub + 1):
        z_done(a)
    for copy in store_small:
        copy.wait()
    for copy in sent:
        copy.wait_send()
    store_act.wait()
    store_grad.wait()


def finish_kernel(count, *refs):
    ins, outs, refs = refs[:count], refs[count : 2 * count], refs[2 * count :]
    held, refs = refs[:count], refs[count:]
    wides, (load_sem, store_sem) = refs[:-2], refs[-2:]
    parts = [(0, None), (1, None)]
    for n in (5, 4, 2, 3):
        parts += [(n, layer) for layer in range(ins[n].shape[0])]
    parts += [(n, None) for n in range(6, count)]

    def view(ref, layer):
        return ref if layer is None else ref.at[layer]

    loads, stores = [], []
    for at, (n, layer) in enumerate(parts):
        copy = pltpu.make_async_copy(view(ins[n], layer), view(held[n], layer), load_sem.at[at])
        copy.start()
        loads.append(copy)
    for at, (n, layer) in enumerate(parts):
        loads[at].wait()
        src = held[n]
        if layer is not None:
            src = wides[n - 2]
            src[layer] = held[n][layer].astype(FULL)
        copy = pltpu.make_async_copy(view(src, layer), view(outs[n], layer), store_sem.at[at])
        copy.start()
        stores.append(copy)
    for copy in stores:
        copy.wait()


def finish(arrays):
    count = len(arrays)
    parts = count - 4 + 4 * arrays[2].shape[0]
    specs = [pl.BlockSpec(memory_space=pl.ANY)] * count
    return pl.pallas_call(
        functools.partial(finish_kernel, count),
        out_shape=[jax.ShapeDtypeStruct(x.shape, FULL) for x in arrays],
        in_specs=specs,
        out_specs=specs,
        scratch_shapes=[pltpu.VMEM(x.shape, x.dtype) for x in arrays]
        + [pltpu.VMEM(x.shape, FULL) for x in arrays[2:6]]
        + [pltpu.SemaphoreType.DMA((parts,))] * 2,
        compiler_params=pltpu.CompilerParams(vmem_limit_bytes=VMEM_LIMIT),
        name="widen",
    )(*arrays)


def on_device(shards, replicas, images, cotangent, counts, *stacks):
    weights, (gains, biases, up_bias) = stacks[:4], stacks[4:]
    layers, rows_d, _ = weights[QKV].shape
    deep = replicas // 2
    tokens, width = images.shape[1:]
    padded = -(-tokens // 16) * 16
    ff = weights[UP].shape[2]
    heads = width // HD
    qkv = weights[QKV].shape[2]
    sems = pltpu.SemaphoreType.DMA
    low = lambda *s: pltpu.VMEM(s, LOW)
    full = lambda *s: pltpu.VMEM(s, FULL)
    small_rows = layers * (GAIN_ROWS + BIAS_ROWS)
    small_rows_pad = -(-small_rows // 8) * 8
    per_up = up_bias.shape[1]
    scratch = [
        full(tokens, width), full(tokens, width), full(padded, width), full(padded, width),
        low(layers, shards * rows_d, qkv), low(layers, shards * rows_d, width),
        low(layers, shards * rows_d, ff), low(layers, ff, width),
        full(small_rows_pad, width), full(8, ff),
        full(small_rows_pad, 128), full(shards, small_rows_pad, 128),
        full(8, per_up), full(shards, 8, per_up),
        full(layers, padded, width), full(layers, padded, 1), low(layers, padded, width),
        low(layers, padded, width), low(layers, padded, width), low(layers, padded, width),
        full(layers, heads, padded, padded), low(layers, padded, width),
        full(layers, padded, width), full(layers, padded, 1), low(layers, padded, width),
        low(layers, padded, ff), full(layers, padded, ff), low(padded, ff), low(padded, width),
        low(padded, qkv),
    ]
    halves = [w.shape[1] // 2 for w in weights]
    columns = [w.shape[2] for w in weights]
    scratch += [low(layers, shards, 2, h, c) for h, c in zip(halves, columns)]
    shapes = [(sub[3], sub[5]) for sub in sub_items(layers, weights, shards)]
    n_sub = len(shapes)
    scratch += [low(shards, *s) for s in shapes] + [low(3, *s) for s in shapes] * 2
    tiny_rows = small_rows + layers * (ff // width)
    scratch += ([low(*s) for s in shapes] + [full(tiny_rows, width)]) * 4
    scratch += [full(4, tiny_rows, width), full(3, tiny_rows, width)]
    n_items = 4 * layers
    scratch += [
        sems((n_items, 2)), sems((n_items, 2)), sems((n_items,)), sems((n_items,)),
        sems((n_items, 3)), sems((n_items, 3)), sems((n_items, 3)), sems((n_items, 3)),
        sems((n_items, 3)), sems((n_items, 3)), sems((2, 3)), sems((2, 3)),
        sems((n_items,)), sems((4,)), sems((n_sub,)), sems((n_sub,)), sems((n_sub,)),
        sems((n_sub,)), sems((n_sub,)), sems((n_sub,)), sems((n_sub + 1, 3)), sems((n_sub + 1, 3)),
        sems((n_sub,)), sems((n_sub,)), sems((n_sub,)), sems((3,)), sems((3,)),
    ]
    shape = jax.ShapeDtypeStruct
    images, cotangent, biases = (x.transpose(1, 0, 2) for x in (images, cotangent, biases))
    scratch += [sems((3,))] + [full(*x.shape) for x in (gains, biases, up_bias)]
    outs = [shape(images.shape, FULL), shape(images.shape, FULL)]
    outs += [shape((layers, 2, h, c), LOW) for h, c in zip(halves, columns)]
    outs += [shape(x.shape, FULL) for x in (gains, biases, up_bias)]
    hbm, vmem = pl.BlockSpec(memory_space=pl.ANY), pl.BlockSpec(memory_space=pltpu.VMEM)
    done = pl.pallas_call(
        functools.partial(fused_kernel, shards, deep),
        out_shape=outs,
        in_specs=[hbm, hbm, pl.BlockSpec(memory_space=pltpu.SMEM)] + [hbm] * 4 + [vmem] * 3,
        out_specs=[hbm] * 9,
        scratch_shapes=scratch,
        compiler_params=pltpu.CompilerParams(
            collective_id=0, has_side_effects=True, vmem_limit_bytes=VMEM_LIMIT
        ),
        name="encoder_step",
    )(images, cotangent, counts, *weights, gains, biases, up_bias)
    done = list(done)
    for kind in range(4):
        done[2 + kind] = done[2 + kind].reshape(weights[kind].shape)
    done = list(finish(done))
    for n in (0, 1, 7):
        done[n] = done[n].transpose(1, 0, 2)
    return tuple(done)


def solution(mesh):
    in_specs = (
        P(("shard", "replica"), None, None),
        P(("shard", "replica"), None, None),
        P(("shard", "replica")),
        P(None, "shard", None),
        P(None, "shard", None),
        P(None, "shard", None),
        P(None, "shard", None),
        P(None, None, "shard"),
        P(None, None, "shard"),
        P(None, "shard"),
    )
    out_specs = (
        P(("shard", "replica"), None, None),
        P(("shard", "replica"), None, None),
        P(None, "shard", None),
        P(None, "shard", None),
        P(None, "shard", None),
        P(None, "shard", None),
        P(None, None, "shard"),
        P(None, None, "shard"),
        P(None, "shard"),
    )
    return jax.shard_map(
        functools.partial(on_device, mesh.shape["shard"], mesh.shape["replica"]), mesh=mesh, in_specs=in_specs, out_specs=out_specs, check_vma=False
    )
```
